32 devices in a mesh: space: 8 (over z, x), freq: 4 (over y, core).
Axes of the slice: x: 2, y: 2, z: 4, core: 2. Of those that a mesh axis runs over, the one named last changes fastest.
Arguments:
- u_velocity: bfloat16 [2176, 16, 512], P(None, 'space', 'freq'), may hold values from -6 to 6
- v_velocity: bfloat16 [2176, 16, 512], P(None, 'space', 'freq'), may hold values from -6 to 6
- cell_weights: float32 [16, 512], P('space', 'freq'), may hold values from 0.25 to 4
- block_offsets: int32 [16], replicated, may hold values from 0 to 1920
- triads: int32 [64, 2], replicated, may hold values from 0 to 63
Outputs:
- eigen_values: float32 [64, 2], replicated
- mode_fields: float32 [64, 2, 16, 512], P(None, None, 'space', 'freq')
The draws below stay inside these ranges and needn't reach their ends.
Inputs may be any that keep to these rules, and one draw needn't show every extreme that they name: `triads`: k and l are each below 64, so k + l is below 128.
All inputs are finite; a program needn't handle non-finite values.
Results may differ from the reference program's by a relative error of at most 0.012.
Values may be sent and summed in bfloat16 or wider, within the bound.
No kernel may reach another device: no remote copies, remote signals or barrier semaphores. Data moves between devices by JAX's collectives and lax.ppermute only.
A program may use at most 64 MiB of HBM per device.

```python
import math
import jax
import jax.numpy as jnp
from jax import lax

NFFT = 256
NB = 16
SX = 2
POW = 4
NT = 2176
NX = 16
NY = 512
NTRI = 64


def plant(drawn, rng, least, largest):
    dims = drawn.shape
    index_at = [jax.random.randint(jax.random.fold_in(rng, axis), (), 0, dims[axis]) for axis in range(len(dims))]
    drawn = drawn.at[tuple(index_at)].set(least)
    longest = dims.index(max(dims))
    index_at[longest] = (index_at[longest] + 1) % dims[longest]
    return drawn.at[tuple(index_at)].set(largest)


def block_scale(own_key, dims, shards, low, top_value):
    loudness = 1.0
    for position, parts in shards:
        steps = jax.random.uniform(jax.random.fold_in(jax.random.fold_in(own_key, 6), position), (parts,), jnp.float32, low / len(shards), top_value / len(shards))
        loudness = loudness * jnp.repeat(jnp.exp(steps), dims[position] // parts).reshape((-1,) + (1,) * (len(dims) - 1 - position))
    return loudness


def bell_draw(rng, dims, spread, limit, cuts=(), held_as=jnp.bfloat16):
    entries = jax.random.normal(rng, dims, jnp.float32) * spread
    if len(cuts) > 0:
        entries = block_scale(rng, dims, cuts, -0.22, 0.18) * entries
    return jnp.clip(entries, min=-limit, max=limit).astype(held_as)


def setup_inputs(seed: int = 0) -> dict:
    arg_keys = jax.random.split(jax.random.key(seed), 6)
    u_velocity = bell_draw(arg_keys[0], (NT, NX, NY), 1.0, 6.0, ((1, 8), (2, 4)))
    v_velocity = bell_draw(arg_keys[1], (NT, NX, NY), 1.0, 6.0, ((1, 8), (2, 4)))
    cell_weights = jnp.clip(jnp.exp(math.log(4.0) - 2.7725887 * jax.random.uniform(arg_keys[2], (NX, NY), jnp.float32) ** block_scale(arg_keys[2], (NX, NY), ((0, 8), (1, 4)), -0.2, 0.2)), 0.25, 4.0)
    block_offsets = plant(jax.random.randint(arg_keys[3], (NB,), 0, NT - NFFT + 1), jax.random.fold_in(arg_keys[3], 1), 0, NT - NFFT).astype(jnp.int32)
    triads = plant(jax.random.randint(arg_keys[4], (NTRI, 2), 0, NFFT // 4), jax.random.fold_in(arg_keys[4], 1), 0, (NFFT // 4) - 1).astype(jnp.int32)
    return {"u_velocity": u_velocity, "v_velocity": v_velocity, "cell_weights": cell_weights, "block_offsets": block_offsets, "triads": triads}


def make_table(length):
    half_len = length // 2
    times_idx = jnp.arange(length, dtype=jnp.int32)
    freq_idx = jnp.arange(half_len, dtype=jnp.int32)
    phases = freq_idx[:, None] * times_idx[None, :] % length
    angles = phases.astype(jnp.float32) * (2.0 * math.pi / length)
    window = 0.5 - 0.5 * jnp.cos(times_idx.astype(jnp.float32) * (2.0 * math.pi / length))
    scaling = 1.0 / jnp.sqrt(jnp.sum(window * window))
    transform = jnp.concatenate([jnp.cos(angles) * scaling, -jnp.sin(angles) * scaling], axis=0)
    return (window, transform.astype(jnp.bfloat16))

def spectra(vorticity, offsets):
    window, transform = make_table(NFFT)
    fluct = vorticity - lax.optimization_barrier(jnp.mean(vorticity, axis=0, keepdims=True))
    blocks = jax.vmap(lambda start: lax.dynamic_slice_in_dim(fluct, start, NFFT, 0))(offsets)
    windowed = (blocks * window[None, :, None, None]).astype(jnp.bfloat16)
    return jnp.einsum('ft,btxy->bfxy', transform.astype(jnp.float32), windowed.astype(jnp.float32), precision=lax.Precision.HIGHEST)

def pick_target(spectrum, triads):
    half_len = spectrum.shape[1] // 2
    target = triads[:, 0] + triads[:, 1]
    return (jnp.take(spectrum[:, :half_len], target, axis=1), jnp.take(spectrum[:, half_len:], target, axis=1))

def partial_sums(spectrum, weights, triads):
    half_len = spectrum.shape[1] // 2
    real_part = spectrum[:, :half_len]
    imag_part = spectrum[:, half_len:]
    first_re = jnp.take(real_part, triads[:, 0], axis=1)
    first_im = jnp.take(imag_part, triads[:, 0], axis=1)
    second_re = jnp.take(real_part, triads[:, 1], axis=1)
    second_im = jnp.take(imag_part, triads[:, 1], axis=1)
    target_re, target_im = pick_target(spectrum, triads)
    prod_re = (first_re * second_re - first_im * second_im) * weights
    prod_im = (first_re * second_im + first_im * second_re) * weights
    high = lax.Precision.HIGHEST
    cross_re = jnp.einsum('btxy,ctxy->tbc', prod_re, target_re, precision=high) + jnp.einsum('btxy,ctxy->tbc', prod_im, target_im, precision=high)
    cross_im = jnp.einsum('btxy,ctxy->tbc', prod_re, target_im, precision=high) - jnp.einsum('btxy,ctxy->tbc', prod_im, target_re, precision=high)
    return jnp.stack([cross_re, cross_im], axis=1)

def leading(matrices):
    high = lax.Precision.HIGHEST
    mat_re = matrices[:, 0]
    mat_im = matrices[:, 1]
    vec_re = jnp.full(mat_re.shape[:2], 1.0 / math.sqrt(mat_re.shape[1]), jnp.float32)
    vec_im = jnp.zeros(mat_re.shape[:2], jnp.float32)

    def apply(part_re, part_im):
        out_re = jnp.einsum('tbc,tc->tb', mat_re, part_re, precision=high) - jnp.einsum('tbc,tc->tb', mat_im, part_im, precision=high)
        out_im = jnp.einsum('tbc,tc->tb', mat_re, part_im, precision=high) + jnp.einsum('tbc,tc->tb', mat_im, part_re, precision=high)
        return (out_re, out_im)
    for repeat in range(POW):
        out_re, out_im = apply(vec_re, vec_im)
        length = jnp.sqrt(lax.optimization_barrier(jnp.sum(out_re * out_re + out_im * out_im, axis=1, keepdims=True)))
        vec_re = out_re / length
        vec_im = out_im / length
    out_re, out_im = apply(vec_re, vec_im)
    value_re = lax.optimization_barrier(jnp.sum(vec_re * out_re + vec_im * out_im, axis=1))
    value_im = lax.optimization_barrier(jnp.sum(vec_re * out_im - vec_im * out_re, axis=1))
    return (jnp.stack([vec_re, vec_im], axis=1), jnp.stack([value_re, value_im], axis=1))

def modes(vectors, target_re, target_im):
    high = lax.Precision.HIGHEST
    vec_re = vectors[:, 0]
    vec_im = vectors[:, 1]
    mode_re = jnp.einsum('tb,btxy->txy', vec_re, target_re, precision=high) - jnp.einsum('tb,btxy->txy', vec_im, target_im, precision=high)
    mode_im = jnp.einsum('tb,btxy->txy', vec_re, target_im, precision=high) + jnp.einsum('tb,btxy->txy', vec_im, target_re, precision=high)
    return jnp.stack([mode_re, mode_im], axis=1)

def reference(u_velocity, v_velocity, cell_weights, block_offsets, triads):
    u_padded = jnp.pad(u_velocity, ((0, 0), (0, 0), (1, 1)))
    v_padded = jnp.pad(v_velocity, ((0, 0), (1, 1), (0, 0)))

    def slab(index):
        start = (index * SX).astype(jnp.int32)
        u_part = lax.dynamic_slice_in_dim(u_padded, start, SX, 1).astype(jnp.float32)
        v_part = lax.dynamic_slice_in_dim(v_padded, start, SX + 2, 1).astype(jnp.float32)
        vorticity = 0.5 * (v_part[:, 2:, :] - v_part[:, :-2, :]) - 0.5 * (u_part[:, :, 2:] - u_part[:, :, :-2])
        weights = lax.dynamic_slice_in_dim(cell_weights, start, SX, 0)
        return (spectra(vorticity, block_offsets), weights)

    def accumulate(carry, index):
        spectrum, weights = slab(index)
        return (carry + partial_sums(spectrum, weights, triads), None)
    indices = jnp.arange(NX // SX, dtype=jnp.int32)
    total, _ = lax.scan(accumulate, jnp.zeros((NTRI, 2, NB, NB), jnp.float32), indices)
    total = total / (NB * math.sqrt(NX * NY))
    vectors, values = leading(total)

    def shape_mode(index):
        spectrum, weights = slab(index)
        target_re, target_im = pick_target(spectrum, triads)
        return modes(vectors, target_re, target_im)
    pieces = lax.map(shape_mode, indices)
    mode_fields = jnp.transpose(pieces, (1, 2, 0, 3, 4)).reshape(NTRI, 2, NX, NY)
    return (values, mode_fields)
```

```python
import functools
import math

import jax
import jax.numpy as jnp
import numpy as np
from jax import lax
from jax.experimental import pallas as pl
from jax.experimental.pallas import tpu as pltpu
from jax.sharding import PartitionSpec as P

NFFT = 256
POW = 4
LANES = 128
F32 = jnp.float32
BF16 = jnp.bfloat16
VMEM = pl.BlockSpec(memory_space=pltpu.VMEM)
SMEM = pl.BlockSpec(memory_space=pltpu.SMEM)


def make_table(length):
    half_len = length // 2
    times_idx = np.arange(length)
    phases = np.arange(half_len)[:, None] * times_idx[None, :] % length
    angles = phases * (2.0 * math.pi / length)
    window = 0.5 - 0.5 * np.cos(times_idx * (2.0 * math.pi / length))
    scaling = 1.0 / np.sqrt(np.sum(window * window))
    transform = np.concatenate([np.cos(angles) * scaling, -np.sin(angles) * scaling], axis=0)
    return window.astype(np.float32), transform.astype(np.float32)


def edge_columns(rows, pieces):
    picks = np.zeros((pieces, 2 * pieces, LANES), np.float32)
    places = np.zeros((pieces, 2 * pieces, LANES), np.float32)
    for m in range(pieces):
        picks[m, m, 0] = 1.0
        picks[m, pieces + m, LANES - 1] = 1.0
        places[m, m, 0] = 0.5
        places[m, pieces + m, LANES - 1] = -0.5
    return picks, places


def pack_kernel(sx, pieces, v_ref, u_ref, picks_ref, first_ref, last_ref, cols_ref, plain):
    rows = v_ref.shape[0]
    times = rows // sx
    plain[...] = v_ref[...].astype(F32)
    first_ref[...] = plain[pl.ds(0, times, stride=sx), :].astype(BF16)
    last_ref[...] = plain[pl.ds(sx - 1, times, stride=sx), :].astype(BF16)
    part = rows // pieces
    cols = jnp.zeros((2 * pieces, part), F32)
    for m in range(pieces):
        cols += lax.dot_general(
            picks_ref[m], u_ref[m * part : (m + 1) * part, :], (((1,), (1,)), ((), ())), preferred_element_type=F32
        )
    cols_ref[...] = cols.astype(BF16)


def pack(v, u, picks, sx):
    rows = v.shape[0]
    pieces = picks.shape[0]
    times = rows // sx
    return pl.pallas_call(
        functools.partial(pack_kernel, sx, pieces),
        out_shape=(
            jax.ShapeDtypeStruct((times, LANES), BF16),
            jax.ShapeDtypeStruct((times, LANES), BF16),
            jax.ShapeDtypeStruct((2 * pieces, rows // pieces), BF16),
        ),
        in_specs=[VMEM] * 3,
        out_specs=(VMEM,) * 3,
        scratch_shapes=[pltpu.VMEM((rows, LANES), F32)],
        name="pack",
    )(v, u, picks)


def local_kernel(sx, pieces, v_ref, u_ref, shift_ref, cols_ref, places_ref, z_ref, sum_ref, plain, slope):
    rows = v_ref.shape[0]
    times = rows // sx
    part = rows // pieces
    plain[...] = 0.5 * v_ref[...].astype(F32)
    for m in range(pieces):
        inner = jnp.dot(u_ref[m * part : (m + 1) * part, :], shift_ref[...], preferred_element_type=F32)
        outer = lax.dot_general(
            cols_ref[...], places_ref[m], (((0,), (0,)), ((), ())), preferred_element_type=F32
        )
        slope[m * part : (m + 1) * part, :] = inner + outer
    for row in range(sx):
        z = slope[pl.ds(row, times, stride=sx), :]
        if row + 1 < sx:
            z += plain[pl.ds(row + 1, times, stride=sx), :]
        if row > 0:
            z -= plain[pl.ds(row - 1, times, stride=sx), :]
        z_ref[row] = z
        sum_ref[row] = jnp.sum(z.reshape(times // 8, 8, LANES), axis=0)


def local_part(v, u, shift, cols, places, sx):
    rows = v.shape[0]
    pieces = places.shape[0]
    times = rows // sx
    return pl.pallas_call(
        functools.partial(local_kernel, sx, pieces),
        out_shape=(
            jax.ShapeDtypeStruct((sx, times, LANES), F32),
            jax.ShapeDtypeStruct((sx, 8, LANES), F32),
        ),
        in_specs=[VMEM] * 5,
        out_specs=(VMEM,) * 2,
        scratch_shapes=[pltpu.VMEM((rows, LANES), F32), pltpu.VMEM((rows, LANES), F32)],
        cost_estimate=pl.CostEstimate(flops=1000000000, bytes_accessed=8000000, transcendentals=0),
        name="local",
    )(v, u, shift, cols, places)


def cross_kernel(
    offsets_ref, triads_ref, z_ref, sum_ref, left_ref, right_ref, weights_ref, window_ref, transform_ref,
    cross_ref, target_ref, full, spec, prod, packed,
):
    sx, times, _ = z_ref.shape
    blocks = offsets_ref.shape[0]
    ntri = triads_ref.shape[0]
    half = NFFT // 2
    groups = LANES // blocks
    per = ntri // groups
    wide = 2 * blocks

    chunk = times // 8
    totals = [sum_ref[row] for row in range(sx)]

    def add_halo(step, carry):
        at = pl.ds(pl.multiple_of(step * chunk, 8), chunk)
        low = 0.5 * left_ref[at, :].astype(F32)
        high = 0.5 * right_ref[at, :].astype(F32)
        for row in range(sx):
            z = z_ref[row, at, :]
            if row == 0:
                z -= low
            if row == sx - 1:
                z += high
            full[row, at, :] = z
        return (
            carry[0] + jnp.sum(low.reshape(chunk // 8, 8, LANES), axis=0),
            carry[1] + jnp.sum(high.reshape(chunk // 8, 8, LANES), axis=0),
        )

    zero = jnp.zeros((8, LANES), F32)
    low_sum, high_sum = lax.fori_loop(0, 8, add_halo, (zero, zero))
    totals[0] = totals[0] - low_sum
    totals[sx - 1] = totals[sx - 1] + high_sum
    means = [jnp.sum(total, axis=0, keepdims=True) * (1.0 / times) for total in totals]

    def one_block(b, carry):
        at = pl.ds(offsets_ref[b], NFFT)
        window = window_ref[...]
        for row in range(sx):
            windowed = ((full[row, at, :] - means[row]) * window).astype(BF16)
            out = jnp.dot(transform_ref[...], windowed, preferred_element_type=F32)
            spec[row, pl.ds(b, NFFT, stride=blocks), :] = out
        return carry

    lax.fori_loop(0, blocks, one_block, 0, unroll=2)

    def one_triad(j, carry):
        k = triads_ref[j, 0]
        l = triads_ref[j, 1]

        def take(f, row):
            re = spec[row, pl.ds(pl.multiple_of(f * blocks, 8), blocks), :]
            im = spec[row, pl.ds(pl.multiple_of((f + half) * blocks, 8), blocks), :]
            return re, im

        base = pl.multiple_of(j * wide, 8)
        for row in range(sx):
            lanes = slice(row * LANES, (row + 1) * LANES)
            first_re, first_im = take(k, row)
            second_re, second_im = take(l, row)
            target_re, target_im = take(k + l, row)
            weight = weights_ref[row : row + 1, :]
            prod[pl.ds(base, wide), lanes] = jnp.concatenate(
                [
                    (first_re * second_re - first_im * second_im) * weight,
                    (first_re * second_im + first_im * second_re) * weight,
                ],
                axis=0,
            ).astype(BF16)
            target_ref[pl.ds(base, wide), lanes] = jnp.concatenate([target_re, target_im], axis=0).astype(BF16)
        return carry

    lax.fori_loop(0, ntri, one_triad, 0, unroll=4)

    tall = per * wide
    lane = lax.broadcasted_iota(jnp.int32, (wide, tall), 1)
    owner = lane // wide
    is_re = (lax.broadcasted_iota(jnp.int32, (blocks, tall), 1) % wide) < blocks

    def one_group(g, carry):
        at = pl.ds(pl.multiple_of(g * tall, 8), tall)
        every = lax.dot_general(
            prod[at, :], target_ref[at, :], (((1,), (1,)), ((), ())), preferred_element_type=F32
        )
        kept = every[0:wide]
        for i in range(1, per):
            kept = jnp.where(owner == i, every[i * wide : (i + 1) * wide], kept)
        by_re = kept[0:blocks]
        by_im = kept[blocks:wide]
        ahead = pltpu.roll(by_im, tall - blocks, 1)
        behind = pltpu.roll(by_im, blocks, 1)
        packed[pl.ds(pl.multiple_of(g * blocks, 8), blocks), :] = by_re + jnp.where(is_re, ahead, -behind)
        return carry

    lax.fori_loop(0, groups, one_group, 0, unroll=2)
    cross_ref[...] = packed[...].T


def cross_part(offsets, triads, z, sums, left, right, weights, window, transform):
    sx, times, _ = z.shape
    blocks = offsets.shape[0]
    ntri = triads.shape[0]
    groups = LANES // blocks
    wide = 2 * blocks
    tall = ntri // groups * wide
    return pl.pallas_call(
        cross_kernel,
        out_shape=(
            jax.ShapeDtypeStruct((tall, LANES), F32),
            jax.ShapeDtypeStruct((ntri * wide, sx * LANES), BF16),
        ),
        in_specs=[SMEM, SMEM] + [VMEM] * 7,
        out_specs=(VMEM,) * 2,
        scratch_shapes=[
            pltpu.VMEM((sx, times, LANES), F32),
            pltpu.VMEM((sx, NFFT * blocks, LANES), F32),
            pltpu.VMEM((ntri * wide, sx * LANES), BF16),
            pltpu.VMEM((LANES, tall), F32),
        ],
        name="cross",
    )(offsets, triads, z, sums, left, right, weights, window, transform)


def swap(x, axis, bit):
    count = lax.axis_size(axis)
    return lax.ppermute(x, axis, [(i, i ^ bit) for i in range(count)])


def sum_over(x, axes):
    for axis in axes:
        count = lax.axis_size(axis)
        if count & (count - 1):
            x = lax.psum(x, axis)
            continue
        bit = 1
        while bit < count:
            x = x + swap(x, axis, bit)
            bit *= 2
    return x


def sum_all(x):
    return sum_over(x, ("freq", "space"))


def modes_kernel(blocks, scaling, cross_ref, target_ref, values_ref, modes_ref):
    tall = cross_ref.shape[0]
    wide = 2 * blocks
    per = tall // wide
    groups = LANES // blocks
    sx = target_ref.shape[1] // LANES
    lane = lax.broadcasted_iota(jnp.int32, (per, LANES), 1)
    start = lane - lane % blocks

    mat_re = [cross_ref[pl.ds(c, per, stride=wide), :] * scaling for c in range(blocks)]
    mat_im = [cross_ref[pl.ds(blocks + c, per, stride=wide), :] * scaling for c in range(blocks)]

    def pick(x, index):
        return jnp.take_along_axis(x, index, axis=1)

    spots = [start + c for c in range(blocks)]

    def apply(part_re, part_im):
        sums = []
        for parity in range(2):
            out_re = jnp.zeros((per, LANES), F32)
            out_im = jnp.zeros((per, LANES), F32)
            for c in range(parity, blocks, 2):
                re = pick(part_re, spots[c])
                im = pick(part_im, spots[c])
                out_re += mat_re[c] * re - mat_im[c] * im
                out_im += mat_re[c] * im + mat_im[c] * re
            sums.append((out_re, out_im))
        return sums[0][0] + sums[1][0], sums[0][1] + sums[1][1]

    def over_blocks(x):
        bit = 1
        while bit < blocks:
            x = x + pick(x, lane ^ bit)
            bit *= 2
        return x

    vec_re = jnp.full((per, LANES), 1.0 / math.sqrt(blocks), F32)
    vec_im = jnp.zeros((per, LANES), F32)
    for _ in range(POW):
        out_re, out_im = apply(vec_re, vec_im)
        length = jnp.sqrt(over_blocks(out_re * out_re + out_im * out_im))
        vec_re = out_re / length
        vec_im = out_im / length
    out_re, out_im = apply(vec_re, vec_im)
    value_re = over_blocks(vec_re * out_re + vec_im * out_im)
    value_im = over_blocks(vec_re * out_im - vec_im * out_re)

    source = jnp.minimum(lane // per * blocks, LANES - 1)
    mine = lax.broadcasted_iota(jnp.int32, (per, LANES), 0) == lane % per
    for part, value in enumerate((value_re, value_im)):
        row = jnp.sum(jnp.where(mine, pick(value, source), 0.0), axis=0, keepdims=True)
        values_ref[part : part + 1, :] = row[:, : values_ref.shape[1]]

    tall_re = vec_re.T
    tall_im = vec_im.T
    for g in range(groups):
        for i in range(per):
            j = g * per + i
            col_re = jnp.broadcast_to(tall_re[g * blocks : (g + 1) * blocks, i : i + 1], (blocks, LANES))
            col_im = jnp.broadcast_to(tall_im[g * blocks : (g + 1) * blocks, i : i + 1], (blocks, LANES))
            for row in range(sx):
                lanes = slice(row * LANES, (row + 1) * LANES)
                re = target_ref[j * wide : j * wide + blocks, lanes].astype(F32)
                im = target_ref[j * wide + blocks : (j + 1) * wide, lanes].astype(F32)
                at = 2 * j * sx + row
                modes_ref[at : at + 1, :] = jnp.sum(col_re * re - col_im * im, axis=0, keepdims=True)
                modes_ref[at + sx : at + sx + 1, :] = jnp.sum(col_re * im + col_im * re, axis=0, keepdims=True)


def modes_part(cross, target, blocks, ntri, scaling):
    sx = target.shape[1] // LANES
    return pl.pallas_call(
        functools.partial(modes_kernel, blocks, scaling),
        out_shape=(
            jax.ShapeDtypeStruct((2, ntri), F32),
            jax.ShapeDtypeStruct((ntri * 2 * sx, LANES), F32),
        ),
        in_specs=[VMEM] * 2,
        out_specs=(VMEM,) * 2,
        name="modes",
    )(cross, target)


def neighbours(low, high, axis):
    ends = lax.axis_size(axis) - 1
    return (
        lax.ppermute(high, axis, [(i, i + 1) for i in range(ends)]),
        lax.ppermute(low, axis, [(i + 1, i) for i in range(ends)]),
    )


def on_device(u_velocity, v_velocity, cell_weights, block_offsets, triads):
    times, sx, columns = u_velocity.shape
    blocks = block_offsets.shape[0]
    ntri = triads.shape[0]
    cells = sx * columns * lax.axis_size("space") * lax.axis_size("freq")
    scaling = 1.0 / (blocks * math.sqrt(cells))
    pieces = 8
    window, transform = make_table(NFFT)
    picks, places = edge_columns(times * sx, pieces)
    shift = 0.5 * (np.eye(LANES, k=1, dtype=np.float32) - np.eye(LANES, k=-1, dtype=np.float32))
    v = v_velocity.reshape(times * sx, columns)
    u = u_velocity.reshape(times * sx, columns)

    first, last, cols = pack(v, u, jnp.asarray(picks, BF16), sx)
    left, right = neighbours(first, last, "space")
    col_left, col_right = neighbours(cols[:pieces], cols[pieces:], "freq")
    z, sums = local_part(
        v, u, jnp.asarray(shift, BF16), jnp.concatenate([col_left, col_right], axis=0), jnp.asarray(places, BF16), sx
    )
    share, target = cross_part(
        block_offsets, triads, z, sums, left, right, cell_weights,
        jnp.asarray(np.broadcast_to(window[:, None], (NFFT, LANES))), jnp.asarray(transform, BF16),
    )
    cross = sum_all(share)
    values, modes = modes_part(cross, target, blocks, ntri, scaling)
    return (values.T, modes.reshape(ntri, 2, sx, columns))


def solution(mesh):
    return jax.shard_map(
        on_device,
        mesh=mesh,
        in_specs=(P(None, "space", "freq"), P(None, "space", "freq"), P("space", "freq"), P(), P()),
        out_specs=(P(), P(None, None, "space", "freq")),
        check_vma=False,
    )
```

```python
import functools
import math

import jax
import jax.numpy as jnp
import numpy as np
from jax import lax
from jax.experimental import pallas as pl
from jax.experimental.pallas import tpu as pltpu
from jax.sharding import PartitionSpec as P

NFFT = 256
POW = 4
NEAR_STEPS = 2
LANES = 128
F32 = jnp.float32
BF16 = jnp.bfloat16
MIB = 2**20
VMEM = pl.BlockSpec(memory_space=pltpu.VMEM)
SMEM = pl.BlockSpec(memory_space=pltpu.SMEM)


def make_table(length):
    half_len = length // 2
    times_idx = np.arange(length)
    phases = np.arange(half_len)[:, None] * times_idx[None, :] % length
    angles = phases * (2.0 * math.pi / length)
    window = 0.5 - 0.5 * np.cos(times_idx * (2.0 * math.pi / length))
    scaling = 1.0 / np.sqrt(np.sum(window * window))
    transform = np.concatenate([np.cos(angles) * scaling, -np.sin(angles) * scaling], axis=0)
    return window.astype(np.float32), transform.astype(np.float32)


def edge_columns(rows, pieces):
    picks = np.zeros((pieces, 2 * pieces, LANES), np.float32)
    places = np.zeros((pieces, 2 * pieces, LANES), np.float32)
    for m in range(pieces):
        picks[m, m, 0] = 1.0
        picks[m, pieces + m, LANES - 1] = 1.0
        places[m, m, 0] = 0.5
        places[m, pieces + m, LANES - 1] = -0.5
    return picks, places


def is_odd():
    return lax.axis_index("space") % 2


def row_at(position, sx, odd):
    return jnp.where(odd == 1, position, sx - 1 - position)


def limit(mib):
    return pltpu.CompilerParams(vmem_limit_bytes=mib * MIB)


def near_kernel(sx, odd_ref, v_ref, near_ref, plain):
    times = near_ref.shape[0]
    plain[...] = v_ref[...].astype(F32)
    near_ref[...] = plain[pl.ds(row_at(0, sx, odd_ref[0]), times, stride=sx), :].astype(BF16)


def near_edge(odd, v, sx):
    rows = v.shape[0]
    steps = NEAR_STEPS
    return pl.pallas_call(
        functools.partial(near_kernel, sx),
        grid=(steps,),
        out_shape=jax.ShapeDtypeStruct((rows // sx, LANES), BF16),
        in_specs=[SMEM, pl.BlockSpec((rows // steps, LANES), lambda i: (i, 0))],
        out_specs=pl.BlockSpec((rows // sx // steps, LANES), lambda i: (i, 0)),
        scratch_shapes=[pltpu.VMEM((rows // steps, LANES), F32)],
        compiler_params=limit(8),
        name="near",
    )(odd, v)


def far_kernel(sx, pieces, odd_ref, v_ref, u_ref, picks_ref, far_ref, low_ref, high_ref, plain):
    rows = v_ref.shape[0]
    times = rows // sx
    plain[...] = v_ref[...].astype(F32)
    far_ref[...] = plain[pl.ds(row_at(sx - 1, sx, odd_ref[0]), times, stride=sx), :].astype(BF16)
    part = rows // pieces
    cols = jnp.zeros((2 * pieces, part), F32)
    for m in range(pieces):
        cols += lax.dot_general(
            picks_ref[m], u_ref[m * part : (m + 1) * part, :], (((1,), (1,)), ((), ())), preferred_element_type=F32
        )
    low_ref[...] = cols[:pieces].astype(BF16)
    high_ref[...] = cols[pieces:].astype(BF16)


def far_edge(odd, v, u, picks, sx):
    rows = v.shape[0]
    pieces = picks.shape[0]
    times = rows // sx
    return pl.pallas_call(
        functools.partial(far_kernel, sx, pieces),
        out_shape=(
            jax.ShapeDtypeStruct((times, LANES), BF16),
            jax.ShapeDtypeStruct((pieces, rows // pieces), BF16),
            jax.ShapeDtypeStruct((pieces, rows // pieces), BF16),
        ),
        in_specs=[SMEM] + [VMEM] * 3,
        out_specs=(VMEM,) * 3,
        scratch_shapes=[pltpu.VMEM((rows, LANES), F32)],
        compiler_params=limit(12),
        cost_estimate=pl.CostEstimate(flops=200000000, bytes_accessed=4000000, transcendentals=0),
        name="far",
    )(odd, v, u, picks)


def local_kernel(
    sx, pieces, odd_ref, v_ref, u_ref, shift_ref, low_ref, high_ref, places_ref, z_ref, sum_ref, plain, slope
):
    rows = v_ref.shape[0]
    times = rows // sx
    part = rows // pieces
    odd = odd_ref[0]
    sign = jnp.where(odd == 1, 0.5, -0.5)
    plain[...] = sign * v_ref[...].astype(F32)
    cols = jnp.concatenate([low_ref[...], high_ref[...]], axis=0)
    for m in range(pieces):
        inner = jnp.dot(u_ref[m * part : (m + 1) * part, :], shift_ref[...], preferred_element_type=F32)
        outer = lax.dot_general(cols, places_ref[m], (((0,), (0,)), ((), ())), preferred_element_type=F32)
        slope[m * part : (m + 1) * part, :] = inner + outer
    for position in range(sx):
        z = slope[pl.ds(row_at(position, sx, odd), times, stride=sx), :]
        if position + 1 < sx:
            z += plain[pl.ds(row_at(position + 1, sx, odd), times, stride=sx), :]
        if position > 0:
            z -= plain[pl.ds(row_at(position - 1, sx, odd), times, stride=sx), :]
        z_ref[position] = z
        sum_ref[position] = jnp.sum(z.reshape(times // 8, 8, LANES), axis=0)


def local_part(odd, v, u, shift, low, high, places, sx):
    rows = v.shape[0]
    pieces = places.shape[0]
    times = rows // sx
    return pl.pallas_call(
        functools.partial(local_kernel, sx, pieces),
        out_shape=(
            jax.ShapeDtypeStruct((sx, times, LANES), F32),
            jax.ShapeDtypeStruct((sx, 8, LANES), F32),
        ),
        in_specs=[SMEM] + [VMEM] * 6,
        out_specs=(VMEM,) * 2,
        scratch_shapes=[pltpu.VMEM((rows, LANES), F32), pltpu.VMEM((rows, LANES), F32)],
        compiler_params=limit(20),
        cost_estimate=pl.CostEstimate(flops=1000000000, bytes_accessed=8000000, transcendentals=0),
        name="local",
    )(odd, v, u, shift, low, high, places)


def cross_kernel(
    sx, begin, odd_ref, offsets_ref, triads_ref, z_ref, sum_ref, halo_ref, weights_ref, window_ref, transform_ref,
    *rest,
):
    far = begin > 0
    if far:
        before_ref, cross_ref, target_ref, full, spec, prod, packed = rest
    else:
        cross_ref, target_ref, full, spec, prod, packed = rest
    count, times, _ = full.shape
    blocks = offsets_ref.shape[0]
    ntri = triads_ref.shape[0]
    half = NFFT // 2
    groups = LANES // blocks
    per = ntri // groups
    wide = 2 * blocks
    pitch = blocks + 1
    odd = odd_ref[0]
    sign = jnp.where(odd == 1, 0.5, -0.5)
    if not far:
        sign = -sign
    touched = count - 1 if far else 0

    chunk = times // 8

    def add_halo(step, carry):
        at = pl.ds(pl.multiple_of(step * chunk, 8), chunk)
        halo = sign * halo_ref[at, :].astype(F32)
        for row in range(count):
            z = z_ref[begin + row, at, :]
            full[row, at, :] = z + halo if row == touched else z
        return carry + jnp.sum(halo.reshape(chunk // 8, 8, LANES), axis=0)

    halo_sum = lax.fori_loop(0, 8, add_halo, jnp.zeros((8, LANES), F32))
    means = []
    for row in range(count):
        total = sum_ref[begin + row]
        if row == touched:
            total = total + halo_sum
        means.append(jnp.sum(total, axis=0, keepdims=True) * (1.0 / times))

    def one_block(b, carry):
        at = pl.ds(offsets_ref[b], NFFT)
        window = window_ref[...]
        for row in range(count):
            windowed = ((full[row, at, :] - means[row]) * window).astype(BF16)
            out = jnp.dot(transform_ref[...], windowed, preferred_element_type=F32)
            spec[row, pl.ds(b, NFFT, stride=pitch), :] = out
        return carry

    lax.fori_loop(0, blocks, one_block, 0, unroll=True)
    weights = [weights_ref[pl.ds(row_at(begin + row, sx, odd), 1), :] for row in range(count)]

    def one_triad(j, carry):
        k = triads_ref[j, 0]
        l = triads_ref[j, 1]

        def take(f, row):
            re = spec[row, pl.ds(f * pitch, blocks), :]
            im = spec[row, pl.ds((f + half) * pitch, blocks), :]
            return re, im

        base = pl.multiple_of(j * wide, 8)
        for row in range(count):
            lanes = slice(row * LANES, (row + 1) * LANES)
            first_re, first_im = take(k, row)
            second_re, second_im = take(l, row)
            target_re, target_im = take(k + l, row)
            weight = weights[row]
            prod[pl.ds(base, wide), lanes] = jnp.concatenate(
                [
                    (first_re * second_re - first_im * second_im) * weight,
                    (first_re * second_im + first_im * second_re) * weight,
                ],
                axis=0,
            ).astype(BF16)
            target_ref[pl.ds(base, wide), lanes] = jnp.concatenate([target_re, target_im], axis=0).astype(BF16)
        return carry

    lax.fori_loop(0, ntri, one_triad, 0, unroll=4)

    tall = per * wide
    lane = lax.broadcasted_iota(jnp.int32, (wide, tall), 1)
    owner = lane // wide
    is_re = (lax.broadcasted_iota(jnp.int32, (blocks, tall), 1) % wide) < blocks

    def one_group(g, carry):
        at = pl.ds(pl.multiple_of(g * tall, 8), tall)
        every = lax.dot_general(
            prod[at, :], target_ref[at, :], (((1,), (1,)), ((), ())), preferred_element_type=F32
        )
        kept = every[0:wide]
        for i in range(1, per):
            kept = jnp.where(owner == i, every[i * wide : (i + 1) * wide], kept)
        by_re = kept[0:blocks]
        by_im = kept[blocks:wide]
        ahead = pltpu.roll(by_im, tall - blocks, 1)
        behind = pltpu.roll(by_im, blocks, 1)
        packed[pl.ds(pl.multiple_of(g * blocks, 8), blocks), :] = by_re + jnp.where(is_re, ahead, -behind)
        return carry

    lax.fori_loop(0, groups, one_group, 0, unroll=True)
    share = packed[...].T
    if far:
        share = share + before_ref[...]
    cross_ref[...] = share


def cross_part(begin, count, odd, offsets, triads, z, sums, halo, weights, window, transform, before=None):
    sx, times, _ = z.shape
    blocks = offsets.shape[0]
    ntri = triads.shape[0]
    groups = LANES // blocks
    wide = 2 * blocks
    tall = ntri // groups * wide
    more = [] if before is None else [before]
    return pl.pallas_call(
        functools.partial(cross_kernel, sx, begin),
        out_shape=(
            jax.ShapeDtypeStruct((tall, LANES), F32),
            jax.ShapeDtypeStruct((ntri * wide, count * LANES), BF16),
        ),
        in_specs=[SMEM] * 3 + [VMEM] * (6 + len(more)),
        out_specs=(VMEM,) * 2,
        scratch_shapes=[
            pltpu.VMEM((count, times, LANES), F32),
            pltpu.VMEM((count, NFFT * (blocks + 1), LANES), F32),
            pltpu.VMEM((ntri * wide, count * LANES), BF16),
            pltpu.VMEM((LANES, tall), F32),
        ],
        compiler_params=limit(26),
        cost_estimate=pl.CostEstimate(flops=2000000000, bytes_accessed=4000000, transcendentals=0),
        name="cross",
    )(odd, offsets, triads, z, sums, halo, weights, window, transform, *more)


def swap(x, axis, bit):
    count = lax.axis_size(axis)
    return lax.ppermute(x, axis, [(i, i ^ bit) for i in range(count)])


def sum_over(x, axis, bit):
    count = lax.axis_size(axis)
    while bit < count:
        x = x + swap(x, axis, bit)
        bit *= 2
    return x


def modes_kernel(sx, blocks, scaling, odd_ref, core_ref, mine_ref, other_ref, near_ref, far_ref, values_ref, modes_ref, cross):
    tall = cross.shape[0]
    wide = 2 * blocks
    per = tall // wide
    groups = LANES // blocks
    odd = odd_ref[0]
    core = core_ref[0]
    half = tall // 2
    cross[pl.ds(pl.multiple_of(core * half, 8), half), :] = mine_ref[...] * scaling
    cross[pl.ds(pl.multiple_of((1 - core) * half, 8), half), :] = other_ref[...] * scaling
    lane = lax.broadcasted_iota(jnp.int32, (per, LANES), 1)
    start = lane - lane % blocks

    mat_re = [cross[pl.ds(c, per, stride=wide), :] for c in range(blocks)]
    mat_im = [cross[pl.ds(blocks + c, per, stride=wide), :] for c in range(blocks)]

    def pick(x, index):
        return jnp.take_along_axis(x, index, axis=1)

    spots = [start + c for c in range(blocks)]

    def apply(part_re, part_im):
        sums = []
        for parity in range(2):
            out_re = jnp.zeros((per, LANES), F32)
            out_im = jnp.zeros((per, LANES), F32)
            for c in range(parity, blocks, 2):
                re = pick(part_re, spots[c])
                im = pick(part_im, spots[c])
                out_re += mat_re[c] * re - mat_im[c] * im
                out_im += mat_re[c] * im + mat_im[c] * re
            sums.append((out_re, out_im))
        return sums[0][0] + sums[1][0], sums[0][1] + sums[1][1]

    def over_blocks(x):
        bit = 1
        while bit < blocks:
            x = x + pick(x, lane ^ bit)
            bit *= 2
        return x

    vec_re = jnp.full((per, LANES), 1.0 / math.sqrt(blocks), F32)
    vec_im = jnp.zeros((per, LANES), F32)
    for _ in range(POW):
        out_re, out_im = apply(vec_re, vec_im)
        length = jnp.sqrt(over_blocks(out_re * out_re + out_im * out_im))
        vec_re = out_re / length
        vec_im = out_im / length
    out_re, out_im = apply(vec_re, vec_im)
    value_re = over_blocks(vec_re * out_re + vec_im * out_im)
    value_im = over_blocks(vec_re * out_im - vec_im * out_re)

    source = jnp.minimum(lane // per * blocks, LANES - 1)
    mine = lax.broadcasted_iota(jnp.int32, (per, LANES), 0) == lane % per
    for part, value in enumerate((value_re, value_im)):
        row = jnp.sum(jnp.where(mine, pick(value, source), 0.0), axis=0, keepdims=True)
        values_ref[part : part + 1, :] = row[:, : values_ref.shape[1]]

    own = lax.broadcasted_iota(jnp.int32, (per, tall), 1) // wide == lax.broadcasted_iota(jnp.int32, (per, tall), 0)
    is_re = lax.broadcasted_iota(jnp.int32, (per, tall), 1) % wide < blocks
    for g in range(groups):
        spot = g * blocks + lane % blocks
        re = jnp.concatenate([pick(vec_re, spot)] * (tall // LANES), axis=1)
        im = jnp.concatenate([pick(vec_im, spot)] * (tall // LANES), axis=1)
        rows = jnp.concatenate(
            [
                jnp.where(own, jnp.where(is_re, re, -im), 0.0),
                jnp.where(own, jnp.where(is_re, im, re), 0.0),
            ],
            axis=0,
        )
        high = rows.astype(BF16)
        both = jnp.concatenate([high, (rows - high.astype(F32)).astype(BF16)], axis=0)
        at = slice(g * tall, (g + 1) * tall)
        for position in range(sx):
            if position + 1 < sx:
                target = near_ref[at, position * LANES : (position + 1) * LANES]
            else:
                target = far_ref[at, :]
            out = jnp.dot(both, target, preferred_element_type=F32)
            out = out[: 2 * per] + out[2 * per :]
            row = row_at(position, sx, odd)
            for part in range(2):
                first = g * per * 2 * sx + part * sx
                modes_ref[pl.ds(first + row, per, stride=2 * sx), :] = out[part * per : (part + 1) * per]


def modes_part(odd, core, mine, other, near, far, blocks, ntri, sx, scaling):
    return pl.pallas_call(
        functools.partial(modes_kernel, sx, blocks, scaling),
        out_shape=(
            jax.ShapeDtypeStruct((2, ntri), F32),
            jax.ShapeDtypeStruct((ntri * 2 * sx, LANES), F32),
        ),
        in_specs=[SMEM] * 2 + [VMEM] * 4,
        out_specs=(VMEM,) * 2,
        scratch_shapes=[pltpu.VMEM((2 * mine.shape[0], LANES), F32)],
        compiler_params=limit(12),
        name="modes",
    )(odd, core, mine, other, near, far)


def on_device(u_velocity, v_velocity, cell_weights, block_offsets, triads):
    times, sx, columns = u_velocity.shape
    blocks = block_offsets.shape[0]
    ntri = triads.shape[0]
    slabs = lax.axis_size("space")
    cells = sx * columns * slabs * lax.axis_size("freq")
    scaling = 1.0 / (blocks * math.sqrt(cells))
    pieces = 8
    window, transform = make_table(NFFT)
    picks, places = edge_columns(times * sx, pieces)
    shift = 0.5 * (np.eye(LANES, k=1, dtype=np.float32) - np.eye(LANES, k=-1, dtype=np.float32))
    v = v_velocity.reshape(times * sx, columns)
    u = u_velocity.reshape(times * sx, columns)
    odd = is_odd()[None]
    core = (lax.axis_index("freq") % 2)[None]

    near = lax.ppermute(near_edge(odd, v, sx), "space", [(i, i ^ 1) for i in range(slabs)])
    far, low, high = far_edge(odd, v, u, jnp.asarray(picks, BF16), sx)
    inner = [(i, i + 1) for i in range(1, slabs - 1, 2)]
    far = lax.ppermute(far, "space", inner + [(b, a) for a, b in inner])
    ends = lax.axis_size("freq") - 1
    col_low = lax.ppermute(high, "freq", [(i, i + 1) for i in range(ends)])
    col_high = lax.ppermute(low, "freq", [(i + 1, i) for i in range(ends)])
    z, sums = local_part(odd, v, u, jnp.asarray(shift, BF16), col_low, col_high, jnp.asarray(places, BF16), sx)
    window = jnp.asarray(np.ascontiguousarray(np.broadcast_to(window[:, None], (NFFT, LANES))))
    transform = jnp.asarray(transform, BF16)
    share, near_target = cross_part(
        0, sx - 1, odd, block_offsets, triads, z, sums, near, cell_weights, window, transform
    )
    share, far_target = cross_part(
        sx - 1, 1, odd, block_offsets, triads, z, sums, far, cell_weights, window, transform, share
    )
    half = share.shape[0] // 2
    mine = lax.dynamic_slice_in_dim(share, core[0] * half, half, 0)
    other = lax.dynamic_slice_in_dim(share, (1 - core[0]) * half, half, 0)
    mine = mine + swap(other, "freq", 1)
    mine = sum_over(sum_over(mine, "freq", 2), "space", 1)
    other = swap(mine, "freq", 1)
    values, modes = modes_part(odd, core, mine, other, near_target, far_target, blocks, ntri, sx, scaling)
    return (values.T, modes.reshape(ntri, 2, sx, columns))


def solution(mesh):
    return jax.shard_map(
        on_device,
        mesh=mesh,
        in_specs=(P(None, "space", "freq"), P(None, "space", "freq"), P("space", "freq"), P(), P()),
        out_specs=(P(), P(None, None, "space", "freq")),
        check_vma=False,
    )
```

```python
import functools
import math

import jax
import jax.numpy as jnp
import numpy as np
from jax import lax
from jax.experimental import pallas as pl
from jax.experimental.pallas import tpu as pltpu
from jax.sharding import PartitionSpec as P


NFFT = 256
POW = 4
LANES = 128
F32 = jnp.float32
BF16 = jnp.bfloat16
MIB = 2**20
VMEM = pl.BlockSpec(memory_space=pltpu.VMEM)
SMEM = pl.BlockSpec(memory_space=pltpu.SMEM)


def make_table(length):
    half_len = length // 2
    times_idx = np.arange(length)
    phases = np.arange(half_len)[:, None] * times_idx[None, :] % length
    angles = phases * (2.0 * math.pi / length)
    window = 0.5 - 0.5 * np.cos(times_idx * (2.0 * math.pi / length))
    scaling = 1.0 / np.sqrt(np.sum(window * window))
    transform = np.concatenate([np.cos(angles) * scaling, -np.sin(angles) * scaling], axis=0)
    return window.astype(np.float32), transform.astype(np.float32)


def edge_columns(pieces):
    picks = np.zeros((pieces, 2 * pieces, LANES), np.float32)
    places = np.zeros((pieces, 2 * pieces, LANES), np.float32)
    for m in range(pieces):
        picks[m, m, 0] = 1.0
        picks[m, pieces + m, LANES - 1] = 1.0
        places[m, m, 0] = 0.5
        places[m, pieces + m, LANES - 1] = -0.5
    return picks, places


def is_odd():
    return lax.axis_index("space") % 2


def row_at(position, sx, odd):
    return jnp.where(odd == 1, position, sx - 1 - position)


def limit(mib):
    return pltpu.CompilerParams(vmem_limit_bytes=mib * MIB)


def near_kernel(sx, odd_ref, v_ref, early_ref, late_ref, plain):
    plain[...] = v_ref[...].astype(F32)
    row = row_at(0, sx, odd_ref[0])
    early, late = early_ref.shape[0], late_ref.shape[0]
    early_ref[...] = plain[pl.ds(row, early, stride=sx), :].astype(BF16)
    late_ref[...] = plain[pl.ds(early * sx + row, late, stride=sx), :].astype(BF16)


def near_edge(odd, v, sx):
    rows = v.shape[0]
    early = rows // sx // 32 * 16
    return pl.pallas_call(
        functools.partial(near_kernel, sx),
        out_shape=(
            jax.ShapeDtypeStruct((early, LANES), BF16),
            jax.ShapeDtypeStruct((rows // sx - early, LANES), BF16),
        ),
        in_specs=[SMEM, VMEM],
        out_specs=(VMEM,) * 2,
        scratch_shapes=[pltpu.VMEM((rows, LANES), F32)],
        compiler_params=limit(8),
        name="near",
    )(odd, v)


def far_kernel(sx, odd_ref, v_ref, after_ref, far_ref, plain):
    times = far_ref.shape[0]
    plain[...] = v_ref[...].astype(F32)
    far_ref[...] = plain[pl.ds(row_at(sx - 1, sx, odd_ref[0]), times, stride=sx), :].astype(BF16)


def far_edge(odd, v, after, sx):
    rows = v.shape[0]
    return pl.pallas_call(
        functools.partial(far_kernel, sx),
        out_shape=jax.ShapeDtypeStruct((rows // sx, LANES), BF16),
        in_specs=[SMEM, VMEM, pl.BlockSpec(memory_space=pl.ANY)],
        out_specs=VMEM,
        scratch_shapes=[pltpu.VMEM((rows, LANES), F32)],
        compiler_params=limit(8),
        name="far",
    )(odd, v, after)


def columns_kernel(pieces, u_ref, picks_ref, low_ref, high_ref):
    rows = u_ref.shape[0]
    part = rows // pieces
    cols = jnp.zeros((2 * pieces, part), F32)
    for m in range(pieces):
        cols += lax.dot_general(
            picks_ref[m], u_ref[m * part : (m + 1) * part, :], (((1,), (1,)), ((), ())), preferred_element_type=F32
        )
    low_ref[...] = cols[:pieces].astype(BF16)
    high_ref[...] = cols[pieces:].astype(BF16)


def columns_edge(u, picks):
    rows = u.shape[0]
    pieces = picks.shape[0]
    return pl.pallas_call(
        functools.partial(columns_kernel, pieces),
        out_shape=(
            jax.ShapeDtypeStruct((pieces, rows // pieces), BF16),
            jax.ShapeDtypeStruct((pieces, rows // pieces), BF16),
        ),
        in_specs=[VMEM] * 2,
        out_specs=(VMEM,) * 2,
        compiler_params=limit(8),
        name="columns",
    )(u, picks)


def local_kernel(
    sx, pieces, odd_ref, v_ref, u_ref, shift_ref, low_ref, high_ref, places_ref, z_ref, sum_ref, plain, slope
):
    rows = v_ref.shape[0]
    times = rows // sx
    part = rows // pieces
    odd = odd_ref[0]
    sign = jnp.where(odd == 1, 0.5, -0.5)
    plain[...] = sign * v_ref[...].astype(F32)
    cols = jnp.concatenate([low_ref[...], high_ref[...]], axis=0)
    for m in range(pieces):
        inner = jnp.dot(u_ref[m * part : (m + 1) * part, :], shift_ref[...], preferred_element_type=F32)
        outer = lax.dot_general(cols, places_ref[m], (((0,), (0,)), ((), ())), preferred_element_type=F32)
        slope[m * part : (m + 1) * part, :] = inner + outer
    for position in range(sx):
        z = slope[pl.ds(row_at(position, sx, odd), times, stride=sx), :]
        if position + 1 < sx:
            z += plain[pl.ds(row_at(position + 1, sx, odd), times, stride=sx), :]
        if position > 0:
            z -= plain[pl.ds(row_at(position - 1, sx, odd), times, stride=sx), :]
        z_ref[position] = z
        sum_ref[position] = jnp.sum(z.reshape(times // 8, 8, LANES), axis=0)


def local_part(odd, v, u, shift, low, high, places, sx):
    rows = v.shape[0]
    pieces = places.shape[0]
    times = rows // sx
    return pl.pallas_call(
        functools.partial(local_kernel, sx, pieces),
        out_shape=(
            jax.ShapeDtypeStruct((sx, times, LANES), F32),
            jax.ShapeDtypeStruct((sx, 8, LANES), F32),
        ),
        in_specs=[SMEM] + [VMEM] * 6,
        out_specs=(VMEM,) * 2,
        scratch_shapes=[pltpu.VMEM((rows, LANES), F32), pltpu.VMEM((rows, LANES), F32)],
        compiler_params=limit(20),
        cost_estimate=pl.CostEstimate(flops=1000000000, bytes_accessed=8000000, transcendentals=0),
        name="local",
    )(odd, v, u, shift, low, high, places)


def cross_kernel(
    sx, begin, pieces, odd_ref, offsets_ref, triads_ref, z_ref, sum_ref, weights_ref, window_ref, transform_ref, *rest
):
    far = begin > 0
    halo_refs, rest = rest[:pieces], rest[pieces:]
    if far:
        before_ref, *rest = rest
    cross_ref, target_ref, full, spec, prod, packed = rest
    count, times, _ = full.shape
    blocks = offsets_ref.shape[0]
    ntri = triads_ref.shape[0]
    half = NFFT // 2
    groups = LANES // blocks
    per = ntri // groups
    wide = 2 * blocks
    pitch = blocks + 1
    odd = odd_ref[0]
    sign = jnp.where(odd == 1, 0.5, -0.5)
    if not far:
        sign = -sign
    touched = count - 1 if far else 0

    halo_sum = jnp.zeros((8, LANES), F32)
    base = 0
    for halo_ref in halo_refs:
        steps = 8 // pieces
        chunk = halo_ref.shape[0] // steps

        def add_halo(step, carry):
            at = pl.ds(pl.multiple_of(step * chunk, 8), chunk)
            to = pl.ds(pl.multiple_of(base + step * chunk, 8), chunk)
            halo = sign * halo_ref[at, :].astype(F32)
            for row in range(count):
                z = z_ref[begin + row, to, :]
                full[row, to, :] = z + halo if row == touched else z
            return carry + jnp.sum(halo.reshape(chunk // 8, 8, LANES), axis=0)

        halo_sum = lax.fori_loop(0, steps, add_halo, halo_sum)
        base += halo_ref.shape[0]
    means = []
    for row in range(count):
        total = sum_ref[begin + row]
        if row == touched:
            total = total + halo_sum
        means.append(jnp.sum(total, axis=0, keepdims=True) * (1.0 / times))

    def one_block(b, carry):
        at = pl.ds(offsets_ref[b], NFFT)
        window = window_ref[...]
        for row in range(count):
            windowed = ((full[row, at, :] - means[row]) * window).astype(BF16)
            out = jnp.dot(transform_ref[...], windowed, preferred_element_type=F32)
            spec[row, pl.ds(b, NFFT, stride=pitch), :] = out
        return carry

    lax.fori_loop(0, blocks, one_block, 0, unroll=True)
    weights = [weights_ref[pl.ds(row_at(begin + row, sx, odd), 1), :] for row in range(count)]

    def one_triad(j, carry):
        k = triads_ref[j, 0]
        l = triads_ref[j, 1]

        def take(f, row):
            re = spec[row, pl.ds(f * pitch, blocks), :]
            im = spec[row, pl.ds((f + half) * pitch, blocks), :]
            return re, im

        base = pl.multiple_of(j * wide, 8)
        for row in range(count):
            lanes = slice(row * LANES, (row + 1) * LANES)
            first_re, first_im = take(k, row)
            second_re, second_im = take(l, row)
            target_re, target_im = take(k + l, row)
            weight = weights[row]
            prod[pl.ds(base, wide), lanes] = jnp.concatenate(
                [
                    (first_re * second_re - first_im * second_im) * weight,
                    (first_re * second_im + first_im * second_re) * weight,
                ],
                axis=0,
            ).astype(BF16)
            target_ref[pl.ds(base, wide), lanes] = jnp.concatenate([target_re, target_im], axis=0).astype(BF16)
        return carry

    lax.fori_loop(0, ntri, one_triad, 0, unroll=4)

    tall = per * wide
    lane = lax.broadcasted_iota(jnp.int32, (wide, tall), 1)
    owner = lane // wide
    is_re = (lax.broadcasted_iota(jnp.int32, (blocks, tall), 1) % wide) < blocks

    def one_group(g, carry):
        at = pl.ds(pl.multiple_of(g * tall, 8), tall)
        every = lax.dot_general(
            prod[at, :], target_ref[at, :], (((1,), (1,)), ((), ())), preferred_element_type=F32
        )
        kept = every[0:wide]
        for i in range(1, per):
            kept = jnp.where(owner == i, every[i * wide : (i + 1) * wide], kept)
        by_re = kept[0:blocks]
        by_im = kept[blocks:wide]
        ahead = pltpu.roll(by_im, tall - blocks, 1)
        behind = pltpu.roll(by_im, blocks, 1)
        packed[pl.ds(pl.multiple_of(g * blocks, 8), blocks), :] = by_re + jnp.where(is_re, ahead, -behind)
        return carry

    lax.fori_loop(0, groups, one_group, 0, unroll=True)
    share = packed[...].T
    if far:
        share = share + before_ref[...]
    cross_ref[...] = share


def cross_part(begin, count, odd, offsets, triads, z, sums, halos, weights, window, transform, before=None):
    sx, times, _ = z.shape
    blocks = offsets.shape[0]
    ntri = triads.shape[0]
    groups = LANES // blocks
    wide = 2 * blocks
    tall = ntri // groups * wide
    more = list(halos) + ([] if before is None else [before])
    return pl.pallas_call(
        functools.partial(cross_kernel, sx, begin, len(halos)),
        out_shape=(
            jax.ShapeDtypeStruct((tall, LANES), F32),
            jax.ShapeDtypeStruct((ntri * wide, count * LANES), BF16),
        ),
        in_specs=[SMEM] * 3 + [VMEM] * (5 + len(more)),
        out_specs=(VMEM,) * 2,
        scratch_shapes=[
            pltpu.VMEM((count, times, LANES), F32),
            pltpu.VMEM((count, NFFT * (blocks + 1), LANES), F32),
            pltpu.VMEM((ntri * wide, count * LANES), BF16),
            pltpu.VMEM((LANES, tall), F32),
        ],
        compiler_params=limit(26),
        cost_estimate=pl.CostEstimate(flops=2000000000, bytes_accessed=4000000, transcendentals=0),
        name="cross_far" if begin else "cross_near",
    )(odd, offsets, triads, z, sums, weights, window, transform, *more)


def swap(x, axis, bit):
    count = lax.axis_size(axis)
    return lax.ppermute(x, axis, [(i, i ^ bit) for i in range(count)])


def sum_over_rest(x):
    slabs, parts = lax.axis_size("space"), lax.axis_size("freq")
    hops = [bit * parts for bit in bits_of(slabs)]
    across = [bit for bit in bits_of(parts)[1:]]
    first = hops[:1] + across + hops[1:]
    second = across + hops[:1] + hops[:0:-1]
    for one, other in zip(first, second, strict=True):
        pairs = [(i, i ^ (other if i % 2 else one)) for i in range(slabs * parts)]
        x = x + lax.ppermute(x, ("space", "freq"), pairs)
    return x


def bits_of(count):
    return [1 << n for n in range(count.bit_length() - 1)]


def modes_kernel(sx, blocks, scaling, odd_ref, core_ref, mine_ref, other_ref, near_ref, far_ref, values_ref, modes_ref, cross):
    tall = cross.shape[0]
    wide = 2 * blocks
    per = tall // wide
    groups = LANES // blocks
    odd = odd_ref[0]
    core = core_ref[0]
    half = tall // 2
    cross[pl.ds(pl.multiple_of(core * half, 8), half), :] = mine_ref[...] * scaling
    cross[pl.ds(pl.multiple_of((1 - core) * half, 8), half), :] = other_ref[...] * scaling
    lane = lax.broadcasted_iota(jnp.int32, (per, LANES), 1)
    start = lane - lane % blocks

    mat_re = [cross[pl.ds(c, per, stride=wide), :] for c in range(blocks)]
    mat_im = [cross[pl.ds(blocks + c, per, stride=wide), :] for c in range(blocks)]

    def pick(x, index):
        return jnp.take_along_axis(x, index, axis=1)

    spots = [start + c for c in range(blocks)]

    def apply(part_re, part_im):
        sums = []
        for parity in range(2):
            out_re = jnp.zeros((per, LANES), F32)
            out_im = jnp.zeros((per, LANES), F32)
            for c in range(parity, blocks, 2):
                re = pick(part_re, spots[c])
                im = pick(part_im, spots[c])
                out_re += mat_re[c] * re - mat_im[c] * im
                out_im += mat_re[c] * im + mat_im[c] * re
            sums.append((out_re, out_im))
        return sums[0][0] + sums[1][0], sums[0][1] + sums[1][1]

    def over_blocks(x):
        bit = 1
        while bit < blocks:
            x = x + pick(x, lane ^ bit)
            bit *= 2
        return x

    vec_re = jnp.full((per, LANES), 1.0 / math.sqrt(blocks), F32)
    vec_im = jnp.zeros((per, LANES), F32)
    for _ in range(POW):
        out_re, out_im = apply(vec_re, vec_im)
        length = jnp.sqrt(over_blocks(out_re * out_re + out_im * out_im))
        vec_re = out_re / length
        vec_im = out_im / length
    out_re, out_im = apply(vec_re, vec_im)
    value_re = over_blocks(vec_re * out_re + vec_im * out_im)
    value_im = over_blocks(vec_re * out_im - vec_im * out_re)

    source = jnp.minimum(lane // per * blocks, LANES - 1)
    mine = lax.broadcasted_iota(jnp.int32, (per, LANES), 0) == lane % per
    for part, value in enumerate((value_re, value_im)):
        row = jnp.sum(jnp.where(mine, pick(value, source), 0.0), axis=0, keepdims=True)
        values_ref[part : part + 1, :] = row[:, : values_ref.shape[1]]

    own = lax.broadcasted_iota(jnp.int32, (per, tall), 1) // wide == lax.broadcasted_iota(jnp.int32, (per, tall), 0)
    is_re = lax.broadcasted_iota(jnp.int32, (per, tall), 1) % wide < blocks
    for g in range(groups):
        spot = g * blocks + lane % blocks
        re = jnp.concatenate([pick(vec_re, spot)] * (tall // LANES), axis=1)
        im = jnp.concatenate([pick(vec_im, spot)] * (tall // LANES), axis=1)
        rows = jnp.concatenate(
            [
                jnp.where(own, jnp.where(is_re, re, -im), 0.0),
                jnp.where(own, jnp.where(is_re, im, re), 0.0),
            ],
            axis=0,
        )
        high = rows.astype(BF16)
        both = jnp.concatenate([high, (rows - high.astype(F32)).astype(BF16)], axis=0)
        at = slice(g * tall, (g + 1) * tall)
        for position in range(sx):
            if position + 1 < sx:
                target = near_ref[at, position * LANES : (position + 1) * LANES]
            else:
                target = far_ref[at, :]
            out = jnp.dot(both, target, preferred_element_type=F32)
            out = out[: 2 * per] + out[2 * per :]
            row = row_at(position, sx, odd)
            for part in range(2):
                first = g * per * 2 * sx + part * sx
                modes_ref[pl.ds(first + row, per, stride=2 * sx), :] = out[part * per : (part + 1) * per]


def modes_part(odd, core, mine, other, near, far, blocks, ntri, sx, scaling):
    return pl.pallas_call(
        functools.partial(modes_kernel, sx, blocks, scaling),
        out_shape=(
            jax.ShapeDtypeStruct((2, ntri), F32),
            jax.ShapeDtypeStruct((ntri * 2 * sx, LANES), F32),
        ),
        in_specs=[SMEM] * 2 + [VMEM] * 4,
        out_specs=(VMEM,) * 2,
        scratch_shapes=[pltpu.VMEM((2 * mine.shape[0], LANES), F32)],
        compiler_params=limit(12),
        name="modes",
    )(odd, core, mine, other, near, far)


def on_device(u_velocity, v_velocity, cell_weights, block_offsets, triads):
    times, sx, columns = u_velocity.shape
    blocks = block_offsets.shape[0]
    ntri = triads.shape[0]
    slabs = lax.axis_size("space")
    cells = sx * columns * slabs * lax.axis_size("freq")
    scaling = 1.0 / (blocks * math.sqrt(cells))
    pieces = 8
    window, transform = make_table(NFFT)
    picks, places = edge_columns(pieces)
    shift = 0.5 * (np.eye(LANES, k=1, dtype=np.float32) - np.eye(LANES, k=-1, dtype=np.float32))
    v = v_velocity.reshape(times * sx, columns)
    u = u_velocity.reshape(times * sx, columns)
    odd = is_odd()[None]
    core = (lax.axis_index("freq") % 2)[None]

    early, late = near_edge(odd, v, sx)
    early = swap(early, "space", 1)
    late = swap(late, "space", 1)
    low, high = columns_edge(u, jnp.asarray(picks, BF16))
    far = far_edge(odd, v, early, sx)
    inner = [(i, i + 1) for i in range(1, slabs - 1, 2)]
    far = lax.ppermute(far, "space", inner + [(b, a) for a, b in inner])
    ends = lax.axis_size("freq") - 1
    col_low = lax.ppermute(high, "freq", [(i, i + 1) for i in range(ends)])
    col_high = lax.ppermute(low, "freq", [(i + 1, i) for i in range(ends)])
    z, sums = local_part(odd, v, u, jnp.asarray(shift, BF16), col_low, col_high, jnp.asarray(places, BF16), sx)
    window = jnp.asarray(np.ascontiguousarray(np.broadcast_to(window[:, None], (NFFT, LANES))))
    transform = jnp.asarray(transform, BF16)
    share, near_target = cross_part(
        0, sx - 1, odd, block_offsets, triads, z, sums, [early, late], cell_weights, window, transform
    )
    share, far_target = cross_part(
        sx - 1, 1, odd, block_offsets, triads, z, sums, [far], cell_weights, window, transform, share
    )
    half = share.shape[0] // 2
    mine = lax.dynamic_slice_in_dim(share, core[0] * half, half, 0)
    other = lax.dynamic_slice_in_dim(share, (1 - core[0]) * half, half, 0)
    mine = mine + swap(other, "freq", 1)
    mine = sum_over_rest(mine)
    other = swap(mine, "freq", 1)
    values, modes = modes_part(odd, core, mine, other, near_target, far_target, blocks, ntri, sx, scaling)
    return (values.T, modes.reshape(ntri, 2, sx, columns))


def solution(mesh):
    return jax.shard_map(
        on_device,
        mesh=mesh,
        in_specs=(P(None, "space", "freq"), P(None, "space", "freq"), P("space", "freq"), P(), P()),
        out_specs=(P(), P(None, None, "space", "freq")),
        check_vma=False,
    )
```

```python
import functools
import math

import jax
import jax.numpy as jnp
import numpy as np
from jax import lax
from jax.experimental import pallas as pl
from jax.experimental.pallas import tpu as pltpu
from jax.sharding import PartitionSpec as P


NFFT = 256
POW = 4
LANES = 128
F32 = jnp.float32
BF16 = jnp.bfloat16
MIB = 2**20
VMEM = pl.BlockSpec(memory_space=pltpu.VMEM)
SMEM = pl.BlockSpec(memory_space=pltpu.SMEM)


def make_table(length):
    half_len = length // 2
    times_idx = np.arange(length)
    phases = np.arange(half_len)[:, None] * times_idx[None, :] % length
    angles = phases * (2.0 * math.pi / length)
    window = 0.5 - 0.5 * np.cos(times_idx * (2.0 * math.pi / length))
    scaling = 1.0 / np.sqrt(np.sum(window * window))
    transform = np.concatenate([np.cos(angles) * scaling, -np.sin(angles) * scaling], axis=0)
    return window.astype(np.float32), transform.astype(np.float32)


def edge_columns(pieces):
    picks = np.zeros((pieces, 2 * pieces, LANES), np.float32)
    places = np.zeros((pieces, 2 * pieces, LANES), np.float32)
    for m in range(pieces):
        picks[m, m, 0] = 1.0
        picks[m, pieces + m, LANES - 1] = 1.0
        places[m, m, 0] = 0.5
        places[m, pieces + m, LANES - 1] = -0.5
    return picks, places


def is_odd():
    return lax.axis_index("space") % 2


def row_at(position, sx, odd):
    return jnp.where(odd == 1, position, sx - 1 - position)


def limit(mib):
    return pltpu.CompilerParams(vmem_limit_bytes=mib * MIB)


def near_kernel(sx, odd_ref, v_ref, early_ref, late_ref, plain):
    plain[...] = v_ref[...].astype(F32)
    row = row_at(0, sx, odd_ref[0])
    early, late = early_ref.shape[0], late_ref.shape[0]
    early_ref[...] = plain[pl.ds(row, early, stride=sx), :].astype(BF16)
    late_ref[...] = plain[pl.ds(early * sx + row, late, stride=sx), :].astype(BF16)


def near_edge(odd, v, sx):
    rows = v.shape[0]
    early = rows // sx * 3 // 4
    return pl.pallas_call(
        functools.partial(near_kernel, sx),
        out_shape=(
            jax.ShapeDtypeStruct((early, LANES), BF16),
            jax.ShapeDtypeStruct((rows // sx - early, LANES), BF16),
        ),
        in_specs=[SMEM, VMEM],
        out_specs=(VMEM,) * 2,
        scratch_shapes=[pltpu.VMEM((rows, LANES), F32)],
        compiler_params=limit(8),
        name="near",
    )(odd, v)


def far_kernel(sx, odd_ref, v_ref, after_ref, far_ref, plain):
    times = far_ref.shape[0]
    plain[...] = v_ref[...].astype(F32)
    far_ref[...] = plain[pl.ds(row_at(sx - 1, sx, odd_ref[0]), times, stride=sx), :].astype(BF16)


def far_edge(odd, v, after, sx):
    rows = v.shape[0]
    return pl.pallas_call(
        functools.partial(far_kernel, sx),
        out_shape=jax.ShapeDtypeStruct((rows // sx, LANES), BF16),
        in_specs=[SMEM, VMEM, pl.BlockSpec(memory_space=pl.ANY)],
        out_specs=VMEM,
        scratch_shapes=[pltpu.VMEM((rows, LANES), F32)],
        compiler_params=limit(8),
        name="far",
    )(odd, v, after)


def columns_kernel(pieces, u_ref, picks_ref, low_ref, high_ref):
    rows = u_ref.shape[0]
    part = rows // pieces
    cols = jnp.zeros((2 * pieces, part), F32)
    for m in range(pieces):
        cols += lax.dot_general(
            picks_ref[m], u_ref[m * part : (m + 1) * part, :], (((1,), (1,)), ((), ())), preferred_element_type=F32
        )
    low_ref[...] = cols[:pieces].astype(BF16)
    high_ref[...] = cols[pieces:].astype(BF16)


def columns_edge(u, picks):
    rows = u.shape[0]
    pieces = picks.shape[0]
    return pl.pallas_call(
        functools.partial(columns_kernel, pieces),
        out_shape=(
            jax.ShapeDtypeStruct((pieces, rows // pieces), BF16),
            jax.ShapeDtypeStruct((pieces, rows // pieces), BF16),
        ),
        in_specs=[VMEM] * 2,
        out_specs=(VMEM,) * 2,
        compiler_params=limit(8),
        name="columns",
    )(u, picks)


def local_kernel(
    sx, pieces, odd_ref, v_ref, u_ref, shift_ref, low_ref, high_ref, places_ref, z_ref, sum_ref, plain, slope
):
    rows = v_ref.shape[0]
    times = rows // sx
    part = rows // pieces
    odd = odd_ref[0]
    sign = jnp.where(odd == 1, 0.5, -0.5)
    plain[...] = sign * v_ref[...].astype(F32)
    cols = jnp.concatenate([low_ref[...], high_ref[...]], axis=0)
    for m in range(pieces):
        inner = jnp.dot(u_ref[m * part : (m + 1) * part, :], shift_ref[...], preferred_element_type=F32)
        outer = lax.dot_general(cols, places_ref[m], (((0,), (0,)), ((), ())), preferred_element_type=F32)
        slope[m * part : (m + 1) * part, :] = inner + outer
    for position in range(sx):
        z = slope[pl.ds(row_at(position, sx, odd), times, stride=sx), :]
        if position + 1 < sx:
            z += plain[pl.ds(row_at(position + 1, sx, odd), times, stride=sx), :]
        if position > 0:
            z -= plain[pl.ds(row_at(position - 1, sx, odd), times, stride=sx), :]
        z_ref[position] = z
        sum_ref[position] = jnp.sum(z.reshape(times // 8, 8, LANES), axis=0)


def local_part(odd, v, u, shift, low, high, places, sx):
    rows = v.shape[0]
    pieces = places.shape[0]
    times = rows // sx
    return pl.pallas_call(
        functools.partial(local_kernel, sx, pieces),
        out_shape=(
            jax.ShapeDtypeStruct((sx, times, LANES), F32),
            jax.ShapeDtypeStruct((sx, 8, LANES), F32),
        ),
        in_specs=[SMEM] + [VMEM] * 6,
        out_specs=(VMEM,) * 2,
        scratch_shapes=[pltpu.VMEM((rows, LANES), F32), pltpu.VMEM((rows, LANES), F32)],
        compiler_params=limit(20),
        cost_estimate=pl.CostEstimate(flops=1000000000, bytes_accessed=8000000, transcendentals=0),
        name="local",
    )(odd, v, u, shift, low, high, places)


def cross_kernel(
    sx, begin, pieces, odd_ref, offsets_ref, triads_ref, z_ref, sum_ref, weights_ref, window_ref, transform_ref, *rest
):
    far = begin > 0
    halo_refs, rest = rest[:pieces], rest[pieces:]
    if far:
        before_ref, *rest = rest
    cross_ref, target_ref, full, spec, prod, packed = rest
    count, times, _ = full.shape
    blocks = offsets_ref.shape[0]
    ntri = triads_ref.shape[0]
    half = NFFT // 2
    groups = LANES // blocks
    per = ntri // groups
    wide = 2 * blocks
    pitch = blocks + 1
    odd = odd_ref[0]
    sign = jnp.where(odd == 1, 0.5, -0.5)
    if not far:
        sign = -sign
    touched = count - 1 if far else 0

    halo_sum = jnp.zeros((8, LANES), F32)
    base = 0
    for halo_ref in halo_refs:
        chunk = times // 8
        steps = halo_ref.shape[0] // chunk

        def add_halo(step, carry):
            at = pl.ds(pl.multiple_of(step * chunk, 8), chunk)
            to = pl.ds(pl.multiple_of(base + step * chunk, 8), chunk)
            halo = sign * halo_ref[at, :].astype(F32)
            for row in range(count):
                z = z_ref[begin + row, to, :]
                full[row, to, :] = z + halo if row == touched else z
            return carry + jnp.sum(halo.reshape(chunk // 8, 8, LANES), axis=0)

        halo_sum = lax.fori_loop(0, steps, add_halo, halo_sum)
        base += halo_ref.shape[0]
    means = []
    for row in range(count):
        total = sum_ref[begin + row]
        if row == touched:
            total = total + halo_sum
        means.append(jnp.sum(total, axis=0, keepdims=True) * (1.0 / times))

    def one_block(b, carry):
        at = pl.ds(offsets_ref[b], NFFT)
        window = window_ref[...]
        for row in range(count):
            windowed = ((full[row, at, :] - means[row]) * window).astype(BF16)
            out = jnp.dot(transform_ref[...], windowed, preferred_element_type=F32)
            spec[row, pl.ds(b, NFFT, stride=pitch), :] = out
        return carry

    lax.fori_loop(0, blocks, one_block, 0, unroll=True)
    weights = [weights_ref[pl.ds(row_at(begin + row, sx, odd), 1), :] for row in range(count)]

    def one_triad(j, carry):
        k = triads_ref[j, 0]
        l = triads_ref[j, 1]

        def take(f, row):
            re = spec[row, pl.ds(f * pitch, blocks), :]
            im = spec[row, pl.ds((f + half) * pitch, blocks), :]
            return re, im

        base = pl.multiple_of(j * wide, 8)
        for row in range(count):
            lanes = slice(row * LANES, (row + 1) * LANES)
            first_re, first_im = take(k, row)
            second_re, second_im = take(l, row)
            target_re, target_im = take(k + l, row)
            weight = weights[row]
            prod[pl.ds(base, wide), lanes] = jnp.concatenate(
                [
                    (first_re * second_re - first_im * second_im) * weight,
                    (first_re * second_im + first_im * second_re) * weight,
                ],
                axis=0,
            ).astype(BF16)
            target_ref[pl.ds(base, wide), lanes] = jnp.concatenate([target_re, target_im], axis=0).astype(BF16)
        return carry

    lax.fori_loop(0, ntri, one_triad, 0, unroll=4)

    tall = per * wide
    lane = lax.broadcasted_iota(jnp.int32, (wide, tall), 1)
    owner = lane // wide
    is_re = (lax.broadcasted_iota(jnp.int32, (blocks, tall), 1) % wide) < blocks

    def one_group(g, carry):
        at = pl.ds(pl.multiple_of(g * tall, 8), tall)
        every = lax.dot_general(
            prod[at, :], target_ref[at, :], (((1,), (1,)), ((), ())), preferred_element_type=F32
        )
        kept = every[0:wide]
        for i in range(1, per):
            kept = jnp.where(owner == i, every[i * wide : (i + 1) * wide], kept)
        by_re = kept[0:blocks]
        by_im = kept[blocks:wide]
        ahead = pltpu.roll(by_im, tall - blocks, 1)
        behind = pltpu.roll(by_im, blocks, 1)
        packed[pl.ds(pl.multiple_of(g * blocks, 8), blocks), :] = by_re + jnp.where(is_re, ahead, -behind)
        return carry

    lax.fori_loop(0, groups, one_group, 0, unroll=True)
    share = packed[...].T
    if far:
        share = share + before_ref[...]
    cross_ref[...] = share


def cross_part(begin, count, odd, offsets, triads, z, sums, halos, weights, window, transform, before=None):
    sx, times, _ = z.shape
    blocks = offsets.shape[0]
    ntri = triads.shape[0]
    groups = LANES // blocks
    wide = 2 * blocks
    tall = ntri // groups * wide
    more = list(halos) + ([] if before is None else [before])
    return pl.pallas_call(
        functools.partial(cross_kernel, sx, begin, len(halos)),
        out_shape=(
            jax.ShapeDtypeStruct((tall, LANES), F32),
            jax.ShapeDtypeStruct((ntri * wide, count * LANES), BF16),
        ),
        in_specs=[SMEM] * 3 + [VMEM] * (5 + len(more)),
        out_specs=(VMEM,) * 2,
        scratch_shapes=[
            pltpu.VMEM((count, times, LANES), F32),
            pltpu.VMEM((count, NFFT * (blocks + 1), LANES), F32),
            pltpu.VMEM((ntri * wide, count * LANES), BF16),
            pltpu.VMEM((LANES, tall), F32),
        ],
        compiler_params=limit(26),
        cost_estimate=pl.CostEstimate(flops=2000000000, bytes_accessed=4000000, transcendentals=0),
        name="cross_far" if begin else "cross_near",
    )(odd, offsets, triads, z, sums, weights, window, transform, *more)


def swap(x, axis, bit):
    count = lax.axis_size(axis)
    return lax.ppermute(x, axis, [(i, i ^ bit) for i in range(count)])


def sum_over_rest(x):
    slabs, parts = lax.axis_size("space"), lax.axis_size("freq")
    hops = [bit * parts for bit in bits_of(slabs)]
    across = [bit for bit in bits_of(parts)[1:]]
    first = hops[:1] + across + hops[1:]
    second = across + hops[:1] + hops[:0:-1]
    for one, other in zip(first, second, strict=True):
        pairs = [(i, i ^ (other if i % 2 else one)) for i in range(slabs * parts)]
        x = x + lax.ppermute(x, ("space", "freq"), pairs)
    return x


def bits_of(count):
    return [1 << n for n in range(count.bit_length() - 1)]


def modes_kernel(sx, blocks, scaling, odd_ref, core_ref, mine_ref, other_ref, near_ref, far_ref, values_ref, modes_ref, cross):
    tall = cross.shape[0]
    wide = 2 * blocks
    per = tall // wide
    groups = LANES // blocks
    odd = odd_ref[0]
    core = core_ref[0]
    half = tall // 2
    cross[pl.ds(pl.multiple_of(core * half, 8), half), :] = mine_ref[...] * scaling
    cross[pl.ds(pl.multiple_of((1 - core) * half, 8), half), :] = other_ref[...] * scaling
    lane = lax.broadcasted_iota(jnp.int32, (per, LANES), 1)
    start = lane - lane % blocks

    mat_re = [cross[pl.ds(c, per, stride=wide), :] for c in range(blocks)]
    mat_im = [cross[pl.ds(blocks + c, per, stride=wide), :] for c in range(blocks)]

    def pick(x, index):
        return jnp.take_along_axis(x, index, axis=1)

    spots = [start + c for c in range(blocks)]

    def apply(part_re, part_im):
        sums = []
        for parity in range(2):
            out_re = jnp.zeros((per, LANES), F32)
            out_im = jnp.zeros((per, LANES), F32)
            for c in range(parity, blocks, 2):
                re = pick(part_re, spots[c])
                im = pick(part_im, spots[c])
                out_re += mat_re[c] * re - mat_im[c] * im
                out_im += mat_re[c] * im + mat_im[c] * re
            sums.append((out_re, out_im))
        return sums[0][0] + sums[1][0], sums[0][1] + sums[1][1]

    def over_blocks(x):
        bit = 1
        while bit < blocks:
            x = x + pick(x, lane ^ bit)
            bit *= 2
        return x

    vec_re = jnp.full((per, LANES), 1.0 / math.sqrt(blocks), F32)
    vec_im = jnp.zeros((per, LANES), F32)
    for _ in range(POW):
        out_re, out_im = apply(vec_re, vec_im)
        length = jnp.sqrt(over_blocks(out_re * out_re + out_im * out_im))
        vec_re = out_re / length
        vec_im = out_im / length
    out_re, out_im = apply(vec_re, vec_im)
    value_re = over_blocks(vec_re * out_re + vec_im * out_im)
    value_im = over_blocks(vec_re * out_im - vec_im * out_re)

    source = jnp.minimum(lane // per * blocks, LANES - 1)
    mine = lax.broadcasted_iota(jnp.int32, (per, LANES), 0) == lane % per
    for part, value in enumerate((value_re, value_im)):
        row = jnp.sum(jnp.where(mine, pick(value, source), 0.0), axis=0, keepdims=True)
        values_ref[part : part + 1, :] = row[:, : values_ref.shape[1]]

    own = lax.broadcasted_iota(jnp.int32, (per, tall), 1) // wide == lax.broadcasted_iota(jnp.int32, (per, tall), 0)
    is_re = lax.broadcasted_iota(jnp.int32, (per, tall), 1) % wide < blocks
    for g in range(groups):
        spot = g * blocks + lane % blocks
        re = jnp.concatenate([pick(vec_re, spot)] * (tall // LANES), axis=1)
        im = jnp.concatenate([pick(vec_im, spot)] * (tall // LANES), axis=1)
        rows = jnp.concatenate(
            [
                jnp.where(own, jnp.where(is_re, re, -im), 0.0),
                jnp.where(own, jnp.where(is_re, im, re), 0.0),
            ],
            axis=0,
        )
        high = rows.astype(BF16)
        both = jnp.concatenate([high, (rows - high.astype(F32)).astype(BF16)], axis=0)
        at = slice(g * tall, (g + 1) * tall)
        for position in range(sx):
            if position + 1 < sx:
                target = near_ref[at, position * LANES : (position + 1) * LANES]
            else:
                target = far_ref[at, :]
            out = jnp.dot(both, target, preferred_element_type=F32)
            out = out[: 2 * per] + out[2 * per :]
            row = row_at(position, sx, odd)
            for part in range(2):
                first = g * per * 2 * sx + part * sx
                modes_ref[pl.ds(first + row, per, stride=2 * sx), :] = out[part * per : (part + 1) * per]


def modes_part(odd, core, mine, other, near, far, blocks, ntri, sx, scaling):
    return pl.pallas_call(
        functools.partial(modes_kernel, sx, blocks, scaling),
        out_shape=(
            jax.ShapeDtypeStruct((2, ntri), F32),
            jax.ShapeDtypeStruct((ntri * 2 * sx, LANES), F32),
        ),
        in_specs=[SMEM] * 2 + [VMEM] * 4,
        out_specs=(VMEM,) * 2,
        scratch_shapes=[pltpu.VMEM((2 * mine.shape[0], LANES), F32)],
        compiler_params=limit(12),
        name="modes",
    )(odd, core, mine, other, near, far)


def on_device(u_velocity, v_velocity, cell_weights, block_offsets, triads):
    times, sx, columns = u_velocity.shape
    blocks = block_offsets.shape[0]
    ntri = triads.shape[0]
    slabs = lax.axis_size("space")
    cells = sx * columns * slabs * lax.axis_size("freq")
    scaling = 1.0 / (blocks * math.sqrt(cells))
    pieces = 8
    window, transform = make_table(NFFT)
    picks, places = edge_columns(pieces)
    shift = 0.5 * (np.eye(LANES, k=1, dtype=np.float32) - np.eye(LANES, k=-1, dtype=np.float32))
    v = v_velocity.reshape(times * sx, columns)
    u = u_velocity.reshape(times * sx, columns)
    odd = is_odd()[None]
    core = (lax.axis_index("freq") % 2)[None]

    early, late = near_edge(odd, v, sx)
    early = swap(early, "space", 1)
    late = swap(late, "space", 1)
    low, high = columns_edge(u, jnp.asarray(picks, BF16))
    far = far_edge(odd, v, early, sx)
    inner = [(i, i + 1) for i in range(1, slabs - 1, 2)]
    far = lax.ppermute(far, "space", inner + [(b, a) for a, b in inner])
    ends = lax.axis_size("freq") - 1
    col_low = lax.ppermute(high, "freq", [(i, i + 1) for i in range(ends)])
    col_high = lax.ppermute(low, "freq", [(i + 1, i) for i in range(ends)])
    z, sums = local_part(odd, v, u, jnp.asarray(shift, BF16), col_low, col_high, jnp.asarray(places, BF16), sx)
    window = jnp.asarray(np.ascontiguousarray(np.broadcast_to(window[:, None], (NFFT, LANES))))
    transform = jnp.asarray(transform, BF16)
    share, near_target = cross_part(
        0, sx - 1, odd, block_offsets, triads, z, sums, [early, late], cell_weights, window, transform
    )
    share, far_target = cross_part(
        sx - 1, 1, odd, block_offsets, triads, z, sums, [far], cell_weights, window, transform, share
    )
    half = share.shape[0] // 2
    mine = lax.dynamic_slice_in_dim(share, core[0] * half, half, 0)
    other = lax.dynamic_slice_in_dim(share, (1 - core[0]) * half, half, 0)
    mine = mine + swap(other, "freq", 1)
    mine = sum_over_rest(mine)
    other = swap(mine, "freq", 1)
    values, modes = modes_part(odd, core, mine, other, near_target, far_target, blocks, ntri, sx, scaling)
    return (values.T, modes.reshape(ntri, 2, sx, columns))


def solution(mesh):
    return jax.shard_map(
        on_device,
        mesh=mesh,
        in_specs=(P(None, "space", "freq"), P(None, "space", "freq"), P("space", "freq"), P(), P()),
        out_specs=(P(), P(None, None, "space", "freq")),
        check_vma=False,
    )
```

```python
import functools
import math

import jax
import jax.numpy as jnp
import numpy as np
from jax import lax
from jax.experimental import pallas as pl
from jax.experimental.pallas import tpu as pltpu
from jax.sharding import PartitionSpec as P


NFFT = 256
POW = 4
LANES = 128
PIECES = 4
F32 = jnp.float32
BF16 = jnp.bfloat16
MIB = 2**20
VMEM = pl.BlockSpec(memory_space=pltpu.VMEM)
SMEM = pl.BlockSpec(memory_space=pltpu.SMEM)


def make_table(length):
    half_len = length // 2
    times_idx = np.arange(length)
    phases = np.arange(half_len)[:, None] * times_idx[None, :] % length
    angles = phases * (2.0 * math.pi / length)
    window = 0.5 - 0.5 * np.cos(times_idx * (2.0 * math.pi / length))
    scaling = 1.0 / np.sqrt(np.sum(window * window))
    transform = np.concatenate([np.cos(angles) * scaling, -np.sin(angles) * scaling], axis=0)
    return window.astype(np.float32), transform.astype(np.float32)


def edge_columns(pieces):
    picks = np.zeros((pieces, 2 * pieces, LANES), np.float32)
    places = np.zeros((pieces, 2 * pieces, LANES), np.float32)
    for m in range(pieces):
        picks[m, m, 0] = 1.0
        picks[m, pieces + m, LANES - 1] = 1.0
        places[m, m, 0] = 0.5
        places[m, pieces + m, LANES - 1] = -0.5
    return picks, places


def is_odd():
    return lax.axis_index("space") % 2


def row_at(position, sx, odd):
    return jnp.where(odd == 1, position, sx - 1 - position)


def limit(mib):
    return pltpu.CompilerParams(vmem_limit_bytes=mib * MIB)


def near_kernel(sx, odd_ref, v_ref, near_ref, plain):
    plain[...] = v_ref[...].astype(F32)
    near_ref[...] = plain[pl.ds(row_at(0, sx, odd_ref[0]), near_ref.shape[0], stride=sx), :].astype(BF16)


def near_edge(odd, v, sx):
    rows = v.shape[0]
    return pl.pallas_call(
        functools.partial(near_kernel, sx),
        out_shape=jax.ShapeDtypeStruct((rows // sx, LANES), BF16),
        in_specs=[SMEM, VMEM],
        out_specs=VMEM,
        scratch_shapes=[pltpu.VMEM((rows, LANES), F32)],
        compiler_params=limit(8),
        name="near",
    )(odd, v)


def far_kernel(sx, odd_ref, v_ref, *rest):
    far_refs, plain = rest[:-1], rest[-1]
    plain[...] = v_ref[...].astype(F32)
    row = row_at(sx - 1, sx, odd_ref[0])
    for k, far_ref in enumerate(far_refs):
        times = far_ref.shape[0]
        far_ref[...] = plain[pl.ds(k * times * sx + row, times, stride=sx), :].astype(BF16)


def far_edge(odd, v, sx):
    rows = v.shape[0]
    return pl.pallas_call(
        functools.partial(far_kernel, sx),
        out_shape=(jax.ShapeDtypeStruct((rows // sx // PIECES, LANES), BF16),) * PIECES,
        in_specs=[SMEM, VMEM],
        out_specs=(VMEM,) * PIECES,
        scratch_shapes=[pltpu.VMEM((rows, LANES), F32)],
        compiler_params=limit(8),
        name="far",
    )(odd, v)


def columns_kernel(pieces, side_ref, u_ref, picks_ref, near_ref, far_ref):
    rows = u_ref.shape[0]
    part = rows // pieces
    cols = jnp.zeros((2 * pieces, part), F32)
    for m in range(pieces):
        cols += lax.dot_general(
            picks_ref[m], u_ref[m * part : (m + 1) * part, :], (((1,), (1,)), ((), ())), preferred_element_type=F32
        )
    low, high = cols[:pieces], cols[pieces:]
    odd = side_ref[0] == 1
    near_ref[...] = jnp.where(odd, low, high).astype(BF16)
    far_ref[...] = jnp.where(odd, high, low).astype(BF16)


def columns_edge(side, u, picks):
    rows = u.shape[0]
    pieces = picks.shape[0]
    return pl.pallas_call(
        functools.partial(columns_kernel, pieces),
        out_shape=(jax.ShapeDtypeStruct((pieces, rows // pieces), BF16),) * 2,
        in_specs=[SMEM] + [VMEM] * 2,
        out_specs=(VMEM,) * 2,
        compiler_params=limit(8),
        name="columns",
    )(side, u, picks)


def local_kernel(
    sx, pieces, odd_ref, side_ref, v_ref, u_ref, shift_ref, near_ref, far_ref, places_ref, z_ref, sum_ref, plain, slope
):
    rows = v_ref.shape[0]
    times = rows // sx
    part = rows // pieces
    odd = odd_ref[0]
    sign = jnp.where(odd == 1, 0.5, -0.5)
    plain[...] = sign * v_ref[...].astype(F32)
    near, far = near_ref[...].astype(F32), far_ref[...].astype(F32)
    side = side_ref[0] == 1
    cols = jnp.concatenate([jnp.where(side, near, far), jnp.where(side, far, near)], axis=0).astype(BF16)
    for m in range(pieces):
        inner = jnp.dot(u_ref[m * part : (m + 1) * part, :], shift_ref[...], preferred_element_type=F32)
        outer = lax.dot_general(cols, places_ref[m], (((0,), (0,)), ((), ())), preferred_element_type=F32)
        slope[m * part : (m + 1) * part, :] = inner + outer
    for position in range(sx):
        z = slope[pl.ds(row_at(position, sx, odd), times, stride=sx), :]
        if position + 1 < sx:
            z += plain[pl.ds(row_at(position + 1, sx, odd), times, stride=sx), :]
        if position > 0:
            z -= plain[pl.ds(row_at(position - 1, sx, odd), times, stride=sx), :]
        z_ref[position] = z
        sum_ref[position] = jnp.sum(z.reshape(times // 8, 8, LANES), axis=0)


def local_part(odd, side, v, u, shift, near, far, places, sx):
    rows = v.shape[0]
    pieces = places.shape[0]
    times = rows // sx
    return pl.pallas_call(
        functools.partial(local_kernel, sx, pieces),
        out_shape=(
            jax.ShapeDtypeStruct((sx, times, LANES), F32),
            jax.ShapeDtypeStruct((sx, 8, LANES), F32),
        ),
        in_specs=[SMEM] * 2 + [VMEM] * 6,
        out_specs=(VMEM,) * 2,
        scratch_shapes=[pltpu.VMEM((rows, LANES), F32), pltpu.VMEM((rows, LANES), F32)],
        compiler_params=limit(20),
        cost_estimate=pl.CostEstimate(flops=1000000000, bytes_accessed=8000000, transcendentals=0),
        name="local",
    )(odd, side, v, u, shift, near, far, places)


def cross_kernel(
    sx, begin, pieces, blocks, ntri, scalars_ref, z_ref, sum_ref, weights_ref, window_ref, transform_ref, *rest
):
    far = begin > 0
    halo_refs, rest = rest[:pieces], rest[pieces:]
    if far:
        before_ref, *rest = rest
    cross_ref, target_ref, full, spec, prod, packed = rest
    count, times, _ = full.shape
    half = NFFT // 2
    groups = LANES // blocks
    per = ntri // groups
    wide = 2 * blocks
    pitch = blocks + 1
    odd = scalars_ref[0]
    sign = jnp.where(odd == 1, 0.5, -0.5)
    if not far:
        sign = -sign
    touched = count - 1 if far else 0

    halo_sum = jnp.zeros((8, LANES), F32)
    base = 0
    for halo_ref in halo_refs:
        chunk = times // 8
        steps = halo_ref.shape[0] // chunk

        def add_halo(step, carry):
            at = pl.ds(pl.multiple_of(step * chunk, 8), chunk)
            to = pl.ds(pl.multiple_of(base + step * chunk, 8), chunk)
            halo = sign * halo_ref[at, :].astype(F32)
            for row in range(count):
                z = z_ref[begin + row, to, :]
                full[row, to, :] = z + halo if row == touched else z
            return carry + jnp.sum(halo.reshape(chunk // 8, 8, LANES), axis=0)

        halo_sum = lax.fori_loop(0, steps, add_halo, halo_sum)
        base += halo_ref.shape[0]
    means = []
    for row in range(count):
        total = sum_ref[begin + row]
        if row == touched:
            total = total + halo_sum
        means.append(jnp.sum(total, axis=0, keepdims=True) * (1.0 / times))

    def one_block(b, carry):
        at = pl.ds(scalars_ref[1 + b], NFFT)
        window = window_ref[...]
        for row in range(count):
            windowed = ((full[row, at, :] - means[row]) * window).astype(BF16)
            out = jnp.dot(transform_ref[...], windowed, preferred_element_type=F32)
            spec[row, pl.ds(b, NFFT, stride=pitch), :] = out
        return carry

    lax.fori_loop(0, blocks, one_block, 0, unroll=True)
    weights = [weights_ref[pl.ds(row_at(begin + row, sx, odd), 1), :] for row in range(count)]

    def one_triad(j, carry):
        k = scalars_ref[1 + blocks + 2 * j]
        l = scalars_ref[2 + blocks + 2 * j]

        def take(f, row):
            re = spec[row, pl.ds(f * pitch, blocks), :]
            im = spec[row, pl.ds((f + half) * pitch, blocks), :]
            return re, im

        base = pl.multiple_of(j * wide, 8)
        for row in range(count):
            lanes = slice(row * LANES, (row + 1) * LANES)
            first_re, first_im = take(k, row)
            second_re, second_im = take(l, row)
            target_re, target_im = take(k + l, row)
            weight = weights[row]
            prod[pl.ds(base, wide), lanes] = jnp.concatenate(
                [
                    (first_re * second_re - first_im * second_im) * weight,
                    (first_re * second_im + first_im * second_re) * weight,
                ],
                axis=0,
            ).astype(BF16)
            target_ref[pl.ds(base, wide), lanes] = jnp.concatenate([target_re, target_im], axis=0).astype(BF16)
        return carry

    lax.fori_loop(0, ntri, one_triad, 0, unroll=4)

    tall = per * wide
    lane = lax.broadcasted_iota(jnp.int32, (wide, tall), 1)
    owner = lane // wide
    is_re = (lax.broadcasted_iota(jnp.int32, (blocks, tall), 1) % wide) < blocks

    def one_group(g, carry):
        at = pl.ds(pl.multiple_of(g * tall, 8), tall)
        every = lax.dot_general(
            prod[at, :], target_ref[at, :], (((1,), (1,)), ((), ())), preferred_element_type=F32
        )
        kept = every[0:wide]
        for i in range(1, per):
            kept = jnp.where(owner == i, every[i * wide : (i + 1) * wide], kept)
        by_re = kept[0:blocks]
        by_im = kept[blocks:wide]
        ahead = pltpu.roll(by_im, tall - blocks, 1)
        behind = pltpu.roll(by_im, blocks, 1)
        packed[pl.ds(pl.multiple_of(g * blocks, 8), blocks), :] = by_re + jnp.where(is_re, ahead, -behind)
        return carry

    lax.fori_loop(0, groups, one_group, 0, unroll=True)
    share = packed[...].T
    if far:
        share = share + before_ref[...]
    cross_ref[...] = share


def cross_part(begin, count, blocks, ntri, scalars, z, sums, halos, weights, window, transform, before=None):
    sx, times, _ = z.shape
    groups = LANES // blocks
    wide = 2 * blocks
    tall = ntri // groups * wide
    more = list(halos) + ([] if before is None else [before])
    return pl.pallas_call(
        functools.partial(cross_kernel, sx, begin, len(halos), blocks, ntri),
        out_shape=(
            jax.ShapeDtypeStruct((tall, LANES), F32),
            jax.ShapeDtypeStruct((ntri * wide, count * LANES), BF16),
        ),
        in_specs=[SMEM] + [VMEM] * (5 + len(more)),
        out_specs=(VMEM,) * 2,
        scratch_shapes=[
            pltpu.VMEM((count, times, LANES), F32),
            pltpu.VMEM((count, NFFT * (blocks + 1), LANES), F32),
            pltpu.VMEM((ntri * wide, count * LANES), BF16),
            pltpu.VMEM((LANES, tall), F32),
        ],
        compiler_params=limit(26),
        cost_estimate=pl.CostEstimate(flops=2000000000, bytes_accessed=4000000, transcendentals=0),
        name="cross_far" if begin else "cross_near",
    )(scalars, z, sums, weights, window, transform, *more)


def swap(x, axis, bit):
    count = lax.axis_size(axis)
    return lax.ppermute(x, axis, [(i, i ^ bit) for i in range(count)])


def sum_over_rest(x):
    slabs, parts = lax.axis_size("space"), lax.axis_size("freq")
    hops = [bit * parts for bit in bits_of(slabs)]
    across = [bit for bit in bits_of(parts)[1:]]
    first = hops[:1] + across + hops[1:]
    second = across + hops[:1] + hops[:0:-1]
    for one, other in zip(first, second, strict=True):
        pairs = [(i, i ^ (other if i % 2 else one)) for i in range(slabs * parts)]
        x = x + lax.ppermute(x, ("space", "freq"), pairs)
    return x


def bits_of(count):
    return [1 << n for n in range(count.bit_length() - 1)]


def modes_kernel(sx, blocks, scaling, odd_ref, core_ref, mine_ref, other_ref, near_ref, far_ref, values_ref, modes_ref, cross):
    tall = cross.shape[0]
    wide = 2 * blocks
    per = tall // wide
    groups = LANES // blocks
    odd = odd_ref[0]
    core = core_ref[0]
    half = tall // 2
    cross[pl.ds(pl.multiple_of(core * half, 8), half), :] = mine_ref[...] * scaling
    cross[pl.ds(pl.multiple_of((1 - core) * half, 8), half), :] = other_ref[...] * scaling
    lane = lax.broadcasted_iota(jnp.int32, (per, LANES), 1)
    start = lane - lane % blocks

    mat_re = [cross[pl.ds(c, per, stride=wide), :] for c in range(blocks)]
    mat_im = [cross[pl.ds(blocks + c, per, stride=wide), :] for c in range(blocks)]

    def pick(x, index):
        return jnp.take_along_axis(x, index, axis=1)

    spots = [start + c for c in range(blocks)]

    def tree(terms):
        while len(terms) > 1:
            terms = [sum(terms[n : n + 2]) for n in range(0, len(terms), 2)]
        return terms[0]

    def apply(part_re, part_im):
        re = [pick(part_re, spot) for spot in spots]
        im = [pick(part_im, spot) for spot in spots]
        every = range(blocks)
        out_re = tree([mat_re[c] * re[c] - mat_im[c] * im[c] for c in every])
        out_im = tree([mat_re[c] * im[c] + mat_im[c] * re[c] for c in every])
        return out_re, out_im

    def over_blocks(x):
        bit = 1
        while bit < blocks:
            if 4 * bit <= blocks:
                x = (x + pick(x, lane ^ bit)) + (pick(x, lane ^ (2 * bit)) + pick(x, lane ^ (3 * bit)))
                bit *= 4
            else:
                x = x + pick(x, lane ^ bit)
                bit *= 2
        return x

    vec_re = jnp.full((per, LANES), 1.0 / math.sqrt(blocks), F32)
    vec_im = jnp.zeros((per, LANES), F32)
    out_re, out_im = apply(vec_re, vec_im)
    for _ in range(POW):
        length = jnp.sqrt(over_blocks(out_re * out_re + out_im * out_im))
        vec_re = out_re / length
        vec_im = out_im / length
        out_re, out_im = apply(out_re, out_im)
        out_re = out_re / length
        out_im = out_im / length
    value_re = over_blocks(vec_re * out_re + vec_im * out_im)
    value_im = over_blocks(vec_re * out_im - vec_im * out_re)

    source = jnp.minimum(lane // per * blocks, LANES - 1)
    mine = lax.broadcasted_iota(jnp.int32, (per, LANES), 0) == lane % per
    for part, value in enumerate((value_re, value_im)):
        row = jnp.sum(jnp.where(mine, pick(value, source), 0.0), axis=0, keepdims=True)
        values_ref[part : part + 1, :] = row[:, : values_ref.shape[1]]

    own = lax.broadcasted_iota(jnp.int32, (per, tall), 1) // wide == lax.broadcasted_iota(jnp.int32, (per, tall), 0)
    is_re = lax.broadcasted_iota(jnp.int32, (per, tall), 1) % wide < blocks
    for g in range(groups):
        spot = g * blocks + lane % blocks
        re = jnp.concatenate([pick(vec_re, spot)] * (tall // LANES), axis=1)
        im = jnp.concatenate([pick(vec_im, spot)] * (tall // LANES), axis=1)
        rows = jnp.concatenate(
            [
                jnp.where(own, jnp.where(is_re, re, -im), 0.0),
                jnp.where(own, jnp.where(is_re, im, re), 0.0),
            ],
            axis=0,
        )
        high = rows.astype(BF16)
        both = jnp.concatenate([high, (rows - high.astype(F32)).astype(BF16)], axis=0)
        at = slice(g * tall, (g + 1) * tall)
        for position in range(sx):
            if position + 1 < sx:
                target = near_ref[at, position * LANES : (position + 1) * LANES]
            else:
                target = far_ref[at, :]
            out = jnp.dot(both, target, preferred_element_type=F32)
            out = out[: 2 * per] + out[2 * per :]
            row = row_at(position, sx, odd)
            for part in range(2):
                first = g * per * 2 * sx + part * sx
                modes_ref[pl.ds(first + row, per, stride=2 * sx), :] = out[part * per : (part + 1) * per]


def modes_part(odd, core, mine, other, near, far, blocks, ntri, sx, scaling):
    return pl.pallas_call(
        functools.partial(modes_kernel, sx, blocks, scaling),
        out_shape=(
            jax.ShapeDtypeStruct((2, ntri), F32),
            jax.ShapeDtypeStruct((ntri * 2 * sx, LANES), F32),
        ),
        in_specs=[SMEM] * 2 + [VMEM] * 4,
        out_specs=(VMEM,) * 2,
        scratch_shapes=[pltpu.VMEM((2 * mine.shape[0], LANES), F32)],
        compiler_params=limit(12),
        name="modes",
    )(odd, core, mine, other, near, far)


def between_pairs(count):
    inner = [(i, i + 1) for i in range(1, count - 1, 2)]
    return inner + [(b, a) for a, b in inner]


def start_of(k, pairs):
    return k * pairs // PIECES


def stage_far(far):
    pairs = lax.axis_size("space") // 2
    index = lax.axis_index("space")
    place = jnp.where(index % 2 == 1, index // 2, pairs - 1 - index // 2)
    staged = []
    for k, piece in enumerate(far):
        start = start_of(k, pairs)
        hops = [(2 * b + 1, 2 * b + 3) for b in range(start, pairs - 1)]
        hops += [(2 * (pairs - 1 - b), 2 * (pairs - 2 - b)) for b in range(start, pairs - 1)]
        if hops:
            passed = lax.ppermute(piece, "space", hops)
            piece = jnp.where(place > start, passed, piece)
        staged.append(piece)
    return staged


def cross_far_edge(staged):
    pairs = lax.axis_size("space") // 2
    far = []
    for k, piece in enumerate(staged):
        start = start_of(k, pairs)
        hops = []
        for b in range(pairs - 1):
            if b < start:
                hops.append((2 * b + 1, 2 * b + 2))
                hops.append((2 * (pairs - 1 - b), 2 * (pairs - 1 - b) - 1))
            else:
                hops.append((2 * b + 3, 2 * b + 2))
                hops.append((2 * (pairs - 2 - b), 2 * (pairs - 2 - b) + 1))
        far.append(lax.ppermute(piece, "space", hops))
    return far


def on_device(u_velocity, v_velocity, cell_weights, block_offsets, triads):
    times, sx, columns = u_velocity.shape
    blocks = block_offsets.shape[0]
    ntri = triads.shape[0]
    slabs = lax.axis_size("space")
    cells = sx * columns * slabs * lax.axis_size("freq")
    scaling = 1.0 / (blocks * math.sqrt(cells))
    pieces = 8
    window, transform = make_table(NFFT)
    picks, places = edge_columns(pieces)
    shift = 0.5 * (np.eye(LANES, k=1, dtype=np.float32) - np.eye(LANES, k=-1, dtype=np.float32))
    v = v_velocity.reshape(times * sx, columns)
    u = u_velocity.reshape(times * sx, columns)
    odd = is_odd()[None]
    core = (lax.axis_index("freq") % 2)[None]
    scalars = jnp.concatenate([odd, block_offsets, triads.reshape(-1)])

    near = near_edge(odd, v, sx)
    near = swap(near, "space", 1)
    far = far_edge(odd, v, sx)
    staged = stage_far(far)
    col_near, col_far = columns_edge(core, u, jnp.asarray(picks, BF16))
    col_near = swap(col_near, "freq", 1)
    col_far = lax.ppermute(col_far, "freq", between_pairs(lax.axis_size("freq")))
    z, sums = local_part(odd, core, v, u, jnp.asarray(shift, BF16), col_near, col_far, jnp.asarray(places, BF16), sx)
    far = cross_far_edge(staged)
    window = jnp.asarray(np.ascontiguousarray(np.broadcast_to(window[:, None], (NFFT, LANES))))
    transform = jnp.asarray(transform, BF16)
    share, near_target = cross_part(0, sx - 1, blocks, ntri, scalars, z, sums, [near], cell_weights, window, transform)
    share, far_target = cross_part(
        sx - 1, 1, blocks, ntri, scalars, z, sums, far, cell_weights, window, transform, share
    )
    half = share.shape[0] // 2
    mine = lax.dynamic_slice_in_dim(share, core[0] * half, half, 0)
    other = lax.dynamic_slice_in_dim(share, (1 - core[0]) * half, half, 0)
    mine = mine + swap(other, "freq", 1)
    mine = sum_over_rest(mine)
    other = swap(mine, "freq", 1)
    values, modes = modes_part(odd, core, mine, other, near_target, far_target, blocks, ntri, sx, scaling)
    return (values.T, modes.reshape(ntri, 2, sx, columns))


def solution(mesh):
    return jax.shard_map(
        on_device,
        mesh=mesh,
        in_specs=(P(None, "space", "freq"), P(None, "space", "freq"), P("space", "freq"), P(), P()),
        out_specs=(P(), P(None, None, "space", "freq")),
        check_vma=False,
    )
```

```python
import functools
import math

import jax
import jax.numpy as jnp
import numpy as np
from jax import lax
from jax.experimental import pallas as pl
from jax.experimental.pallas import tpu as pltpu
from jax.sharding import PartitionSpec as P


NFFT = 256
POW = 4
LANES = 128
AHEAD = 5
F32 = jnp.float32
BF16 = jnp.bfloat16
MIB = 2**20
VMEM = pl.BlockSpec(memory_space=pltpu.VMEM)
SMEM = pl.BlockSpec(memory_space=pltpu.SMEM)


def make_table(length):
    half_len = length // 2
    times_idx = np.arange(length)
    phases = np.arange(half_len)[:, None] * times_idx[None, :] % length
    angles = phases * (2.0 * math.pi / length)
    window = 0.5 - 0.5 * np.cos(times_idx * (2.0 * math.pi / length))
    scaling = 1.0 / np.sqrt(np.sum(window * window))
    transform = np.concatenate([np.cos(angles) * scaling, -np.sin(angles) * scaling], axis=0)
    return window.astype(np.float32), transform.astype(np.float32)


def edge_columns(pieces):
    picks = np.zeros((pieces, 2 * pieces, LANES), np.float32)
    places = np.zeros((pieces, 2 * pieces, LANES), np.float32)
    for m in range(pieces):
        picks[m, m, 0] = 1.0
        picks[m, pieces + m, LANES - 1] = 1.0
        places[m, m, 0] = 0.5
        places[m, pieces + m, LANES - 1] = -0.5
    return picks, places


def is_odd():
    return lax.axis_index("space") % 2


def row_at(position, sx, odd):
    return jnp.where(odd == 1, position, sx - 1 - position)


def limit(mib):
    return pltpu.CompilerParams(vmem_limit_bytes=mib * MIB)


def near_kernel(sx, odd_ref, v_ref, early_ref, late_ref, plain):
    plain[...] = v_ref[...].astype(F32)
    row = row_at(0, sx, odd_ref[0])
    early, late = early_ref.shape[0], late_ref.shape[0]
    early_ref[...] = plain[pl.ds(row, early, stride=sx), :].astype(BF16)
    late_ref[...] = plain[pl.ds(early * sx + row, late, stride=sx), :].astype(BF16)


def near_edge(odd, v, sx):
    rows = v.shape[0]
    early = rows // sx * AHEAD // 8
    return pl.pallas_call(
        functools.partial(near_kernel, sx),
        out_shape=(
            jax.ShapeDtypeStruct((early, LANES), BF16),
            jax.ShapeDtypeStruct((rows // sx - early, LANES), BF16),
        ),
        in_specs=[SMEM, VMEM],
        out_specs=(VMEM,) * 2,
        scratch_shapes=[pltpu.VMEM((rows, LANES), F32)],
        compiler_params=limit(8),
        name="near",
    )(odd, v)


def far_kernel(sx, odd_ref, v_ref, after_ref, far_ref, plain):
    times = far_ref.shape[0]
    plain[...] = v_ref[...].astype(F32)
    far_ref[...] = plain[pl.ds(row_at(sx - 1, sx, odd_ref[0]), times, stride=sx), :].astype(BF16)


def far_edge(odd, v, after, sx):
    rows = v.shape[0]
    return pl.pallas_call(
        functools.partial(far_kernel, sx),
        out_shape=jax.ShapeDtypeStruct((rows // sx, LANES), BF16),
        in_specs=[SMEM, VMEM, pl.BlockSpec(memory_space=pl.ANY)],
        out_specs=VMEM,
        scratch_shapes=[pltpu.VMEM((rows, LANES), F32)],
        compiler_params=limit(8),
        name="far",
    )(odd, v, after)


def columns_kernel(pieces, side_ref, u_ref, picks_ref, near_ref, far_ref):
    rows = u_ref.shape[0]
    part = rows // pieces
    cols = jnp.zeros((2 * pieces, part), F32)
    for m in range(pieces):
        cols += lax.dot_general(
            picks_ref[m], u_ref[m * part : (m + 1) * part, :], (((1,), (1,)), ((), ())), preferred_element_type=F32
        )
    low, high = cols[:pieces], cols[pieces:]
    odd = side_ref[0] == 1
    near_ref[...] = jnp.where(odd, low, high).astype(BF16)
    far_ref[...] = jnp.where(odd, high, low).astype(BF16)


def columns_edge(side, u, picks):
    rows = u.shape[0]
    pieces = picks.shape[0]
    return pl.pallas_call(
        functools.partial(columns_kernel, pieces),
        out_shape=(jax.ShapeDtypeStruct((pieces, rows // pieces), BF16),) * 2,
        in_specs=[SMEM] + [VMEM] * 2,
        out_specs=(VMEM,) * 2,
        compiler_params=limit(8),
        name="columns",
    )(side, u, picks)


def local_kernel(
    sx, pieces, odd_ref, side_ref, v_ref, u_ref, shift_ref, near_ref, far_ref, places_ref, z_ref, sum_ref, plain, slope
):
    rows = v_ref.shape[0]
    times = rows // sx
    part = rows // pieces
    odd = odd_ref[0]
    sign = jnp.where(odd == 1, 0.5, -0.5)
    plain[...] = sign * v_ref[...].astype(F32)
    near, far = near_ref[...].astype(F32), far_ref[...].astype(F32)
    side = side_ref[0] == 1
    cols = jnp.concatenate([jnp.where(side, near, far), jnp.where(side, far, near)], axis=0).astype(BF16)
    for m in range(pieces):
        inner = jnp.dot(u_ref[m * part : (m + 1) * part, :], shift_ref[...], preferred_element_type=F32)
        outer = lax.dot_general(cols, places_ref[m], (((0,), (0,)), ((), ())), preferred_element_type=F32)
        slope[m * part : (m + 1) * part, :] = inner + outer
    for position in range(sx):
        z = slope[pl.ds(row_at(position, sx, odd), times, stride=sx), :]
        if position + 1 < sx:
            z += plain[pl.ds(row_at(position + 1, sx, odd), times, stride=sx), :]
        if position > 0:
            z -= plain[pl.ds(row_at(position - 1, sx, odd), times, stride=sx), :]
        z_ref[position] = z
        sum_ref[position] = jnp.sum(z.reshape(times // 8, 8, LANES), axis=0)


def local_part(odd, side, v, u, shift, near, far, places, sx):
    rows = v.shape[0]
    pieces = places.shape[0]
    times = rows // sx
    return pl.pallas_call(
        functools.partial(local_kernel, sx, pieces),
        out_shape=(
            jax.ShapeDtypeStruct((sx, times, LANES), F32),
            jax.ShapeDtypeStruct((sx, 8, LANES), F32),
        ),
        in_specs=[SMEM] * 2 + [VMEM] * 6,
        out_specs=(VMEM,) * 2,
        scratch_shapes=[pltpu.VMEM((rows, LANES), F32), pltpu.VMEM((rows, LANES), F32)],
        compiler_params=limit(20),
        cost_estimate=pl.CostEstimate(flops=1000000000, bytes_accessed=8000000, transcendentals=0),
        name="local",
    )(odd, side, v, u, shift, near, far, places)


def cross_kernel(
    sx, begin, pieces, blocks, ntri, scalars_ref, z_ref, sum_ref, weights_ref, window_ref, transform_ref, *rest
):
    far = begin > 0
    halo_refs, rest = rest[:pieces], rest[pieces:]
    if far:
        before_ref, *rest = rest
    cross_ref, target_ref, full, spec, prod, packed = rest
    count, times, _ = full.shape
    half = NFFT // 2
    groups = LANES // blocks
    per = ntri // groups
    wide = 2 * blocks
    pitch = blocks + 1
    odd = scalars_ref[0]
    sign = jnp.where(odd == 1, 0.5, -0.5)
    if not far:
        sign = -sign
    touched = count - 1 if far else 0

    halo_sum = jnp.zeros((8, LANES), F32)
    base = 0
    for halo_ref in halo_refs:
        chunk = times // 8
        steps = halo_ref.shape[0] // chunk

        def add_halo(step, carry):
            at = pl.ds(pl.multiple_of(step * chunk, 8), chunk)
            to = pl.ds(pl.multiple_of(base + step * chunk, 8), chunk)
            halo = sign * halo_ref[at, :].astype(F32)
            for row in range(count):
                z = z_ref[begin + row, to, :]
                full[row, to, :] = z + halo if row == touched else z
            return carry + jnp.sum(halo.reshape(chunk // 8, 8, LANES), axis=0)

        halo_sum = lax.fori_loop(0, steps, add_halo, halo_sum)
        base += halo_ref.shape[0]
    means = []
    for row in range(count):
        total = sum_ref[begin + row]
        if row == touched:
            total = total + halo_sum
        means.append(jnp.sum(total, axis=0, keepdims=True) * (1.0 / times))

    def one_block(b, carry):
        at = pl.ds(scalars_ref[1 + b], NFFT)
        window = window_ref[...]
        for row in range(count):
            windowed = ((full[row, at, :] - means[row]) * window).astype(BF16)
            out = jnp.dot(transform_ref[...], windowed, preferred_element_type=F32)
            spec[row, pl.ds(b, NFFT, stride=pitch), :] = out
        return carry

    lax.fori_loop(0, blocks, one_block, 0, unroll=True)
    weights = [weights_ref[pl.ds(row_at(begin + row, sx, odd), 1), :] for row in range(count)]

    def one_triad(j, carry):
        k = scalars_ref[1 + blocks + 2 * j]
        l = scalars_ref[2 + blocks + 2 * j]

        def take(f, row):
            re = spec[row, pl.ds(f * pitch, blocks), :]
            im = spec[row, pl.ds((f + half) * pitch, blocks), :]
            return re, im

        base = pl.multiple_of(j * wide, 8)
        for row in range(count):
            lanes = slice(row * LANES, (row + 1) * LANES)
            first_re, first_im = take(k, row)
            second_re, second_im = take(l, row)
            target_re, target_im = take(k + l, row)
            weight = weights[row]
            prod[pl.ds(base, wide), lanes] = jnp.concatenate(
                [
                    (first_re * second_re - first_im * second_im) * weight,
                    (first_re * second_im + first_im * second_re) * weight,
                ],
                axis=0,
            ).astype(BF16)
            target_ref[pl.ds(base, wide), lanes] = jnp.concatenate([target_re, target_im], axis=0).astype(BF16)
        return carry

    lax.fori_loop(0, ntri, one_triad, 0, unroll=4)

    tall = per * wide
    lane = lax.broadcasted_iota(jnp.int32, (wide, tall), 1)
    owner = lane // wide
    is_re = (lax.broadcasted_iota(jnp.int32, (blocks, tall), 1) % wide) < blocks

    def one_group(g, carry):
        at = pl.ds(pl.multiple_of(g * tall, 8), tall)
        every = lax.dot_general(
            prod[at, :], target_ref[at, :], (((1,), (1,)), ((), ())), preferred_element_type=F32
        )
        kept = every[0:wide]
        for i in range(1, per):
            kept = jnp.where(owner == i, every[i * wide : (i + 1) * wide], kept)
        by_re = kept[0:blocks]
        by_im = kept[blocks:wide]
        ahead = pltpu.roll(by_im, tall - blocks, 1)
        behind = pltpu.roll(by_im, blocks, 1)
        packed[pl.ds(pl.multiple_of(g * blocks, 8), blocks), :] = by_re + jnp.where(is_re, ahead, -behind)
        return carry

    lax.fori_loop(0, groups, one_group, 0, unroll=True)
    share = packed[...].T
    if far:
        share = share + before_ref[...]
    cross_ref[...] = share


def cross_part(begin, count, blocks, ntri, scalars, z, sums, halos, weights, window, transform, before=None):
    sx, times, _ = z.shape
    groups = LANES // blocks
    wide = 2 * blocks
    tall = ntri // groups * wide
    more = list(halos) + ([] if before is None else [before])
    return pl.pallas_call(
        functools.partial(cross_kernel, sx, begin, len(halos), blocks, ntri),
        out_shape=(
            jax.ShapeDtypeStruct((tall, LANES), F32),
            jax.ShapeDtypeStruct((ntri * wide, count * LANES), BF16),
        ),
        in_specs=[SMEM] + [VMEM] * (5 + len(more)),
        out_specs=(VMEM,) * 2,
        scratch_shapes=[
            pltpu.VMEM((count, times, LANES), F32),
            pltpu.VMEM((count, NFFT * (blocks + 1), LANES), F32),
            pltpu.VMEM((ntri * wide, count * LANES), BF16),
            pltpu.VMEM((LANES, tall), F32),
        ],
        compiler_params=limit(26),
        cost_estimate=pl.CostEstimate(flops=2000000000, bytes_accessed=4000000, transcendentals=0),
        name="cross_far" if begin else "cross_near",
    )(scalars, z, sums, weights, window, transform, *more)


def swap(x, axis, bit):
    count = lax.axis_size(axis)
    return lax.ppermute(x, axis, [(i, i ^ bit) for i in range(count)])


def sum_over_rest(x):
    slabs, parts = lax.axis_size("space"), lax.axis_size("freq")
    hops = [bit * parts for bit in bits_of(slabs)]
    across = [bit for bit in bits_of(parts)[1:]]
    first = hops[:1] + across + hops[1:]
    second = across + hops[:1] + hops[:0:-1]
    for one, other in zip(first, second, strict=True):
        pairs = [(i, i ^ (other if i % 2 else one)) for i in range(slabs * parts)]
        x = x + lax.ppermute(x, ("space", "freq"), pairs)
    return x


def bits_of(count):
    return [1 << n for n in range(count.bit_length() - 1)]


def modes_kernel(sx, blocks, scaling, odd_ref, core_ref, mine_ref, other_ref, near_ref, far_ref, values_ref, modes_ref, cross):
    tall = cross.shape[0]
    wide = 2 * blocks
    per = tall // wide
    groups = LANES // blocks
    odd = odd_ref[0]
    core = core_ref[0]
    half = tall // 2
    cross[pl.ds(pl.multiple_of(core * half, 8), half), :] = mine_ref[...] * scaling
    cross[pl.ds(pl.multiple_of((1 - core) * half, 8), half), :] = other_ref[...] * scaling
    lane = lax.broadcasted_iota(jnp.int32, (per, LANES), 1)
    start = lane - lane % blocks

    mat_re = [cross[pl.ds(c, per, stride=wide), :] for c in range(blocks)]
    mat_im = [cross[pl.ds(blocks + c, per, stride=wide), :] for c in range(blocks)]

    def pick(x, index):
        return jnp.take_along_axis(x, index, axis=1)

    spots = [start + c for c in range(blocks)]

    def tree(terms):
        while len(terms) > 1:
            terms = [sum(terms[n : n + 2]) for n in range(0, len(terms), 2)]
        return terms[0]

    def apply(part_re, part_im):
        re = [pick(part_re, spot) for spot in spots]
        im = [pick(part_im, spot) for spot in spots]
        every = range(blocks)
        out_re = tree([mat_re[c] * re[c] - mat_im[c] * im[c] for c in every])
        out_im = tree([mat_re[c] * im[c] + mat_im[c] * re[c] for c in every])
        return out_re, out_im

    def over_blocks(x):
        bit = 1
        while bit < blocks:
            if 4 * bit <= blocks:
                x = (x + pick(x, lane ^ bit)) + (pick(x, lane ^ (2 * bit)) + pick(x, lane ^ (3 * bit)))
                bit *= 4
            else:
                x = x + pick(x, lane ^ bit)
                bit *= 2
        return x

    vec_re = jnp.full((per, LANES), 1.0 / math.sqrt(blocks), F32)
    vec_im = jnp.zeros((per, LANES), F32)
    out_re, out_im = apply(vec_re, vec_im)
    for _ in range(POW):
        length = jnp.sqrt(over_blocks(out_re * out_re + out_im * out_im))
        vec_re = out_re / length
        vec_im = out_im / length
        out_re, out_im = apply(out_re, out_im)
        out_re = out_re / length
        out_im = out_im / length
    value_re = over_blocks(vec_re * out_re + vec_im * out_im)
    value_im = over_blocks(vec_re * out_im - vec_im * out_re)

    source = jnp.minimum(lane // per * blocks, LANES - 1)
    mine = lax.broadcasted_iota(jnp.int32, (per, LANES), 0) == lane % per
    for part, value in enumerate((value_re, value_im)):
        row = jnp.sum(jnp.where(mine, pick(value, source), 0.0), axis=0, keepdims=True)
        values_ref[part : part + 1, :] = row[:, : values_ref.shape[1]]

    own = lax.broadcasted_iota(jnp.int32, (per, tall), 1) // wide == lax.broadcasted_iota(jnp.int32, (per, tall), 0)
    is_re = lax.broadcasted_iota(jnp.int32, (per, tall), 1) % wide < blocks
    for g in range(groups):
        spot = g * blocks + lane % blocks
        re = jnp.concatenate([pick(vec_re, spot)] * (tall // LANES), axis=1)
        im = jnp.concatenate([pick(vec_im, spot)] * (tall // LANES), axis=1)
        rows = jnp.concatenate(
            [
                jnp.where(own, jnp.where(is_re, re, -im), 0.0),
                jnp.where(own, jnp.where(is_re, im, re), 0.0),
            ],
            axis=0,
        )
        high = rows.astype(BF16)
        both = jnp.concatenate([high, (rows - high.astype(F32)).astype(BF16)], axis=0)
        at = slice(g * tall, (g + 1) * tall)
        for position in range(sx):
            if position + 1 < sx:
                target = near_ref[at, position * LANES : (position + 1) * LANES]
            else:
                target = far_ref[at, :]
            out = jnp.dot(both, target, preferred_element_type=F32)
            out = out[: 2 * per] + out[2 * per :]
            row = row_at(position, sx, odd)
            for part in range(2):
                first = g * per * 2 * sx + part * sx
                modes_ref[pl.ds(first + row, per, stride=2 * sx), :] = out[part * per : (part + 1) * per]


def modes_part(odd, core, mine, other, near, far, blocks, ntri, sx, scaling):
    return pl.pallas_call(
        functools.partial(modes_kernel, sx, blocks, scaling),
        out_shape=(
            jax.ShapeDtypeStruct((2, ntri), F32),
            jax.ShapeDtypeStruct((ntri * 2 * sx, LANES), F32),
        ),
        in_specs=[SMEM] * 2 + [VMEM] * 4,
        out_specs=(VMEM,) * 2,
        scratch_shapes=[pltpu.VMEM((2 * mine.shape[0], LANES), F32)],
        compiler_params=limit(12),
        name="modes",
    )(odd, core, mine, other, near, far)


def between_pairs(count):
    inner = [(i, i + 1) for i in range(1, count - 1, 2)]
    return inner + [(b, a) for a, b in inner]


def on_device(u_velocity, v_velocity, cell_weights, block_offsets, triads):
    times, sx, columns = u_velocity.shape
    blocks = block_offsets.shape[0]
    ntri = triads.shape[0]
    slabs = lax.axis_size("space")
    cells = sx * columns * slabs * lax.axis_size("freq")
    scaling = 1.0 / (blocks * math.sqrt(cells))
    pieces = 8
    window, transform = make_table(NFFT)
    picks, places = edge_columns(pieces)
    shift = 0.5 * (np.eye(LANES, k=1, dtype=np.float32) - np.eye(LANES, k=-1, dtype=np.float32))
    v = v_velocity.reshape(times * sx, columns)
    u = u_velocity.reshape(times * sx, columns)
    odd = is_odd()[None]
    core = (lax.axis_index("freq") % 2)[None]
    scalars = jnp.concatenate([odd, block_offsets, triads.reshape(-1)])

    early, late = near_edge(odd, v, sx)
    early = swap(early, "space", 1)
    late = swap(late, "space", 1)
    col_near, col_far = columns_edge(core, u, jnp.asarray(picks, BF16))
    col_near = swap(col_near, "freq", 1)
    col_far = lax.ppermute(col_far, "freq", between_pairs(lax.axis_size("freq")))
    z, sums = local_part(odd, core, v, u, jnp.asarray(shift, BF16), col_near, col_far, jnp.asarray(places, BF16), sx)
    far = far_edge(odd, v, early, sx)
    far = lax.ppermute(far, "space", between_pairs(slabs))
    window = jnp.asarray(np.ascontiguousarray(np.broadcast_to(window[:, None], (NFFT, LANES))))
    transform = jnp.asarray(transform, BF16)
    share, near_target = cross_part(
        0, sx - 1, blocks, ntri, scalars, z, sums, [early, late], cell_weights, window, transform
    )
    share, far_target = cross_part(
        sx - 1, 1, blocks, ntri, scalars, z, sums, [far], cell_weights, window, transform, share
    )
    half = share.shape[0] // 2
    mine = lax.dynamic_slice_in_dim(share, core[0] * half, half, 0)
    other = lax.dynamic_slice_in_dim(share, (1 - core[0]) * half, half, 0)
    mine = mine + swap(other, "freq", 1)
    mine = sum_over_rest(mine)
    other = swap(mine, "freq", 1)
    values, modes = modes_part(odd, core, mine, other, near_target, far_target, blocks, ntri, sx, scaling)
    return (values.T, modes.reshape(ntri, 2, sx, columns))


def solution(mesh):
    return jax.shard_map(
        on_device,
        mesh=mesh,
        in_specs=(P(None, "space", "freq"), P(None, "space", "freq"), P("space", "freq"), P(), P()),
        out_specs=(P(), P(None, None, "space", "freq")),
        check_vma=False,
    )
```

```python
import functools
import math

import jax
import jax.numpy as jnp
import numpy as np
from jax import lax
from jax.experimental import pallas as pl
from jax.experimental.pallas import tpu as pltpu
from jax.sharding import PartitionSpec as P


NFFT = 256
POW = 4
LANES = 128
AHEAD = 5
F32 = jnp.float32
BF16 = jnp.bfloat16
MIB = 2**20
VMEM = pl.BlockSpec(memory_space=pltpu.VMEM)
SMEM = pl.BlockSpec(memory_space=pltpu.SMEM)


def make_table(length):
    half_len = length // 2
    times_idx = np.arange(length)
    phases = np.arange(half_len)[:, None] * times_idx[None, :] % length
    angles = phases * (2.0 * math.pi / length)
    window = 0.5 - 0.5 * np.cos(times_idx * (2.0 * math.pi / length))
    scaling = 1.0 / np.sqrt(np.sum(window * window))
    transform = np.concatenate([np.cos(angles) * scaling, -np.sin(angles) * scaling], axis=0)
    return window.astype(np.float32), transform.astype(np.float32)


def edge_columns(pieces):
    picks = np.zeros((pieces, 2 * pieces, LANES), np.float32)
    places = np.zeros((pieces, 2 * pieces, LANES), np.float32)
    for m in range(pieces):
        picks[m, m, 0] = 1.0
        picks[m, pieces + m, LANES - 1] = 1.0
        places[m, m, 0] = 0.5
        places[m, pieces + m, LANES - 1] = -0.5
    return picks, places


def is_odd():
    return lax.axis_index("space") % 2


def row_at(position, sx, odd):
    return jnp.where(odd == 1, position, sx - 1 - position)


def limit(mib):
    return pltpu.CompilerParams(vmem_limit_bytes=mib * MIB)


def near_kernel(sx, odd_ref, v_ref, early_ref, late_ref, plain):
    plain[...] = v_ref[...].astype(F32)
    row = row_at(0, sx, odd_ref[0])
    early, late = early_ref.shape[0], late_ref.shape[0]
    early_ref[...] = plain[pl.ds(row, early, stride=sx), :].astype(BF16)
    late_ref[...] = plain[pl.ds(early * sx + row, late, stride=sx), :].astype(BF16)


def near_edge(odd, v, sx):
    rows = v.shape[0]
    early = rows // sx * AHEAD // 8
    return pl.pallas_call(
        functools.partial(near_kernel, sx),
        out_shape=(
            jax.ShapeDtypeStruct((early, LANES), BF16),
            jax.ShapeDtypeStruct((rows // sx - early, LANES), BF16),
        ),
        in_specs=[SMEM, VMEM],
        out_specs=(VMEM,) * 2,
        scratch_shapes=[pltpu.VMEM((rows, LANES), F32)],
        compiler_params=limit(8),
        name="near",
    )(odd, v)


def far_kernel(sx, odd_ref, v_ref, far_ref, plain):
    plain[...] = v_ref[...].astype(F32)
    far_ref[...] = plain[pl.ds(row_at(sx - 1, sx, odd_ref[0]), far_ref.shape[0], stride=sx), :].astype(BF16)


def far_edge(odd, v, sx):
    rows = v.shape[0]
    return pl.pallas_call(
        functools.partial(far_kernel, sx),
        out_shape=jax.ShapeDtypeStruct((rows // sx, LANES), BF16),
        in_specs=[SMEM, VMEM],
        out_specs=VMEM,
        scratch_shapes=[pltpu.VMEM((rows, LANES), F32)],
        compiler_params=limit(8),
        name="far",
    )(odd, v)


def columns_kernel(pieces, side_ref, u_ref, picks_ref, near_ref, far_ref):
    rows = u_ref.shape[0]
    part = rows // pieces
    cols = jnp.zeros((2 * pieces, part), F32)
    for m in range(pieces):
        cols += lax.dot_general(
            picks_ref[m], u_ref[m * part : (m + 1) * part, :], (((1,), (1,)), ((), ())), preferred_element_type=F32
        )
    low, high = cols[:pieces], cols[pieces:]
    odd = side_ref[0] == 1
    near_ref[...] = jnp.where(odd, low, high).astype(BF16)
    far_ref[...] = jnp.where(odd, high, low).astype(BF16)


def columns_edge(side, u, picks):
    rows = u.shape[0]
    pieces = picks.shape[0]
    return pl.pallas_call(
        functools.partial(columns_kernel, pieces),
        out_shape=(jax.ShapeDtypeStruct((pieces, rows // pieces), BF16),) * 2,
        in_specs=[SMEM] + [VMEM] * 2,
        out_specs=(VMEM,) * 2,
        compiler_params=limit(8),
        name="columns",
    )(side, u, picks)


def local_kernel(
    sx, pieces, odd_ref, side_ref, v_ref, u_ref, shift_ref, near_ref, far_ref, places_ref, z_ref, sum_ref, plain, slope
):
    rows = v_ref.shape[0]
    times = rows // sx
    part = rows // pieces
    odd = odd_ref[0]
    sign = jnp.where(odd == 1, 0.5, -0.5)
    plain[...] = sign * v_ref[...].astype(F32)
    near, far = near_ref[...].astype(F32), far_ref[...].astype(F32)
    side = side_ref[0] == 1
    cols = jnp.concatenate([jnp.where(side, near, far), jnp.where(side, far, near)], axis=0).astype(BF16)
    for m in range(pieces):
        inner = jnp.dot(u_ref[m * part : (m + 1) * part, :], shift_ref[...], preferred_element_type=F32)
        outer = lax.dot_general(cols, places_ref[m], (((0,), (0,)), ((), ())), preferred_element_type=F32)
        slope[m * part : (m + 1) * part, :] = inner + outer
    for position in range(sx):
        z = slope[pl.ds(row_at(position, sx, odd), times, stride=sx), :]
        if position + 1 < sx:
            z += plain[pl.ds(row_at(position + 1, sx, odd), times, stride=sx), :]
        if position > 0:
            z -= plain[pl.ds(row_at(position - 1, sx, odd), times, stride=sx), :]
        z_ref[position] = z
        sum_ref[position] = jnp.sum(z.reshape(times // 8, 8, LANES), axis=0)


def local_part(odd, side, v, u, shift, near, far, places, sx):
    rows = v.shape[0]
    pieces = places.shape[0]
    times = rows // sx
    return pl.pallas_call(
        functools.partial(local_kernel, sx, pieces),
        out_shape=(
            jax.ShapeDtypeStruct((sx, times, LANES), F32),
            jax.ShapeDtypeStruct((sx, 8, LANES), F32),
        ),
        in_specs=[SMEM] * 2 + [VMEM] * 6,
        out_specs=(VMEM,) * 2,
        scratch_shapes=[pltpu.VMEM((rows, LANES), F32), pltpu.VMEM((rows, LANES), F32)],
        compiler_params=limit(20),
        cost_estimate=pl.CostEstimate(flops=1000000000, bytes_accessed=8000000, transcendentals=0),
        name="local",
    )(odd, side, v, u, shift, near, far, places)


def cross_kernel(
    sx, begin, pieces, odd_ref, core_ref, offsets_ref, triads_ref, z_ref, sum_ref, weights_ref, window_ref, transform_ref,
    *rest,
):
    far = begin > 0
    halo_refs, rest = rest[:pieces], rest[pieces:]
    if far:
        before_ref, *rest = rest
    *cross_refs, target_ref, full, spec, prod, packed = rest
    count, times, _ = full.shape
    blocks = offsets_ref.shape[0]
    ntri = triads_ref.shape[1]
    half = NFFT // 2
    groups = LANES // blocks
    per = ntri // groups
    wide = 2 * blocks
    pitch = blocks + 1
    odd = odd_ref[0]
    sign = jnp.where(odd == 1, 0.5, -0.5)
    if not far:
        sign = -sign
    touched = count - 1 if far else 0

    halo_sum = jnp.zeros((8, LANES), F32)
    base = 0
    for halo_ref in halo_refs:
        chunk = times // 8
        steps = halo_ref.shape[0] // chunk

        def add_halo(step, carry):
            at = pl.ds(pl.multiple_of(step * chunk, 8), chunk)
            to = pl.ds(pl.multiple_of(base + step * chunk, 8), chunk)
            halo = sign * halo_ref[at, :].astype(F32)
            for row in range(count):
                z = z_ref[begin + row, to, :]
                full[row, to, :] = z + halo if row == touched else z
            return carry + jnp.sum(halo.reshape(chunk // 8, 8, LANES), axis=0)

        halo_sum = lax.fori_loop(0, steps, add_halo, halo_sum)
        base += halo_ref.shape[0]
    means = []
    for row in range(count):
        total = sum_ref[begin + row]
        if row == touched:
            total = total + halo_sum
        means.append(jnp.sum(total, axis=0, keepdims=True) * (1.0 / times))

    def two_blocks(h, carry):
        window = window_ref[...]
        pair = (2 * h, 2 * h + 1)
        for row in range(count):
            windowed = [
                ((full[row, pl.ds(offsets_ref[b], NFFT), :] - means[row]) * window).astype(BF16) for b in pair
            ]
            out = jnp.dot(transform_ref[...], jnp.concatenate(windowed, axis=1), preferred_element_type=F32)
            for n, b in enumerate(pair):
                spec[row, pl.ds(b, NFFT, stride=pitch), :] = out[:, n * LANES : (n + 1) * LANES]
        return carry

    lax.fori_loop(0, blocks // 2, two_blocks, 0, unroll=True)
    weights = [weights_ref[pl.ds(row_at(begin + row, sx, odd), 1), :] for row in range(count)]

    def one_triad(j, carry):
        k = triads_ref[0, j]
        l = triads_ref[1, j]

        def take(f, row):
            re = spec[row, pl.ds(f * pitch, blocks), :]
            im = spec[row, pl.ds((f + half) * pitch, blocks), :]
            return re, im

        base = pl.multiple_of(j * wide, 8)
        for row in range(count):
            lanes = slice(row * LANES, (row + 1) * LANES)
            first_re, first_im = take(k, row)
            second_re, second_im = take(l, row)
            target_re, target_im = take(k + l, row)
            weight = weights[row]
            prod[pl.ds(base, wide), lanes] = jnp.concatenate(
                [
                    (first_re * second_re - first_im * second_im) * weight,
                    (first_re * second_im + first_im * second_re) * weight,
                ],
                axis=0,
            ).astype(BF16)
            target_ref[pl.ds(base, wide), lanes] = jnp.concatenate([target_re, target_im], axis=0).astype(BF16)
        return carry

    lax.fori_loop(0, ntri, one_triad, 0, unroll=4)

    tall = per * wide
    lane = lax.broadcasted_iota(jnp.int32, (wide, tall), 1)
    owner = lane // wide
    is_re = (lax.broadcasted_iota(jnp.int32, (blocks, tall), 1) % wide) < blocks

    def one_group(g, carry):
        at = pl.ds(pl.multiple_of(g * tall, 8), tall)
        every = lax.dot_general(
            prod[at, :], target_ref[at, :], (((1,), (1,)), ((), ())), preferred_element_type=F32
        )
        kept = every[0:wide]
        for i in range(1, per):
            kept = jnp.where(owner == i, every[i * wide : (i + 1) * wide], kept)
        by_re = kept[0:blocks]
        by_im = kept[blocks:wide]
        ahead = pltpu.roll(by_im, tall - blocks, 1)
        behind = pltpu.roll(by_im, blocks, 1)
        packed[pl.ds(pl.multiple_of(g * blocks, 8), blocks), :] = by_re + jnp.where(is_re, ahead, -behind)
        return carry

    lax.fori_loop(0, groups, one_group, 0, unroll=True)
    share = packed[...].T
    if not far:
        cross_refs[0][...] = share
        return
    share = share + before_ref[...]
    lower, upper = share[: tall // 2], share[tall // 2 :]
    second = core_ref[0] == 1
    cross_refs[0][...] = jnp.where(second, upper, lower)
    cross_refs[1][...] = jnp.where(second, lower, upper)


def cross_part(begin, count, odd, core, offsets, triads, z, sums, halos, weights, window, transform, before=None):
    sx, times, _ = z.shape
    blocks = offsets.shape[0]
    ntri = triads.shape[1]
    groups = LANES // blocks
    wide = 2 * blocks
    tall = ntri // groups * wide
    more = list(halos) + ([] if before is None else [before])
    parts = 1 if before is None else 2
    return pl.pallas_call(
        functools.partial(cross_kernel, sx, begin, len(halos)),
        out_shape=(jax.ShapeDtypeStruct((tall // parts, LANES), F32),) * parts
        + (jax.ShapeDtypeStruct((ntri * wide, count * LANES), BF16),),
        in_specs=[SMEM] * 4 + [VMEM] * (5 + len(more)),
        out_specs=(VMEM,) * (parts + 1),
        scratch_shapes=[
            pltpu.VMEM((count, times, LANES), F32),
            pltpu.VMEM((count, NFFT * (blocks + 1), LANES), F32),
            pltpu.VMEM((ntri * wide, count * LANES), BF16),
            pltpu.VMEM((LANES, tall), F32),
        ],
        compiler_params=limit(26),
        cost_estimate=pl.CostEstimate(flops=2000000000, bytes_accessed=4000000, transcendentals=0),
        name="cross_far" if begin else "cross_near",
    )(odd, core, offsets, triads, z, sums, weights, window, transform, *more)


def swap(x, axis, bit):
    count = lax.axis_size(axis)
    return lax.ppermute(x, axis, [(i, i ^ bit) for i in range(count)])


def sum_over_rest(x):
    slabs, parts = lax.axis_size("space"), lax.axis_size("freq")
    hops = [bit * parts for bit in bits_of(slabs)]
    across = [bit for bit in bits_of(parts)[1:]]
    first = hops[:1] + across + hops[1:]
    second = across + hops[:1] + hops[:0:-1]
    for one, other in zip(first, second, strict=True):
        pairs = [(i, i ^ (other if i % 2 else one)) for i in range(slabs * parts)]
        x = x + lax.ppermute(x, ("space", "freq"), pairs)
    return x


def bits_of(count):
    return [1 << n for n in range(count.bit_length() - 1)]


def modes_kernel(sx, blocks, scaling, odd_ref, core_ref, mine_ref, other_ref, near_ref, far_ref, values_ref, modes_ref, cross):
    tall = cross.shape[0]
    wide = 2 * blocks
    per = tall // wide
    groups = LANES // blocks
    odd = odd_ref[0]
    core = core_ref[0]
    half = tall // 2
    cross[pl.ds(pl.multiple_of(core * half, 8), half), :] = mine_ref[...] * scaling
    cross[pl.ds(pl.multiple_of((1 - core) * half, 8), half), :] = other_ref[...] * scaling
    lane = lax.broadcasted_iota(jnp.int32, (per, LANES), 1)
    start = lane - lane % blocks

    mat_re = [cross[pl.ds(c, per, stride=wide), :] for c in range(blocks)]
    mat_im = [cross[pl.ds(blocks + c, per, stride=wide), :] for c in range(blocks)]

    def pick(x, index):
        return jnp.take_along_axis(x, index, axis=1)

    spots = [start + c for c in range(blocks)]

    def tree(terms):
        while len(terms) > 1:
            terms = [sum(terms[n : n + 2]) for n in range(0, len(terms), 2)]
        return terms[0]

    def apply(part_re, part_im):
        re = [pick(part_re, spot) for spot in spots]
        im = [pick(part_im, spot) for spot in spots]
        every = range(blocks)
        out_re = tree([mat_re[c] * re[c] - mat_im[c] * im[c] for c in every])
        out_im = tree([mat_re[c] * im[c] + mat_im[c] * re[c] for c in every])
        return out_re, out_im

    def over_blocks(x):
        bit = 1
        while bit < blocks:
            if 4 * bit <= blocks:
                x = (x + pick(x, lane ^ bit)) + (pick(x, lane ^ (2 * bit)) + pick(x, lane ^ (3 * bit)))
                bit *= 4
            else:
                x = x + pick(x, lane ^ bit)
                bit *= 2
        return x

    vec_re = jnp.full((per, LANES), 1.0 / math.sqrt(blocks), F32)
    vec_im = jnp.zeros((per, LANES), F32)
    out_re, out_im = apply(vec_re, vec_im)
    for _ in range(POW):
        length = jnp.sqrt(over_blocks(out_re * out_re + out_im * out_im))
        vec_re = out_re / length
        vec_im = out_im / length
        out_re, out_im = apply(out_re, out_im)
        out_re = out_re / length
        out_im = out_im / length
    value_re = over_blocks(vec_re * out_re + vec_im * out_im)
    value_im = over_blocks(vec_re * out_im - vec_im * out_re)

    source = jnp.minimum(lane // per * blocks, LANES - 1)
    mine = lax.broadcasted_iota(jnp.int32, (per, LANES), 0) == lane % per
    for part, value in enumerate((value_re, value_im)):
        row = jnp.sum(jnp.where(mine, pick(value, source), 0.0), axis=0, keepdims=True)
        values_ref[part : part + 1, :] = row[:, : values_ref.shape[1]]

    own = lax.broadcasted_iota(jnp.int32, (per, tall), 1) // wide == lax.broadcasted_iota(jnp.int32, (per, tall), 0)
    is_re = lax.broadcasted_iota(jnp.int32, (per, tall), 1) % wide < blocks
    for g in range(groups):
        spot = g * blocks + lane % blocks
        re = jnp.concatenate([pick(vec_re, spot)] * (tall // LANES), axis=1)
        im = jnp.concatenate([pick(vec_im, spot)] * (tall // LANES), axis=1)
        rows = jnp.concatenate(
            [
                jnp.where(own, jnp.where(is_re, re, -im), 0.0),
                jnp.where(own, jnp.where(is_re, im, re), 0.0),
            ],
            axis=0,
        )
        high = rows.astype(BF16)
        both = jnp.concatenate([high, (rows - high.astype(F32)).astype(BF16)], axis=0)
        at = slice(g * tall, (g + 1) * tall)
        for position in range(sx):
            if position + 1 < sx:
                target = near_ref[at, position * LANES : (position + 1) * LANES]
            else:
                target = far_ref[at, :]
            out = jnp.dot(both, target, preferred_element_type=F32)
            out = out[: 2 * per] + out[2 * per :]
            row = row_at(position, sx, odd)
            for part in range(2):
                first = g * per * 2 * sx + part * sx
                modes_ref[pl.ds(first + row, per, stride=2 * sx), :] = out[part * per : (part + 1) * per]


def modes_part(odd, core, mine, other, near, far, blocks, ntri, sx, scaling):
    return pl.pallas_call(
        functools.partial(modes_kernel, sx, blocks, scaling),
        out_shape=(
            jax.ShapeDtypeStruct((2, ntri), F32),
            jax.ShapeDtypeStruct((ntri * 2 * sx, LANES), F32),
        ),
        in_specs=[SMEM] * 2 + [VMEM] * 4,
        out_specs=(VMEM,) * 2,
        scratch_shapes=[pltpu.VMEM((2 * mine.shape[0], LANES), F32)],
        compiler_params=limit(12),
        name="modes",
    )(odd, core, mine, other, near, far)


def between_pairs(count):
    inner = [(i, i + 1) for i in range(1, count - 1, 2)]
    return inner + [(b, a) for a, b in inner]


def on_device(u_velocity, v_velocity, cell_weights, block_offsets, triads):
    times, sx, columns = u_velocity.shape
    blocks = block_offsets.shape[0]
    ntri = triads.shape[0]
    slabs = lax.axis_size("space")
    cells = sx * columns * slabs * lax.axis_size("freq")
    scaling = 1.0 / (blocks * math.sqrt(cells))
    pieces = 8
    window, transform = make_table(NFFT)
    picks, places = edge_columns(pieces)
    shift = 0.5 * (np.eye(LANES, k=1, dtype=np.float32) - np.eye(LANES, k=-1, dtype=np.float32))
    v = v_velocity.reshape(times * sx, columns)
    u = u_velocity.reshape(times * sx, columns)
    odd = is_odd()[None]
    core = (lax.axis_index("freq") % 2)[None]
    pairs = triads.T

    early, late = near_edge(odd, v, sx)
    early = swap(early, "space", 1)
    late = swap(late, "space", 1)
    col_near, col_far = columns_edge(core, u, jnp.asarray(picks, BF16))
    col_near = swap(col_near, "freq", 1)
    col_far = lax.ppermute(col_far, "freq", between_pairs(lax.axis_size("freq")))
    z, sums = local_part(odd, core, v, u, jnp.asarray(shift, BF16), col_near, col_far, jnp.asarray(places, BF16), sx)
    far = far_edge(odd, v, sx)
    far = lax.ppermute(far, "space", between_pairs(slabs))
    window = jnp.asarray(np.ascontiguousarray(np.broadcast_to(window[:, None], (NFFT, LANES))))
    transform = jnp.asarray(transform, BF16)
    share, near_target = cross_part(
        0, sx - 1, odd, core, block_offsets, pairs, z, sums, [early, late], cell_weights, window, transform
    )
    mine, other, far_target = cross_part(
        sx - 1, 1, odd, core, block_offsets, pairs, z, sums, [far], cell_weights, window, transform, share
    )
    mine = mine + swap(other, "freq", 1)
    mine = sum_over_rest(mine)
    other = swap(mine, "freq", 1)
    values, modes = modes_part(odd, core, mine, other, near_target, far_target, blocks, ntri, sx, scaling)
    return (values.T, modes.reshape(ntri, 2, sx, columns))


def solution(mesh):
    return jax.shard_map(
        on_device,
        mesh=mesh,
        in_specs=(P(None, "space", "freq"), P(None, "space", "freq"), P("space", "freq"), P(), P()),
        out_specs=(P(), P(None, None, "space", "freq")),
        check_vma=False,
    )
```

```python
import functools
import math

import jax
import jax.numpy as jnp
import numpy as np
from jax import lax
from jax.experimental import pallas as pl
from jax.experimental.pallas import tpu as pltpu
from jax.sharding import PartitionSpec as P


NFFT = 256
POW = 4
LANES = 128
AHEAD = 11
F32 = jnp.float32
BF16 = jnp.bfloat16
MIB = 2**20
VMEM = pl.BlockSpec(memory_space=pltpu.VMEM)
SMEM = pl.BlockSpec(memory_space=pltpu.SMEM)


def make_table(length):
    half_len = length // 2
    times_idx = np.arange(length)
    phases = np.arange(half_len)[:, None] * times_idx[None, :] % length
    angles = phases * (2.0 * math.pi / length)
    window = 0.5 - 0.5 * np.cos(times_idx * (2.0 * math.pi / length))
    scaling = 1.0 / np.sqrt(np.sum(window * window))
    transform = np.concatenate([np.cos(angles) * scaling, -np.sin(angles) * scaling], axis=0)
    return window.astype(np.float32), transform.astype(np.float32)


def edge_columns(pieces):
    picks = np.zeros((pieces, 2 * pieces, LANES), np.float32)
    places = np.zeros((pieces, 2 * pieces, LANES), np.float32)
    for m in range(pieces):
        picks[m, m, 0] = 1.0
        picks[m, pieces + m, LANES - 1] = 1.0
        places[m, m, 0] = 0.5
        places[m, pieces + m, LANES - 1] = -0.5
    return picks, places


def is_odd():
    return lax.axis_index("space") % 2


def row_at(position, sx, odd):
    return jnp.where(odd == 1, position, sx - 1 - position)


def limit(mib):
    return pltpu.CompilerParams(vmem_limit_bytes=mib * MIB)


def near_kernel(sx, odd_ref, v_ref, early_ref, late_ref, plain):
    plain[...] = v_ref[...].astype(F32)
    row = row_at(0, sx, odd_ref[0])
    early, late = early_ref.shape[0], late_ref.shape[0]
    early_ref[...] = plain[pl.ds(row, early, stride=sx), :].astype(BF16)
    late_ref[...] = plain[pl.ds(early * sx + row, late, stride=sx), :].astype(BF16)


def near_edge(odd, v, sx):
    rows = v.shape[0]
    early = rows // sx * AHEAD // 1024 * 64
    return pl.pallas_call(
        functools.partial(near_kernel, sx),
        out_shape=(
            jax.ShapeDtypeStruct((early, LANES), BF16),
            jax.ShapeDtypeStruct((rows // sx - early, LANES), BF16),
        ),
        in_specs=[SMEM, VMEM],
        out_specs=(VMEM,) * 2,
        scratch_shapes=[pltpu.VMEM((rows, LANES), F32)],
        compiler_params=limit(8),
        name="near",
    )(odd, v)


def far_kernel(sx, odd_ref, v_ref, far_ref, plain):
    plain[...] = v_ref[...].astype(F32)
    far_ref[...] = plain[pl.ds(row_at(sx - 1, sx, odd_ref[0]), far_ref.shape[0], stride=sx), :].astype(BF16)


def far_edge(odd, v, sx):
    rows = v.shape[0]
    return pl.pallas_call(
        functools.partial(far_kernel, sx),
        out_shape=jax.ShapeDtypeStruct((rows // sx, LANES), BF16),
        in_specs=[SMEM, VMEM],
        out_specs=VMEM,
        scratch_shapes=[pltpu.VMEM((rows, LANES), F32)],
        compiler_params=limit(8),
        name="far",
    )(odd, v)


def columns_kernel(pieces, side_ref, u_ref, picks_ref, near_ref, far_ref):
    rows = u_ref.shape[0]
    part = rows // pieces
    cols = jnp.zeros((2 * pieces, part), F32)
    for m in range(pieces):
        cols += lax.dot_general(
            picks_ref[m], u_ref[m * part : (m + 1) * part, :], (((1,), (1,)), ((), ())), preferred_element_type=F32
        )
    low, high = cols[:pieces], cols[pieces:]
    odd = side_ref[0] == 1
    near_ref[...] = jnp.where(odd, low, high).astype(BF16)
    far_ref[...] = jnp.where(odd, high, low).astype(BF16)


def columns_edge(side, u, picks):
    rows = u.shape[0]
    pieces = picks.shape[0]
    return pl.pallas_call(
        functools.partial(columns_kernel, pieces),
        out_shape=(jax.ShapeDtypeStruct((pieces, rows // pieces), BF16),) * 2,
        in_specs=[SMEM] + [VMEM] * 2,
        out_specs=(VMEM,) * 2,
        compiler_params=limit(8),
        name="columns",
    )(side, u, picks)


def local_kernel(
    sx, pieces, odd_ref, side_ref, v_ref, u_ref, shift_ref, near_ref, far_ref, places_ref, z_ref, sum_ref, plain, slope
):
    rows = v_ref.shape[0]
    times = rows // sx
    part = rows // pieces
    odd = odd_ref[0]
    sign = jnp.where(odd == 1, 0.5, -0.5)
    plain[...] = sign * v_ref[...].astype(F32)
    near, far = near_ref[...].astype(F32), far_ref[...].astype(F32)
    side = side_ref[0] == 1
    cols = jnp.concatenate([jnp.where(side, near, far), jnp.where(side, far, near)], axis=0).astype(BF16)
    for m in range(pieces):
        inner = jnp.dot(u_ref[m * part : (m + 1) * part, :], shift_ref[...], preferred_element_type=F32)
        outer = lax.dot_general(cols, places_ref[m], (((0,), (0,)), ((), ())), preferred_element_type=F32)
        slope[m * part : (m + 1) * part, :] = inner + outer
    for position in range(sx):
        z = slope[pl.ds(row_at(position, sx, odd), times, stride=sx), :]
        if position + 1 < sx:
            z += plain[pl.ds(row_at(position + 1, sx, odd), times, stride=sx), :]
        if position > 0:
            z -= plain[pl.ds(row_at(position - 1, sx, odd), times, stride=sx), :]
        z_ref[position] = z
        sum_ref[position] = jnp.sum(z.reshape(times // 8, 8, LANES), axis=0)


def local_part(odd, side, v, u, shift, near, far, places, sx):
    rows = v.shape[0]
    pieces = places.shape[0]
    times = rows // sx
    return pl.pallas_call(
        functools.partial(local_kernel, sx, pieces),
        out_shape=(
            jax.ShapeDtypeStruct((sx, times, LANES), F32),
            jax.ShapeDtypeStruct((sx, 8, LANES), F32),
        ),
        in_specs=[SMEM] * 2 + [VMEM] * 6,
        out_specs=(VMEM,) * 2,
        scratch_shapes=[pltpu.VMEM((rows, LANES), F32), pltpu.VMEM((rows, LANES), F32)],
        compiler_params=limit(20),
        cost_estimate=pl.CostEstimate(flops=1000000000, bytes_accessed=8000000, transcendentals=0),
        name="local",
    )(odd, side, v, u, shift, near, far, places)


def cross_kernel(
    sx, begin, pieces, odd_ref, core_ref, offsets_ref, triads_ref, z_ref, sum_ref, weights_ref, window_ref, transform_ref,
    *rest,
):
    far = begin > 0
    halo_refs, rest = rest[:pieces], rest[pieces:]
    if far:
        before_ref, *rest = rest
    *cross_refs, target_ref, full, spec, prod, packed = rest
    count, times, _ = full.shape
    blocks = offsets_ref.shape[0]
    ntri = triads_ref.shape[1]
    half = NFFT // 2
    groups = LANES // blocks
    per = ntri // groups
    wide = 2 * blocks
    pitch = blocks + 1
    odd = odd_ref[0]
    sign = jnp.where(odd == 1, 0.5, -0.5)
    if not far:
        sign = -sign
    touched = count - 1 if far else 0

    halo_sum = jnp.zeros((8, LANES), F32)
    base = 0
    for halo_ref in halo_refs:
        length = halo_ref.shape[0]
        steps = max(n for n in range(1, 9) if length % (16 * n) == 0)
        chunk = length // steps

        def add_halo(step, carry):
            at = pl.ds(pl.multiple_of(step * chunk, 8), chunk)
            to = pl.ds(pl.multiple_of(base + step * chunk, 8), chunk)
            halo = sign * halo_ref[at, :].astype(F32)
            for row in range(count):
                z = z_ref[begin + row, to, :]
                full[row, to, :] = z + halo if row == touched else z
            return carry + jnp.sum(halo.reshape(chunk // 8, 8, LANES), axis=0)

        halo_sum = lax.fori_loop(0, steps, add_halo, halo_sum)
        base += halo_ref.shape[0]
    means = []
    for row in range(count):
        total = sum_ref[begin + row]
        if row == touched:
            total = total + halo_sum
        means.append(jnp.sum(total, axis=0, keepdims=True) * (1.0 / times))

    def two_blocks(h, carry):
        window = window_ref[...]
        pair = (2 * h, 2 * h + 1)
        for row in range(count):
            windowed = [
                ((full[row, pl.ds(offsets_ref[b], NFFT), :] - means[row]) * window).astype(BF16) for b in pair
            ]
            out = jnp.dot(transform_ref[...], jnp.concatenate(windowed, axis=1), preferred_element_type=F32)
            for n, b in enumerate(pair):
                spec[row, pl.ds(b, NFFT, stride=pitch), :] = out[:, n * LANES : (n + 1) * LANES]
        return carry

    lax.fori_loop(0, blocks // 2, two_blocks, 0, unroll=True)
    weights = [weights_ref[pl.ds(row_at(begin + row, sx, odd), 1), :] for row in range(count)]

    def one_triad(j, carry):
        k = triads_ref[0, j]
        l = triads_ref[1, j]

        def take(f, row):
            re = spec[row, pl.ds(f * pitch, blocks), :]
            im = spec[row, pl.ds((f + half) * pitch, blocks), :]
            return re, im

        base = pl.multiple_of(j * wide, 8)
        for row in range(count):
            lanes = slice(row * LANES, (row + 1) * LANES)
            first_re, first_im = take(k, row)
            second_re, second_im = take(l, row)
            target_re, target_im = take(k + l, row)
            weight = weights[row]
            prod[pl.ds(base, wide), lanes] = jnp.concatenate(
                [
                    (first_re * second_re - first_im * second_im) * weight,
                    (first_re * second_im + first_im * second_re) * weight,
                ],
                axis=0,
            ).astype(BF16)
            target_ref[pl.ds(base, wide), lanes] = jnp.concatenate([target_re, target_im], axis=0).astype(BF16)
        return carry

    lax.fori_loop(0, ntri, one_triad, 0, unroll=4)

    tall = per * wide
    lane = lax.broadcasted_iota(jnp.int32, (wide, tall), 1)
    owner = lane // wide
    is_re = (lax.broadcasted_iota(jnp.int32, (blocks, tall), 1) % wide) < blocks

    def one_group(g, carry):
        at = pl.ds(pl.multiple_of(g * tall, 8), tall)
        every = lax.dot_general(
            prod[at, :], target_ref[at, :], (((1,), (1,)), ((), ())), preferred_element_type=F32
        )
        kept = every[0:wide]
        for i in range(1, per):
            kept = jnp.where(owner == i, every[i * wide : (i + 1) * wide], kept)
        by_re = kept[0:blocks]
        by_im = kept[blocks:wide]
        ahead = pltpu.roll(by_im, tall - blocks, 1)
        behind = pltpu.roll(by_im, blocks, 1)
        packed[pl.ds(pl.multiple_of(g * blocks, 8), blocks), :] = by_re + jnp.where(is_re, ahead, -behind)
        return carry

    lax.fori_loop(0, groups, one_group, 0, unroll=True)
    share = packed[...].T
    if not far:
        cross_refs[0][...] = share
        return
    share = share + before_ref[...]
    lower, upper = share[: tall // 2], share[tall // 2 :]
    second = core_ref[0] == 1
    cross_refs[0][...] = jnp.where(second, upper, lower)
    cross_refs[1][...] = jnp.where(second, lower, upper)


def cross_part(begin, count, odd, core, offsets, triads, z, sums, halos, weights, window, transform, before=None):
    sx, times, _ = z.shape
    blocks = offsets.shape[0]
    ntri = triads.shape[1]
    groups = LANES // blocks
    wide = 2 * blocks
    tall = ntri // groups * wide
    more = list(halos) + ([] if before is None else [before])
    parts = 1 if before is None else 2
    return pl.pallas_call(
        functools.partial(cross_kernel, sx, begin, len(halos)),
        out_shape=(jax.ShapeDtypeStruct((tall // parts, LANES), F32),) * parts
        + (jax.ShapeDtypeStruct((ntri * wide, count * LANES), BF16),),
        in_specs=[SMEM] * 4 + [VMEM] * (5 + len(more)),
        out_specs=(VMEM,) * (parts + 1),
        scratch_shapes=[
            pltpu.VMEM((count, times, LANES), F32),
            pltpu.VMEM((count, NFFT * (blocks + 1), LANES), F32),
            pltpu.VMEM((ntri * wide, count * LANES), BF16),
            pltpu.VMEM((LANES, tall), F32),
        ],
        compiler_params=limit(26),
        cost_estimate=pl.CostEstimate(flops=2000000000, bytes_accessed=4000000, transcendentals=0),
        name="cross_far" if begin else "cross_near",
    )(odd, core, offsets, triads, z, sums, weights, window, transform, *more)


def swap(x, axis, bit):
    count = lax.axis_size(axis)
    return lax.ppermute(x, axis, [(i, i ^ bit) for i in range(count)])


def sum_over_rest(x):
    slabs, parts = lax.axis_size("space"), lax.axis_size("freq")
    hops = [bit * parts for bit in bits_of(slabs)]
    across = [bit for bit in bits_of(parts)[1:]]
    first = hops[:1] + across + hops[1:]
    second = across + hops[:1] + hops[:0:-1]
    for one, other in zip(first, second, strict=True):
        pairs = [(i, i ^ (other if i % 2 else one)) for i in range(slabs * parts)]
        x = x + lax.ppermute(x, ("space", "freq"), pairs)
    return x


def bits_of(count):
    return [1 << n for n in range(count.bit_length() - 1)]


def modes_kernel(sx, blocks, scaling, odd_ref, core_ref, mine_ref, other_ref, near_ref, far_ref, values_ref, modes_ref, cross):
    tall = cross.shape[0]
    wide = 2 * blocks
    per = tall // wide
    groups = LANES // blocks
    odd = odd_ref[0]
    core = core_ref[0]
    half = tall // 2
    cross[pl.ds(pl.multiple_of(core * half, 8), half), :] = mine_ref[...] * scaling
    cross[pl.ds(pl.multiple_of((1 - core) * half, 8), half), :] = other_ref[...] * scaling
    lane = lax.broadcasted_iota(jnp.int32, (per, LANES), 1)
    start = lane - lane % blocks

    mat_re = [cross[pl.ds(c, per, stride=wide), :] for c in range(blocks)]
    mat_im = [cross[pl.ds(blocks + c, per, stride=wide), :] for c in range(blocks)]

    def pick(x, index):
        return jnp.take_along_axis(x, index, axis=1)

    spots = [start + c for c in range(blocks)]

    def tree(terms):
        while len(terms) > 1:
            terms = [sum(terms[n : n + 2]) for n in range(0, len(terms), 2)]
        return terms[0]

    def apply(part_re, part_im):
        re = [pick(part_re, spot) for spot in spots]
        im = [pick(part_im, spot) for spot in spots]
        every = range(blocks)
        out_re = tree([mat_re[c] * re[c] - mat_im[c] * im[c] for c in every])
        out_im = tree([mat_re[c] * im[c] + mat_im[c] * re[c] for c in every])
        return out_re, out_im

    def over_blocks(x):
        bit = 1
        while bit < blocks:
            if 4 * bit <= blocks:
                x = (x + pick(x, lane ^ bit)) + (pick(x, lane ^ (2 * bit)) + pick(x, lane ^ (3 * bit)))
                bit *= 4
            else:
                x = x + pick(x, lane ^ bit)
                bit *= 2
        return x

    vec_re = jnp.full((per, LANES), 1.0 / math.sqrt(blocks), F32)
    vec_im = jnp.zeros((per, LANES), F32)
    out_re, out_im = apply(vec_re, vec_im)
    for _ in range(POW):
        length = jnp.sqrt(over_blocks(out_re * out_re + out_im * out_im))
        vec_re = out_re / length
        vec_im = out_im / length
        out_re, out_im = apply(out_re, out_im)
        out_re = out_re / length
        out_im = out_im / length
    value_re = over_blocks(vec_re * out_re + vec_im * out_im)
    value_im = over_blocks(vec_re * out_im - vec_im * out_re)

    source = jnp.minimum(lane // per * blocks, LANES - 1)
    mine = lax.broadcasted_iota(jnp.int32, (per, LANES), 0) == lane % per
    for part, value in enumerate((value_re, value_im)):
        row = jnp.sum(jnp.where(mine, pick(value, source), 0.0), axis=0, keepdims=True)
        values_ref[part : part + 1, :] = row[:, : values_ref.shape[1]]

    own = lax.broadcasted_iota(jnp.int32, (per, tall), 1) // wide == lax.broadcasted_iota(jnp.int32, (per, tall), 0)
    is_re = lax.broadcasted_iota(jnp.int32, (per, tall), 1) % wide < blocks
    for g in range(groups):
        spot = g * blocks + lane % blocks
        re = jnp.concatenate([pick(vec_re, spot)] * (tall // LANES), axis=1)
        im = jnp.concatenate([pick(vec_im, spot)] * (tall // LANES), axis=1)
        rows = jnp.concatenate(
            [
                jnp.where(own, jnp.where(is_re, re, -im), 0.0),
                jnp.where(own, jnp.where(is_re, im, re), 0.0),
            ],
            axis=0,
        )
        high = rows.astype(BF16)
        both = jnp.concatenate([high, (rows - high.astype(F32)).astype(BF16)], axis=0)
        at = slice(g * tall, (g + 1) * tall)
        for position in range(sx):
            if position + 1 < sx:
                target = near_ref[at, position * LANES : (position + 1) * LANES]
            else:
                target = far_ref[at, :]
            out = jnp.dot(both, target, preferred_element_type=F32)
            out = out[: 2 * per] + out[2 * per :]
            row = row_at(position, sx, odd)
            for part in range(2):
                first = g * per * 2 * sx + part * sx
                modes_ref[pl.ds(first + row, per, stride=2 * sx), :] = out[part * per : (part + 1) * per]


def modes_part(odd, core, mine, other, near, far, blocks, ntri, sx, scaling):
    return pl.pallas_call(
        functools.partial(modes_kernel, sx, blocks, scaling),
        out_shape=(
            jax.ShapeDtypeStruct((2, ntri), F32),
            jax.ShapeDtypeStruct((ntri * 2 * sx, LANES), F32),
        ),
        in_specs=[SMEM] * 2 + [VMEM] * 4,
        out_specs=(VMEM,) * 2,
        scratch_shapes=[pltpu.VMEM((2 * mine.shape[0], LANES), F32)],
        compiler_params=limit(12),
        name="modes",
    )(odd, core, mine, other, near, far)


def between_pairs(count):
    inner = [(i, i + 1) for i in range(1, count - 1, 2)]
    return inner + [(b, a) for a, b in inner]


def on_device(u_velocity, v_velocity, cell_weights, block_offsets, triads):
    times, sx, columns = u_velocity.shape
    blocks = block_offsets.shape[0]
    ntri = triads.shape[0]
    slabs = lax.axis_size("space")
    cells = sx * columns * slabs * lax.axis_size("freq")
    scaling = 1.0 / (blocks * math.sqrt(cells))
    pieces = 8
    window, transform = make_table(NFFT)
    picks, places = edge_columns(pieces)
    shift = 0.5 * (np.eye(LANES, k=1, dtype=np.float32) - np.eye(LANES, k=-1, dtype=np.float32))
    v = v_velocity.reshape(times * sx, columns)
    u = u_velocity.reshape(times * sx, columns)
    odd = is_odd()[None]
    core = (lax.axis_index("freq") % 2)[None]
    pairs = triads.T

    early, late = near_edge(odd, v, sx)
    early = swap(early, "space", 1)
    late = swap(late, "space", 1)
    col_near, col_far = columns_edge(core, u, jnp.asarray(picks, BF16))
    col_near = swap(col_near, "freq", 1)
    col_far = lax.ppermute(col_far, "freq", between_pairs(lax.axis_size("freq")))
    z, sums = local_part(odd, core, v, u, jnp.asarray(shift, BF16), col_near, col_far, jnp.asarray(places, BF16), sx)
    far = far_edge(odd, v, sx)
    far = lax.ppermute(far, "space", between_pairs(slabs))
    window = jnp.asarray(np.ascontiguousarray(np.broadcast_to(window[:, None], (NFFT, LANES))))
    transform = jnp.asarray(transform, BF16)
    share, near_target = cross_part(
        0, sx - 1, odd, core, block_offsets, pairs, z, sums, [early, late], cell_weights, window, transform
    )
    mine, other, far_target = cross_part(
        sx - 1, 1, odd, core, block_offsets, pairs, z, sums, [far], cell_weights, window, transform, share
    )
    mine = mine + swap(other, "freq", 1)
    mine = sum_over_rest(mine)
    other = swap(mine, "freq", 1)
    values, modes = modes_part(odd, core, mine, other, near_target, far_target, blocks, ntri, sx, scaling)
    return (values.T, modes.reshape(ntri, 2, sx, columns))


def solution(mesh):
    return jax.shard_map(
        on_device,
        mesh=mesh,
        in_specs=(P(None, "space", "freq"), P(None, "space", "freq"), P("space", "freq"), P(), P()),
        out_specs=(P(), P(None, None, "space", "freq")),
        check_vma=False,
    )
```

```python
import functools
import math

import jax
import jax.numpy as jnp
import numpy as np
from jax import lax
from jax.experimental import pallas as pl
from jax.experimental.pallas import tpu as pltpu
from jax.sharding import PartitionSpec as P


NFFT = 256
POW = 4
LANES = 128
AHEAD = 11
F32 = jnp.float32
BF16 = jnp.bfloat16
MIB = 2**20
VMEM = pl.BlockSpec(memory_space=pltpu.VMEM)
SMEM = pl.BlockSpec(memory_space=pltpu.SMEM)


def make_table(length):
    half_len = length // 2
    times_idx = np.arange(length)
    phases = np.arange(half_len)[:, None] * times_idx[None, :] % length
    angles = phases * (2.0 * math.pi / length)
    window = 0.5 - 0.5 * np.cos(times_idx * (2.0 * math.pi / length))
    scaling = 1.0 / np.sqrt(np.sum(window * window))
    transform = np.concatenate([np.cos(angles) * scaling, -np.sin(angles) * scaling], axis=0)
    return window.astype(np.float32), transform.astype(np.float32)


def edge_columns(pieces):
    picks = np.zeros((pieces, 2 * pieces, LANES), np.float32)
    places = np.zeros((pieces, 2 * pieces, LANES), np.float32)
    for m in range(pieces):
        picks[m, m, 0] = 1.0
        picks[m, pieces + m, LANES - 1] = 1.0
        places[m, m, 0] = 0.5
        places[m, pieces + m, LANES - 1] = -0.5
    return picks, places


def is_odd():
    return lax.axis_index("space") % 2


def row_at(position, sx, odd):
    return jnp.where(odd == 1, position, sx - 1 - position)


def limit(mib):
    return pltpu.CompilerParams(vmem_limit_bytes=mib * MIB)


def near_kernel(sx, odd_ref, v_ref, early_ref, late_ref, plain):
    plain[...] = v_ref[...].astype(F32)
    row = row_at(0, sx, odd_ref[0])
    early, late = early_ref.shape[0], late_ref.shape[0]
    early_ref[...] = plain[pl.ds(row, early, stride=sx), :].astype(BF16)
    late_ref[...] = plain[pl.ds(early * sx + row, late, stride=sx), :].astype(BF16)


def near_edge(odd, v, sx):
    rows = v.shape[0]
    early = rows // sx * AHEAD // 1024 * 64
    return pl.pallas_call(
        functools.partial(near_kernel, sx),
        out_shape=(
            jax.ShapeDtypeStruct((early, LANES), BF16),
            jax.ShapeDtypeStruct((rows // sx - early, LANES), BF16),
        ),
        in_specs=[SMEM, VMEM],
        out_specs=(VMEM,) * 2,
        scratch_shapes=[pltpu.VMEM((rows, LANES), F32)],
        compiler_params=limit(8),
        name="near",
    )(odd, v)


def far_kernel(sx, odd_ref, v_ref, far_ref, plain):
    plain[...] = v_ref[...].astype(F32)
    far_ref[...] = plain[pl.ds(row_at(sx - 1, sx, odd_ref[0]), far_ref.shape[0], stride=sx), :].astype(BF16)


def far_edge(odd, v, sx):
    rows = v.shape[0]
    return pl.pallas_call(
        functools.partial(far_kernel, sx),
        out_shape=jax.ShapeDtypeStruct((rows // sx, LANES), BF16),
        in_specs=[SMEM, VMEM],
        out_specs=VMEM,
        scratch_shapes=[pltpu.VMEM((rows, LANES), F32)],
        compiler_params=limit(8),
        name="far",
    )(odd, v)


def columns_kernel(pieces, side_ref, u_ref, picks_ref, near_ref, far_ref):
    rows = u_ref.shape[0]
    part = rows // pieces
    cols = jnp.zeros((2 * pieces, part), F32)
    for m in range(pieces):
        cols += lax.dot_general(
            picks_ref[m], u_ref[m * part : (m + 1) * part, :], (((1,), (1,)), ((), ())), preferred_element_type=F32
        )
    low, high = cols[:pieces], cols[pieces:]
    odd = side_ref[0] == 1
    near_ref[...] = jnp.where(odd, low, high).astype(BF16)
    far_ref[...] = jnp.where(odd, high, low).astype(BF16)


def columns_edge(side, u, picks):
    rows = u.shape[0]
    pieces = picks.shape[0]
    return pl.pallas_call(
        functools.partial(columns_kernel, pieces),
        out_shape=(jax.ShapeDtypeStruct((pieces, rows // pieces), BF16),) * 2,
        in_specs=[SMEM] + [VMEM] * 2,
        out_specs=(VMEM,) * 2,
        compiler_params=limit(8),
        name="columns",
    )(side, u, picks)


def local_kernel(
    sx, pieces, odd_ref, side_ref, v_ref, u_ref, shift_ref, near_ref, far_ref, places_ref, z_ref, sum_ref, plain, slope
):
    rows = v_ref.shape[0]
    times = rows // sx
    part = rows // pieces
    odd = odd_ref[0]
    sign = jnp.where(odd == 1, 0.5, -0.5)
    plain[...] = sign * v_ref[...].astype(F32)
    near, far = near_ref[...].astype(F32), far_ref[...].astype(F32)
    side = side_ref[0] == 1
    cols = jnp.concatenate([jnp.where(side, near, far), jnp.where(side, far, near)], axis=0).astype(BF16)
    for m in range(pieces):
        inner = jnp.dot(u_ref[m * part : (m + 1) * part, :], shift_ref[...], preferred_element_type=F32)
        outer = lax.dot_general(cols, places_ref[m], (((0,), (0,)), ((), ())), preferred_element_type=F32)
        slope[m * part : (m + 1) * part, :] = inner + outer
    for position in range(sx):
        z = slope[pl.ds(row_at(position, sx, odd), times, stride=sx), :]
        if position + 1 < sx:
            z += plain[pl.ds(row_at(position + 1, sx, odd), times, stride=sx), :]
        if position > 0:
            z -= plain[pl.ds(row_at(position - 1, sx, odd), times, stride=sx), :]
        z_ref[position] = z
        sum_ref[position] = jnp.sum(z.reshape(times // 8, 8, LANES), axis=0)


def local_part(odd, side, v, u, shift, near, far, places, sx):
    rows = v.shape[0]
    pieces = places.shape[0]
    times = rows // sx
    return pl.pallas_call(
        functools.partial(local_kernel, sx, pieces),
        out_shape=(
            jax.ShapeDtypeStruct((sx, times, LANES), F32),
            jax.ShapeDtypeStruct((sx, 8, LANES), F32),
        ),
        in_specs=[SMEM] * 2 + [VMEM] * 6,
        out_specs=(VMEM,) * 2,
        scratch_shapes=[pltpu.VMEM((rows, LANES), F32), pltpu.VMEM((rows, LANES), F32)],
        compiler_params=limit(20),
        cost_estimate=pl.CostEstimate(flops=1000000000, bytes_accessed=8000000, transcendentals=0),
        name="local",
    )(odd, side, v, u, shift, near, far, places)


def cross_kernel(
    sx, begin, pieces, odd_ref, core_ref, offsets_ref, triads_ref, z_ref, sum_ref, weights_ref, window_ref, transform_ref,
    *rest,
):
    far = begin > 0
    halo_refs, rest = rest[:pieces], rest[pieces:]
    if far:
        before_ref, *rest = rest
    *cross_refs, target_ref, full, spec, prod, packed = rest
    count, times, _ = full.shape
    blocks = offsets_ref.shape[0]
    ntri = triads_ref.shape[1]
    half = NFFT // 2
    groups = LANES // blocks
    per = ntri // groups
    wide = 2 * blocks
    pitch = blocks + 1
    odd = odd_ref[0]
    sign = jnp.where(odd == 1, 0.5, -0.5)
    if not far:
        sign = -sign
    touched = count - 1 if far else 0

    halo_sum = jnp.zeros((8, LANES), F32)
    base = 0
    for halo_ref in halo_refs:
        length = halo_ref.shape[0]
        steps = max(n for n in range(1, 9) if length % (16 * n) == 0)
        chunk = length // steps

        def add_halo(step, carry):
            at = pl.ds(pl.multiple_of(step * chunk, 8), chunk)
            to = pl.ds(pl.multiple_of(base + step * chunk, 8), chunk)
            halo = sign * halo_ref[at, :].astype(F32)
            for row in range(count):
                z = z_ref[begin + row, to, :]
                full[row, to, :] = z + halo if row == touched else z
            return carry + jnp.sum(halo.reshape(chunk // 8, 8, LANES), axis=0)

        halo_sum = lax.fori_loop(0, steps, add_halo, halo_sum)
        base += halo_ref.shape[0]
    means = []
    for row in range(count):
        total = sum_ref[begin + row]
        if row == touched:
            total = total + halo_sum
        means.append(jnp.sum(total, axis=0, keepdims=True) * (1.0 / times))

    def two_blocks(h, carry):
        window = window_ref[...]
        pair = (2 * h, 2 * h + 1)
        for row in range(count):
            windowed = [
                ((full[row, pl.ds(offsets_ref[b], NFFT), :] - means[row]) * window).astype(BF16) for b in pair
            ]
            out = jnp.dot(transform_ref[...], jnp.concatenate(windowed, axis=1), preferred_element_type=F32)
            for n, b in enumerate(pair):
                spec[row, pl.ds(b, NFFT, stride=pitch), :] = out[:, n * LANES : (n + 1) * LANES]
        return carry

    lax.fori_loop(0, blocks // 2, two_blocks, 0, unroll=True)
    weights = [weights_ref[pl.ds(row_at(begin + row, sx, odd), 1), :] for row in range(count)]

    def one_triad(j):
        k = triads_ref[0, j]
        l = triads_ref[1, j]

        def take(f, row):
            re = spec[row, pl.ds(f * pitch, blocks), :]
            im = spec[row, pl.ds((f + half) * pitch, blocks), :]
            return re, im

        base = pl.multiple_of(j * wide, 8)
        for row in range(count):
            lanes = slice(row * LANES, (row + 1) * LANES)
            first_re, first_im = take(k, row)
            second_re, second_im = take(l, row)
            target_re, target_im = take(k + l, row)
            weight = weights[row]
            prod[pl.ds(base, wide), lanes] = jnp.concatenate(
                [
                    (first_re * second_re - first_im * second_im) * weight,
                    (first_re * second_im + first_im * second_re) * weight,
                ],
                axis=0,
            ).astype(BF16)
            target_ref[pl.ds(base, wide), lanes] = jnp.concatenate([target_re, target_im], axis=0).astype(BF16)

    tall = per * wide
    lane = lax.broadcasted_iota(jnp.int32, (wide, tall), 1)
    owner = lane // wide
    is_re = (lax.broadcasted_iota(jnp.int32, (blocks, tall), 1) % wide) < blocks

    def one_group(g, carry):
        for i in range(per):
            one_triad(g * per + i)
        at = pl.ds(pl.multiple_of(g * tall, 8), tall)
        every = lax.dot_general(
            prod[at, :], target_ref[at, :], (((1,), (1,)), ((), ())), preferred_element_type=F32
        )
        kept = every[0:wide]
        for i in range(1, per):
            kept = jnp.where(owner == i, every[i * wide : (i + 1) * wide], kept)
        by_re = kept[0:blocks]
        by_im = kept[blocks:wide]
        ahead = pltpu.roll(by_im, tall - blocks, 1)
        behind = pltpu.roll(by_im, blocks, 1)
        packed[pl.ds(pl.multiple_of(g * blocks, 8), blocks), :] = by_re + jnp.where(is_re, ahead, -behind)
        return carry

    lax.fori_loop(0, groups, one_group, 0, unroll=True)
    share = packed[...].T
    if not far:
        cross_refs[0][...] = share
        return
    share = share + before_ref[...]
    lower, upper = share[: tall // 2], share[tall // 2 :]
    second = core_ref[0] == 1
    cross_refs[0][...] = jnp.where(second, upper, lower)
    cross_refs[1][...] = jnp.where(second, lower, upper)


def cross_part(begin, count, odd, core, offsets, triads, z, sums, halos, weights, window, transform, before=None):
    sx, times, _ = z.shape
    blocks = offsets.shape[0]
    ntri = triads.shape[1]
    groups = LANES // blocks
    wide = 2 * blocks
    tall = ntri // groups * wide
    more = list(halos) + ([] if before is None else [before])
    parts = 1 if before is None else 2
    return pl.pallas_call(
        functools.partial(cross_kernel, sx, begin, len(halos)),
        out_shape=(jax.ShapeDtypeStruct((tall // parts, LANES), F32),) * parts
        + (jax.ShapeDtypeStruct((ntri * wide, count * LANES), BF16),),
        in_specs=[SMEM] * 4 + [VMEM] * (5 + len(more)),
        out_specs=(VMEM,) * (parts + 1),
        scratch_shapes=[
            pltpu.VMEM((count, times, LANES), F32),
            pltpu.VMEM((count, NFFT * (blocks + 1), LANES), F32),
            pltpu.VMEM((ntri * wide, count * LANES), BF16),
            pltpu.VMEM((LANES, tall), F32),
        ],
        compiler_params=limit(26),
        cost_estimate=pl.CostEstimate(flops=2000000000, bytes_accessed=4000000, transcendentals=0),
        name="cross_far" if begin else "cross_near",
    )(odd, core, offsets, triads, z, sums, weights, window, transform, *more)


def swap(x, axis, bit):
    count = lax.axis_size(axis)
    return lax.ppermute(x, axis, [(i, i ^ bit) for i in range(count)])


def sum_over_rest(x):
    slabs, parts = lax.axis_size("space"), lax.axis_size("freq")
    hops = [bit * parts for bit in bits_of(slabs)]
    across = [bit for bit in bits_of(parts)[1:]]
    first = hops[:1] + across + hops[1:]
    second = across + hops[:1] + hops[:0:-1]
    for one, other in zip(first, second, strict=True):
        pairs = [(i, i ^ (other if i % 2 else one)) for i in range(slabs * parts)]
        x = x + lax.ppermute(x, ("space", "freq"), pairs)
    return x


def bits_of(count):
    return [1 << n for n in range(count.bit_length() - 1)]


def modes_kernel(sx, blocks, scaling, odd_ref, core_ref, mine_ref, other_ref, near_ref, far_ref, values_ref, modes_ref, cross):
    tall = cross.shape[0]
    wide = 2 * blocks
    per = tall // wide
    groups = LANES // blocks
    odd = odd_ref[0]
    core = core_ref[0]
    half = tall // 2
    cross[pl.ds(pl.multiple_of(core * half, 8), half), :] = mine_ref[...] * scaling
    cross[pl.ds(pl.multiple_of((1 - core) * half, 8), half), :] = other_ref[...] * scaling
    lane = lax.broadcasted_iota(jnp.int32, (per, LANES), 1)
    start = lane - lane % blocks

    mat_re = [cross[pl.ds(c, per, stride=wide), :] for c in range(blocks)]
    mat_im = [cross[pl.ds(blocks + c, per, stride=wide), :] for c in range(blocks)]

    def pick(x, index):
        return jnp.take_along_axis(x, index, axis=1)

    spots = [start + c for c in range(blocks)]

    def tree(terms):
        while len(terms) > 1:
            terms = [sum(terms[n : n + 2]) for n in range(0, len(terms), 2)]
        return terms[0]

    def apply(part_re, part_im):
        re = [pick(part_re, spot) for spot in spots]
        im = [pick(part_im, spot) for spot in spots]
        every = range(blocks)
        out_re = tree([mat_re[c] * re[c] - mat_im[c] * im[c] for c in every])
        out_im = tree([mat_re[c] * im[c] + mat_im[c] * re[c] for c in every])
        return out_re, out_im

    def over_blocks(x):
        bit = 1
        while bit < blocks:
            if 4 * bit <= blocks:
                x = (x + pick(x, lane ^ bit)) + (pick(x, lane ^ (2 * bit)) + pick(x, lane ^ (3 * bit)))
                bit *= 4
            else:
                x = x + pick(x, lane ^ bit)
                bit *= 2
        return x

    vec_re = jnp.full((per, LANES), 1.0 / math.sqrt(blocks), F32)
    vec_im = jnp.zeros((per, LANES), F32)
    out_re, out_im = apply(vec_re, vec_im)
    for _ in range(POW):
        length = jnp.sqrt(over_blocks(out_re * out_re + out_im * out_im))
        vec_re = out_re / length
        vec_im = out_im / length
        out_re, out_im = apply(out_re, out_im)
        out_re = out_re / length
        out_im = out_im / length
    value_re = over_blocks(vec_re * out_re + vec_im * out_im)
    value_im = over_blocks(vec_re * out_im - vec_im * out_re)

    source = jnp.minimum(lane // per * blocks, LANES - 1)
    mine = lax.broadcasted_iota(jnp.int32, (per, LANES), 0) == lane % per
    for part, value in enumerate((value_re, value_im)):
        row = jnp.sum(jnp.where(mine, pick(value, source), 0.0), axis=0, keepdims=True)
        values_ref[part : part + 1, :] = row[:, : values_ref.shape[1]]

    own = lax.broadcasted_iota(jnp.int32, (per, tall), 1) // wide == lax.broadcasted_iota(jnp.int32, (per, tall), 0)
    is_re = lax.broadcasted_iota(jnp.int32, (per, tall), 1) % wide < blocks
    for g in range(groups):
        spot = g * blocks + lane % blocks
        re = jnp.concatenate([pick(vec_re, spot)] * (tall // LANES), axis=1)
        im = jnp.concatenate([pick(vec_im, spot)] * (tall // LANES), axis=1)
        rows = jnp.concatenate(
            [
                jnp.where(own, jnp.where(is_re, re, -im), 0.0),
                jnp.where(own, jnp.where(is_re, im, re), 0.0),
            ],
            axis=0,
        )
        high = rows.astype(BF16)
        both = jnp.concatenate([high, (rows - high.astype(F32)).astype(BF16)], axis=0)
        at = slice(g * tall, (g + 1) * tall)
        target = jnp.concatenate([near_ref[at, :], far_ref[at, :]], axis=1)
        out = jnp.dot(both, target, preferred_element_type=F32)
        out = out[: 2 * per] + out[2 * per :]
        for position in range(sx):
            lanes = slice(position * LANES, (position + 1) * LANES)
            row = row_at(position, sx, odd)
            for part in range(2):
                first = g * per * 2 * sx + part * sx
                modes_ref[pl.ds(first + row, per, stride=2 * sx), :] = out[part * per : (part + 1) * per, lanes]


def modes_part(odd, core, mine, other, near, far, blocks, ntri, sx, scaling):
    return pl.pallas_call(
        functools.partial(modes_kernel, sx, blocks, scaling),
        out_shape=(
            jax.ShapeDtypeStruct((2, ntri), F32),
            jax.ShapeDtypeStruct((ntri * 2 * sx, LANES), F32),
        ),
        in_specs=[SMEM] * 2 + [VMEM] * 4,
        out_specs=(VMEM,) * 2,
        scratch_shapes=[pltpu.VMEM((2 * mine.shape[0], LANES), F32)],
        compiler_params=limit(12),
        name="modes",
    )(odd, core, mine, other, near, far)


def between_pairs(count):
    inner = [(i, i + 1) for i in range(1, count - 1, 2)]
    return inner + [(b, a) for a, b in inner]


def on_device(u_velocity, v_velocity, cell_weights, block_offsets, triads):
    times, sx, columns = u_velocity.shape
    blocks = block_offsets.shape[0]
    ntri = triads.shape[0]
    slabs = lax.axis_size("space")
    cells = sx * columns * slabs * lax.axis_size("freq")
    scaling = 1.0 / (blocks * math.sqrt(cells))
    pieces = 8
    window, transform = make_table(NFFT)
    picks, places = edge_columns(pieces)
    shift = 0.5 * (np.eye(LANES, k=1, dtype=np.float32) - np.eye(LANES, k=-1, dtype=np.float32))
    v = v_velocity.reshape(times * sx, columns)
    u = u_velocity.reshape(times * sx, columns)
    odd = is_odd()[None]
    core = (lax.axis_index("freq") % 2)[None]
    pairs = triads.T

    early, late = near_edge(odd, v, sx)
    early = swap(early, "space", 1)
    late = swap(late, "space", 1)
    col_near, col_far = columns_edge(core, u, jnp.asarray(picks, BF16))
    col_near = swap(col_near, "freq", 1)
    col_far = lax.ppermute(col_far, "freq", between_pairs(lax.axis_size("freq")))
    z, sums = local_part(odd, core, v, u, jnp.asarray(shift, BF16), col_near, col_far, jnp.asarray(places, BF16), sx)
    far = far_edge(odd, v, sx)
    far = lax.ppermute(far, "space", between_pairs(slabs))
    window = jnp.asarray(np.ascontiguousarray(np.broadcast_to(window[:, None], (NFFT, LANES))))
    transform = jnp.asarray(transform, BF16)
    share, near_target = cross_part(
        0, sx - 1, odd, core, block_offsets, pairs, z, sums, [early, late], cell_weights, window, transform
    )
    mine, other, far_target = cross_part(
        sx - 1, 1, odd, core, block_offsets, pairs, z, sums, [far], cell_weights, window, transform, share
    )
    mine = mine + swap(other, "freq", 1)
    mine = sum_over_rest(mine)
    other = swap(mine, "freq", 1)
    values, modes = modes_part(odd, core, mine, other, near_target, far_target, blocks, ntri, sx, scaling)
    return (values.T, modes.reshape(ntri, 2, sx, columns))


def solution(mesh):
    return jax.shard_map(
        on_device,
        mesh=mesh,
        in_specs=(P(None, "space", "freq"), P(None, "space", "freq"), P("space", "freq"), P(), P()),
        out_specs=(P(), P(None, None, "space", "freq")),
        check_vma=False,
    )
```

```python
import functools
import math

import jax
import jax.numpy as jnp
import numpy as np
from jax import lax
from jax.experimental import pallas as pl
from jax.experimental.pallas import tpu as pltpu
from jax.sharding import PartitionSpec as P


NFFT = 256
POW = 4
LANES = 128
PIECES = 4
F32 = jnp.float32
BF16 = jnp.bfloat16
MIB = 2**20
VMEM = pl.BlockSpec(memory_space=pltpu.VMEM)
SMEM = pl.BlockSpec(memory_space=pltpu.SMEM)


def make_table(length):
    half_len = length // 2
    times_idx = np.arange(length)
    phases = np.arange(half_len)[:, None] * times_idx[None, :] % length
    angles = phases * (2.0 * math.pi / length)
    window = 0.5 - 0.5 * np.cos(times_idx * (2.0 * math.pi / length))
    scaling = 1.0 / np.sqrt(np.sum(window * window))
    transform = np.concatenate([np.cos(angles) * scaling, -np.sin(angles) * scaling], axis=0)
    return window.astype(np.float32), transform.astype(np.float32)


def edge_columns(pieces):
    picks = np.zeros((pieces, 2 * pieces, LANES), np.float32)
    places = np.zeros((pieces, 2 * pieces, LANES), np.float32)
    for m in range(pieces):
        picks[m, m, 0] = 1.0
        picks[m, pieces + m, LANES - 1] = 1.0
        places[m, m, 0] = 0.5
        places[m, pieces + m, LANES - 1] = -0.5
    return picks, places


def is_odd():
    return lax.axis_index("space") % 2


def row_at(position, sx, odd):
    return jnp.where(odd == 1, position, sx - 1 - position)


def limit(mib):
    return pltpu.CompilerParams(vmem_limit_bytes=mib * MIB)


def near_kernel(sx, odd_ref, v_ref, near_ref, plain):
    plain[...] = v_ref[...].astype(F32)
    near_ref[...] = plain[pl.ds(row_at(0, sx, odd_ref[0]), near_ref.shape[0], stride=sx), :].astype(BF16)


def near_edge(odd, v, sx):
    rows = v.shape[0]
    return pl.pallas_call(
        functools.partial(near_kernel, sx),
        out_shape=jax.ShapeDtypeStruct((rows // sx, LANES), BF16),
        in_specs=[SMEM, VMEM],
        out_specs=VMEM,
        scratch_shapes=[pltpu.VMEM((rows, LANES), F32)],
        compiler_params=limit(8),
        name="near",
    )(odd, v)


def far_kernel(sx, odd_ref, v_ref, moved_ref, direct_ref, plain):
    plain[...] = v_ref[...].astype(F32)
    row = row_at(sx - 1, sx, odd_ref[0])
    moved, direct = moved_ref.shape[0], direct_ref.shape[0]
    moved_ref[...] = plain[pl.ds(row, moved, stride=sx), :].astype(BF16)
    direct_ref[...] = plain[pl.ds(moved * sx + row, direct, stride=sx), :].astype(BF16)


def far_edge(odd, v, sx):
    rows = v.shape[0]
    piece = rows // sx // PIECES
    return pl.pallas_call(
        functools.partial(far_kernel, sx),
        out_shape=(
            jax.ShapeDtypeStruct((piece * (PIECES - 1), LANES), BF16),
            jax.ShapeDtypeStruct((piece, LANES), BF16),
        ),
        in_specs=[SMEM, VMEM],
        out_specs=(VMEM,) * 2,
        scratch_shapes=[pltpu.VMEM((rows, LANES), F32)],
        compiler_params=limit(8),
        name="far",
    )(odd, v)


def choose_kernel(starts, place_ref, own_ref, passed_ref, *out_refs):
    for k, out_ref in enumerate(out_refs):
        piece = out_ref.shape[0]
        at = slice(k * piece, (k + 1) * piece)
        relays = place_ref[0] > starts[k]

        @pl.when(relays)
        def _():
            out_ref[...] = passed_ref[at, :]

        @pl.when(jnp.logical_not(relays))
        def _():
            out_ref[...] = own_ref[at, :]


def choose(place, own, passed, starts):
    count = len(starts)
    piece = own.shape[0] // count
    return pl.pallas_call(
        functools.partial(choose_kernel, starts),
        out_shape=(jax.ShapeDtypeStruct((piece, LANES), BF16),) * count,
        in_specs=[SMEM] + [VMEM] * 2,
        out_specs=(VMEM,) * count,
        compiler_params=limit(8),
        name="choose",
    )(place, own, passed)


def columns_kernel(pieces, side_ref, u_ref, picks_ref, near_ref, far_ref):
    rows = u_ref.shape[0]
    part = rows // pieces
    cols = jnp.zeros((2 * pieces, part), F32)
    for m in range(pieces):
        cols += lax.dot_general(
            picks_ref[m], u_ref[m * part : (m + 1) * part, :], (((1,), (1,)), ((), ())), preferred_element_type=F32
        )
    low, high = cols[:pieces], cols[pieces:]
    odd = side_ref[0] == 1
    near_ref[...] = jnp.where(odd, low, high).astype(BF16)
    far_ref[...] = jnp.where(odd, high, low).astype(BF16)


def columns_edge(side, u, picks):
    rows = u.shape[0]
    pieces = picks.shape[0]
    return pl.pallas_call(
        functools.partial(columns_kernel, pieces),
        out_shape=(jax.ShapeDtypeStruct((pieces, rows // pieces), BF16),) * 2,
        in_specs=[SMEM] + [VMEM] * 2,
        out_specs=(VMEM,) * 2,
        compiler_params=limit(8),
        name="columns",
    )(side, u, picks)


def local_kernel(
    sx, pieces, odd_ref, side_ref, v_ref, u_ref, shift_ref, near_ref, far_ref, places_ref, z_ref, sum_ref, plain, slope
):
    rows = v_ref.shape[0]
    times = rows // sx
    part = rows // pieces
    odd = odd_ref[0]
    sign = jnp.where(odd == 1, 0.5, -0.5)
    plain[...] = sign * v_ref[...].astype(F32)
    near, far = near_ref[...].astype(F32), far_ref[...].astype(F32)
    side = side_ref[0] == 1
    cols = jnp.concatenate([jnp.where(side, near, far), jnp.where(side, far, near)], axis=0).astype(BF16)
    for m in range(pieces):
        inner = jnp.dot(u_ref[m * part : (m + 1) * part, :], shift_ref[...], preferred_element_type=F32)
        outer = lax.dot_general(cols, places_ref[m], (((0,), (0,)), ((), ())), preferred_element_type=F32)
        slope[m * part : (m + 1) * part, :] = inner + outer
    for position in range(sx):
        z = slope[pl.ds(row_at(position, sx, odd), times, stride=sx), :]
        if position + 1 < sx:
            z += plain[pl.ds(row_at(position + 1, sx, odd), times, stride=sx), :]
        if position > 0:
            z -= plain[pl.ds(row_at(position - 1, sx, odd), times, stride=sx), :]
        z_ref[position] = z
        sum_ref[position] = jnp.sum(z.reshape(times // 8, 8, LANES), axis=0)


def local_part(odd, side, v, u, shift, near, far, places, sx):
    rows = v.shape[0]
    pieces = places.shape[0]
    times = rows // sx
    return pl.pallas_call(
        functools.partial(local_kernel, sx, pieces),
        out_shape=(
            jax.ShapeDtypeStruct((sx, times, LANES), F32),
            jax.ShapeDtypeStruct((sx, 8, LANES), F32),
        ),
        in_specs=[SMEM] * 2 + [VMEM] * 6,
        out_specs=(VMEM,) * 2,
        scratch_shapes=[pltpu.VMEM((rows, LANES), F32), pltpu.VMEM((rows, LANES), F32)],
        compiler_params=limit(20),
        cost_estimate=pl.CostEstimate(flops=1000000000, bytes_accessed=8000000, transcendentals=0),
        name="local",
    )(odd, side, v, u, shift, near, far, places)


def cross_kernel(
    sx, begin, pieces, odd_ref, core_ref, offsets_ref, triads_ref, z_ref, sum_ref, weights_ref, window_ref, transform_ref,
    *rest,
):
    far = begin > 0
    halo_refs, rest = rest[:pieces], rest[pieces:]
    if far:
        before_ref, *rest = rest
    *cross_refs, target_ref, full, spec, prod, packed = rest
    count, times, _ = full.shape
    blocks = offsets_ref.shape[0]
    ntri = triads_ref.shape[1]
    half = NFFT // 2
    groups = LANES // blocks
    per = ntri // groups
    wide = 2 * blocks
    pitch = blocks + 1
    odd = odd_ref[0]
    sign = jnp.where(odd == 1, 0.5, -0.5)
    if not far:
        sign = -sign
    touched = count - 1 if far else 0

    halo_sum = jnp.zeros((8, LANES), F32)
    base = 0
    for halo_ref in halo_refs:
        length = halo_ref.shape[0]
        steps = max(n for n in range(1, 9) if length % (16 * n) == 0)
        chunk = length // steps

        def add_halo(step, carry):
            at = pl.ds(pl.multiple_of(step * chunk, 8), chunk)
            to = pl.ds(pl.multiple_of(base + step * chunk, 8), chunk)
            halo = sign * halo_ref[at, :].astype(F32)
            for row in range(count):
                z = z_ref[begin + row, to, :]
                full[row, to, :] = z + halo if row == touched else z
            return carry + jnp.sum(halo.reshape(chunk // 8, 8, LANES), axis=0)

        halo_sum = lax.fori_loop(0, steps, add_halo, halo_sum)
        base += halo_ref.shape[0]
    means = []
    for row in range(count):
        total = sum_ref[begin + row]
        if row == touched:
            total = total + halo_sum
        means.append(jnp.sum(total, axis=0, keepdims=True) * (1.0 / times))

    def two_blocks(h, carry):
        window = window_ref[...]
        pair = (2 * h, 2 * h + 1)
        for row in range(count):
            windowed = [
                ((full[row, pl.ds(offsets_ref[b], NFFT), :] - means[row]) * window).astype(BF16) for b in pair
            ]
            out = jnp.dot(transform_ref[...], jnp.concatenate(windowed, axis=1), preferred_element_type=F32)
            for n, b in enumerate(pair):
                spec[row, pl.ds(b, NFFT, stride=pitch), :] = out[:, n * LANES : (n + 1) * LANES]
        return carry

    lax.fori_loop(0, blocks // 2, two_blocks, 0, unroll=True)
    weights = [weights_ref[pl.ds(row_at(begin + row, sx, odd), 1), :] for row in range(count)]

    def one_triad(j):
        k = triads_ref[0, j]
        l = triads_ref[1, j]

        def take(f, row):
            re = spec[row, pl.ds(f * pitch, blocks), :]
            im = spec[row, pl.ds((f + half) * pitch, blocks), :]
            return re, im

        base = pl.multiple_of(j * wide, 8)
        for row in range(count):
            lanes = slice(row * LANES, (row + 1) * LANES)
            first_re, first_im = take(k, row)
            second_re, second_im = take(l, row)
            target_re, target_im = take(k + l, row)
            weight = weights[row]
            prod[pl.ds(base, wide), lanes] = jnp.concatenate(
                [
                    (first_re * second_re - first_im * second_im) * weight,
                    (first_re * second_im + first_im * second_re) * weight,
                ],
                axis=0,
            ).astype(BF16)
            target_ref[pl.ds(base, wide), lanes] = jnp.concatenate([target_re, target_im], axis=0).astype(BF16)

    tall = per * wide
    lane = lax.broadcasted_iota(jnp.int32, (wide, tall), 1)
    owner = lane // wide
    is_re = (lax.broadcasted_iota(jnp.int32, (blocks, tall), 1) % wide) < blocks

    def one_group(g, carry):
        for i in range(per):
            one_triad(g * per + i)
        at = pl.ds(pl.multiple_of(g * tall, 8), tall)
        every = lax.dot_general(
            prod[at, :], target_ref[at, :], (((1,), (1,)), ((), ())), preferred_element_type=F32
        )
        kept = every[0:wide]
        for i in range(1, per):
            kept = jnp.where(owner == i, every[i * wide : (i + 1) * wide], kept)
        by_re = kept[0:blocks]
        by_im = kept[blocks:wide]
        ahead = pltpu.roll(by_im, tall - blocks, 1)
        behind = pltpu.roll(by_im, blocks, 1)
        packed[pl.ds(pl.multiple_of(g * blocks, 8), blocks), :] = by_re + jnp.where(is_re, ahead, -behind)
        return carry

    lax.fori_loop(0, groups, one_group, 0, unroll=True)
    share = packed[...].T
    if not far:
        cross_refs[0][...] = share
        return
    share = share + before_ref[...]
    lower, upper = share[: tall // 2], share[tall // 2 :]
    second = core_ref[0] == 1
    cross_refs[0][...] = jnp.where(second, upper, lower)
    cross_refs[1][...] = jnp.where(second, lower, upper)


def cross_part(begin, count, odd, core, offsets, triads, z, sums, halos, weights, window, transform, before=None):
    sx, times, _ = z.shape
    blocks = offsets.shape[0]
    ntri = triads.shape[1]
    groups = LANES // blocks
    wide = 2 * blocks
    tall = ntri // groups * wide
    more = list(halos) + ([] if before is None else [before])
    parts = 1 if before is None else 2
    return pl.pallas_call(
        functools.partial(cross_kernel, sx, begin, len(halos)),
        out_shape=(jax.ShapeDtypeStruct((tall // parts, LANES), F32),) * parts
        + (jax.ShapeDtypeStruct((ntri * wide, count * LANES), BF16),),
        in_specs=[SMEM] * 4 + [VMEM] * (5 + len(more)),
        out_specs=(VMEM,) * (parts + 1),
        scratch_shapes=[
            pltpu.VMEM((count, times, LANES), F32),
            pltpu.VMEM((count, NFFT * (blocks + 1), LANES), F32),
            pltpu.VMEM((ntri * wide, count * LANES), BF16),
            pltpu.VMEM((LANES, tall), F32),
        ],
        compiler_params=limit(26),
        cost_estimate=pl.CostEstimate(flops=2000000000, bytes_accessed=4000000, transcendentals=0),
        name="cross_far" if begin else "cross_near",
    )(odd, core, offsets, triads, z, sums, weights, window, transform, *more)


def swap(x, axis, bit):
    count = lax.axis_size(axis)
    return lax.ppermute(x, axis, [(i, i ^ bit) for i in range(count)])


def sum_over_rest(x):
    slabs, parts = lax.axis_size("space"), lax.axis_size("freq")
    hops = [bit * parts for bit in bits_of(slabs)]
    across = [bit for bit in bits_of(parts)[1:]]
    first = hops[:1] + across + hops[1:]
    second = across + hops[:1] + hops[:0:-1]
    for one, other in zip(first, second, strict=True):
        pairs = [(i, i ^ (other if i % 2 else one)) for i in range(slabs * parts)]
        x = x + lax.ppermute(x, ("space", "freq"), pairs)
    return x


def bits_of(count):
    return [1 << n for n in range(count.bit_length() - 1)]


def modes_kernel(sx, blocks, scaling, odd_ref, core_ref, mine_ref, other_ref, near_ref, far_ref, values_ref, modes_ref, cross):
    tall = cross.shape[0]
    wide = 2 * blocks
    per = tall // wide
    groups = LANES // blocks
    odd = odd_ref[0]
    core = core_ref[0]
    half = tall // 2
    cross[pl.ds(pl.multiple_of(core * half, 8), half), :] = mine_ref[...] * scaling
    cross[pl.ds(pl.multiple_of((1 - core) * half, 8), half), :] = other_ref[...] * scaling
    lane = lax.broadcasted_iota(jnp.int32, (per, LANES), 1)
    start = lane - lane % blocks

    mat_re = [cross[pl.ds(c, per, stride=wide), :] for c in range(blocks)]
    mat_im = [cross[pl.ds(blocks + c, per, stride=wide), :] for c in range(blocks)]

    def pick(x, index):
        return jnp.take_along_axis(x, index, axis=1)

    spots = [start + c for c in range(blocks)]

    def tree(terms):
        while len(terms) > 1:
            terms = [sum(terms[n : n + 2]) for n in range(0, len(terms), 2)]
        return terms[0]

    def apply(part_re, part_im):
        re = [pick(part_re, spot) for spot in spots]
        im = [pick(part_im, spot) for spot in spots]
        every = range(blocks)
        out_re = tree([mat_re[c] * re[c] - mat_im[c] * im[c] for c in every])
        out_im = tree([mat_re[c] * im[c] + mat_im[c] * re[c] for c in every])
        return out_re, out_im

    def over_blocks(x):
        bit = 1
        while bit < blocks:
            if 4 * bit <= blocks:
                x = (x + pick(x, lane ^ bit)) + (pick(x, lane ^ (2 * bit)) + pick(x, lane ^ (3 * bit)))
                bit *= 4
            else:
                x = x + pick(x, lane ^ bit)
                bit *= 2
        return x

    vec_re = jnp.full((per, LANES), 1.0 / math.sqrt(blocks), F32)
    vec_im = jnp.zeros((per, LANES), F32)
    out_re, out_im = apply(vec_re, vec_im)
    for _ in range(POW):
        length = jnp.sqrt(over_blocks(out_re * out_re + out_im * out_im))
        vec_re = out_re / length
        vec_im = out_im / length
        out_re, out_im = apply(out_re, out_im)
        out_re = out_re / length
        out_im = out_im / length
    value_re = over_blocks(vec_re * out_re + vec_im * out_im)
    value_im = over_blocks(vec_re * out_im - vec_im * out_re)

    source = jnp.minimum(lane // per * blocks, LANES - 1)
    mine = lax.broadcasted_iota(jnp.int32, (per, LANES), 0) == lane % per
    for part, value in enumerate((value_re, value_im)):
        row = jnp.sum(jnp.where(mine, pick(value, source), 0.0), axis=0, keepdims=True)
        values_ref[part : part + 1, :] = row[:, : values_ref.shape[1]]

    own = lax.broadcasted_iota(jnp.int32, (per, tall), 1) // wide == lax.broadcasted_iota(jnp.int32, (per, tall), 0)
    is_re = lax.broadcasted_iota(jnp.int32, (per, tall), 1) % wide < blocks
    for g in range(groups):
        spot = g * blocks + lane % blocks
        re = jnp.concatenate([pick(vec_re, spot)] * (tall // LANES), axis=1)
        im = jnp.concatenate([pick(vec_im, spot)] * (tall // LANES), axis=1)
        rows = jnp.concatenate(
            [
                jnp.where(own, jnp.where(is_re, re, -im), 0.0),
                jnp.where(own, jnp.where(is_re, im, re), 0.0),
            ],
            axis=0,
        )
        high = rows.astype(BF16)
        both = jnp.concatenate([high, (rows - high.astype(F32)).astype(BF16)], axis=0)
        at = slice(g * tall, (g + 1) * tall)
        target = jnp.concatenate([near_ref[at, :], far_ref[at, :]], axis=1)
        out = jnp.dot(both, target, preferred_element_type=F32)
        out = out[: 2 * per] + out[2 * per :]
        for position in range(sx):
            lanes = slice(position * LANES, (position + 1) * LANES)
            row = row_at(position, sx, odd)
            for part in range(2):
                first = g * per * 2 * sx + part * sx
                modes_ref[pl.ds(first + row, per, stride=2 * sx), :] = out[part * per : (part + 1) * per, lanes]


def modes_part(odd, core, mine, other, near, far, blocks, ntri, sx, scaling):
    return pl.pallas_call(
        functools.partial(modes_kernel, sx, blocks, scaling),
        out_shape=(
            jax.ShapeDtypeStruct((2, ntri), F32),
            jax.ShapeDtypeStruct((ntri * 2 * sx, LANES), F32),
        ),
        in_specs=[SMEM] * 2 + [VMEM] * 4,
        out_specs=(VMEM,) * 2,
        scratch_shapes=[pltpu.VMEM((2 * mine.shape[0], LANES), F32)],
        compiler_params=limit(12),
        name="modes",
    )(odd, core, mine, other, near, far)


def between_pairs(count):
    inner = [(i, i + 1) for i in range(1, count - 1, 2)]
    return inner + [(b, a) for a, b in inner]


def start_of(k, pairs):
    return k * pairs // PIECES


def along_side(pairs):
    hops = [(2 * b + 1, 2 * b + 3) for b in range(pairs - 1)]
    return hops + [(2 * b + 2, 2 * b) for b in range(pairs - 1)]


def across(k, pairs):
    hops = []
    last = pairs - 1
    for b in range(last):
        if b < start_of(k, pairs):
            hops += [(2 * b + 1, 2 * b + 2), (2 * (last - b), 2 * (last - b) - 1)]
        else:
            hops += [(2 * b + 3, 2 * b + 2), (2 * (last - b) - 2, 2 * (last - b) - 1)]
    return hops


def on_device(u_velocity, v_velocity, cell_weights, block_offsets, triads):
    times, sx, columns = u_velocity.shape
    blocks = block_offsets.shape[0]
    ntri = triads.shape[0]
    slabs = lax.axis_size("space")
    cells = sx * columns * slabs * lax.axis_size("freq")
    scaling = 1.0 / (blocks * math.sqrt(cells))
    pieces = 8
    window, transform = make_table(NFFT)
    picks, places = edge_columns(pieces)
    shift = 0.5 * (np.eye(LANES, k=1, dtype=np.float32) - np.eye(LANES, k=-1, dtype=np.float32))
    v = v_velocity.reshape(times * sx, columns)
    u = u_velocity.reshape(times * sx, columns)
    odd = is_odd()[None]
    core = (lax.axis_index("freq") % 2)[None]
    pairs = triads.T

    near = near_edge(odd, v, sx)
    near = swap(near, "space", 1)
    moved, direct = far_edge(odd, v, sx)
    passed = lax.ppermute(moved, "space", along_side(slabs // 2))
    col_near, col_far = columns_edge(core, u, jnp.asarray(picks, BF16))
    col_near = swap(col_near, "freq", 1)
    col_far = lax.ppermute(col_far, "freq", between_pairs(lax.axis_size("freq")))
    z, sums = local_part(odd, core, v, u, jnp.asarray(shift, BF16), col_near, col_far, jnp.asarray(places, BF16), sx)
    count = slabs // 2
    index = lax.axis_index("space") // 2
    place = jnp.where(odd == 1, index, count - 1 - index)
    far = choose(place, moved, passed, [start_of(k, count) for k in range(PIECES - 1)])
    far = [*far, direct]
    for k in reversed(range(PIECES)):
        far[k] = lax.ppermute(far[k], "space", across(k, count))
    window = jnp.asarray(np.ascontiguousarray(np.broadcast_to(window[:, None], (NFFT, LANES))))
    transform = jnp.asarray(transform, BF16)
    share, near_target = cross_part(
        0, sx - 1, odd, core, block_offsets, pairs, z, sums, [near], cell_weights, window, transform
    )
    mine, other, far_target = cross_part(
        sx - 1, 1, odd, core, block_offsets, pairs, z, sums, far, cell_weights, window, transform, share
    )
    mine = mine + swap(other, "freq", 1)
    mine = sum_over_rest(mine)
    other = swap(mine, "freq", 1)
    values, modes = modes_part(odd, core, mine, other, near_target, far_target, blocks, ntri, sx, scaling)
    return (values.T, modes.reshape(ntri, 2, sx, columns))


def solution(mesh):
    return jax.shard_map(
        on_device,
        mesh=mesh,
        in_specs=(P(None, "space", "freq"), P(None, "space", "freq"), P("space", "freq"), P(), P()),
        out_specs=(P(), P(None, None, "space", "freq")),
        check_vma=False,
    )
```

```python
import functools
import math

import jax
import jax.numpy as jnp
import numpy as np
from jax import lax
from jax.experimental import pallas as pl
from jax.experimental.pallas import tpu as pltpu
from jax.sharding import PartitionSpec as P


NFFT = 256
POW = 4
LANES = 128
CUTS = (0, 4, 11, 16)
F32 = jnp.float32
BF16 = jnp.bfloat16
MIB = 2**20
VMEM = pl.BlockSpec(memory_space=pltpu.VMEM)
SMEM = pl.BlockSpec(memory_space=pltpu.SMEM)


def make_table(length):
    half_len = length // 2
    times_idx = np.arange(length)
    phases = np.arange(half_len)[:, None] * times_idx[None, :] % length
    angles = phases * (2.0 * math.pi / length)
    window = 0.5 - 0.5 * np.cos(times_idx * (2.0 * math.pi / length))
    scaling = 1.0 / np.sqrt(np.sum(window * window))
    transform = np.concatenate([np.cos(angles) * scaling, -np.sin(angles) * scaling], axis=0)
    return window.astype(np.float32), transform.astype(np.float32)


def edge_columns(pieces):
    picks = np.zeros((pieces, 2 * pieces, LANES), np.float32)
    places = np.zeros((pieces, 2 * pieces, LANES), np.float32)
    for m in range(pieces):
        picks[m, m, 0] = 1.0
        picks[m, pieces + m, LANES - 1] = 1.0
        places[m, m, 0] = 0.5
        places[m, pieces + m, LANES - 1] = -0.5
    return picks, places


def is_odd():
    return lax.axis_index("space") % 2


def row_at(position, sx, odd):
    return jnp.where(odd == 1, position, sx - 1 - position)


def limit(mib):
    return pltpu.CompilerParams(vmem_limit_bytes=mib * MIB)


def near_kernel(sx, odd_ref, v_ref, near_ref, plain):
    plain[...] = v_ref[...].astype(F32)
    near_ref[...] = plain[pl.ds(row_at(0, sx, odd_ref[0]), near_ref.shape[0], stride=sx), :].astype(BF16)


def near_edge(odd, v, sx):
    rows = v.shape[0]
    return pl.pallas_call(
        functools.partial(near_kernel, sx),
        out_shape=jax.ShapeDtypeStruct((rows // sx, LANES), BF16),
        in_specs=[SMEM, VMEM],
        out_specs=VMEM,
        scratch_shapes=[pltpu.VMEM((rows, LANES), F32)],
        compiler_params=limit(8),
        name="near",
    )(odd, v)


def far_kernel(sx, odd_ref, v_ref, far_ref, plain):
    plain[...] = v_ref[...].astype(F32)
    far_ref[...] = plain[pl.ds(row_at(sx - 1, sx, odd_ref[0]), far_ref.shape[0], stride=sx), :].astype(BF16)


def far_edge(odd, v, sx):
    rows = v.shape[0]
    return pl.pallas_call(
        functools.partial(far_kernel, sx),
        out_shape=jax.ShapeDtypeStruct((rows // sx, LANES), BF16),
        in_specs=[SMEM, VMEM],
        out_specs=VMEM,
        scratch_shapes=[pltpu.VMEM((rows, LANES), F32)],
        compiler_params=limit(8),
        name="far",
    )(odd, v)


def columns_kernel(pieces, side_ref, u_ref, picks_ref, near_ref, far_ref):
    rows = u_ref.shape[0]
    part = rows // pieces
    cols = jnp.zeros((2 * pieces, part), F32)
    for m in range(pieces):
        cols += lax.dot_general(
            picks_ref[m], u_ref[m * part : (m + 1) * part, :], (((1,), (1,)), ((), ())), preferred_element_type=F32
        )
    low, high = cols[:pieces], cols[pieces:]
    odd = side_ref[0] == 1
    near_ref[...] = jnp.where(odd, low, high).astype(BF16)
    far_ref[...] = jnp.where(odd, high, low).astype(BF16)


def columns_edge(side, u, picks):
    rows = u.shape[0]
    pieces = picks.shape[0]
    return pl.pallas_call(
        functools.partial(columns_kernel, pieces),
        out_shape=(jax.ShapeDtypeStruct((pieces, rows // pieces), BF16),) * 2,
        in_specs=[SMEM] + [VMEM] * 2,
        out_specs=(VMEM,) * 2,
        compiler_params=limit(8),
        name="columns",
    )(side, u, picks)


def local_kernel(
    sx, pieces, odd_ref, side_ref, v_ref, u_ref, shift_ref, near_ref, far_ref, places_ref, z_ref, sum_ref, plain, slope
):
    rows = v_ref.shape[0]
    times = rows // sx
    part = rows // pieces
    odd = odd_ref[0]
    sign = jnp.where(odd == 1, 0.5, -0.5)
    plain[...] = sign * v_ref[...].astype(F32)
    near, far = near_ref[...].astype(F32), far_ref[...].astype(F32)
    side = side_ref[0] == 1
    cols = jnp.concatenate([jnp.where(side, near, far), jnp.where(side, far, near)], axis=0).astype(BF16)
    for m in range(pieces):
        inner = jnp.dot(u_ref[m * part : (m + 1) * part, :], shift_ref[...], preferred_element_type=F32)
        outer = lax.dot_general(cols, places_ref[m], (((0,), (0,)), ((), ())), preferred_element_type=F32)
        slope[m * part : (m + 1) * part, :] = inner + outer
    for position in range(sx):
        z = slope[pl.ds(row_at(position, sx, odd), times, stride=sx), :]
        if position + 1 < sx:
            z += plain[pl.ds(row_at(position + 1, sx, odd), times, stride=sx), :]
        if position > 0:
            z -= plain[pl.ds(row_at(position - 1, sx, odd), times, stride=sx), :]
        z_ref[position] = z
        sum_ref[position] = jnp.sum(z.reshape(times // 8, 8, LANES), axis=0)


def local_part(odd, side, v, u, shift, near, far, places, sx):
    rows = v.shape[0]
    pieces = places.shape[0]
    times = rows // sx
    return pl.pallas_call(
        functools.partial(local_kernel, sx, pieces),
        out_shape=(
            jax.ShapeDtypeStruct((sx, times, LANES), F32),
            jax.ShapeDtypeStruct((sx, 8, LANES), F32),
        ),
        in_specs=[SMEM] * 2 + [VMEM] * 6,
        out_specs=(VMEM,) * 2,
        scratch_shapes=[pltpu.VMEM((rows, LANES), F32), pltpu.VMEM((rows, LANES), F32)],
        compiler_params=limit(20),
        cost_estimate=pl.CostEstimate(flops=1000000000, bytes_accessed=8000000, transcendentals=0),
        name="local",
    )(odd, side, v, u, shift, near, far, places)


def cross_kernel(
    sx, begin, pieces, odd_ref, core_ref, offsets_ref, triads_ref, z_ref, sum_ref, weights_ref, window_ref, transform_ref,
    *rest,
):
    far = begin > 0
    halo_refs, rest = rest[:pieces], rest[pieces:]
    if far:
        before_ref, *rest = rest
    *cross_refs, target_ref, full, spec, prod, packed = rest
    count, times, _ = full.shape
    blocks = offsets_ref.shape[0]
    ntri = triads_ref.shape[1]
    half = NFFT // 2
    groups = LANES // blocks
    per = ntri // groups
    wide = 2 * blocks
    pitch = blocks + 1
    odd = odd_ref[0]
    sign = jnp.where(odd == 1, 0.5, -0.5)
    if not far:
        sign = -sign
    touched = count - 1 if far else 0

    halo_sum = jnp.zeros((8, LANES), F32)
    base = 0
    for halo_ref in halo_refs:
        length = halo_ref.shape[0]
        steps = max(n for n in range(1, 9) if length % (16 * n) == 0)
        chunk = length // steps

        def add_halo(step, carry):
            at = pl.ds(pl.multiple_of(step * chunk, 8), chunk)
            to = pl.ds(pl.multiple_of(base + step * chunk, 8), chunk)
            halo = sign * halo_ref[at, :].astype(F32)
            for row in range(count):
                z = z_ref[begin + row, to, :]
                full[row, to, :] = z + halo if row == touched else z
            return carry + jnp.sum(halo.reshape(chunk // 8, 8, LANES), axis=0)

        halo_sum = lax.fori_loop(0, steps, add_halo, halo_sum)
        base += halo_ref.shape[0]
    means = []
    for row in range(count):
        total = sum_ref[begin + row]
        if row == touched:
            total = total + halo_sum
        means.append(jnp.sum(total, axis=0, keepdims=True) * (1.0 / times))

    def two_blocks(h, carry):
        window = window_ref[...]
        pair = (2 * h, 2 * h + 1)
        for row in range(count):
            windowed = [
                ((full[row, pl.ds(offsets_ref[b], NFFT), :] - means[row]) * window).astype(BF16) for b in pair
            ]
            out = jnp.dot(transform_ref[...], jnp.concatenate(windowed, axis=1), preferred_element_type=F32)
            for n, b in enumerate(pair):
                spec[row, pl.ds(b, NFFT, stride=pitch), :] = out[:, n * LANES : (n + 1) * LANES]
        return carry

    lax.fori_loop(0, blocks // 2, two_blocks, 0, unroll=True)
    weights = [weights_ref[pl.ds(row_at(begin + row, sx, odd), 1), :] for row in range(count)]

    def one_triad(j):
        k = triads_ref[0, j]
        l = triads_ref[1, j]

        def take(f, row):
            re = spec[row, pl.ds(f * pitch, blocks), :]
            im = spec[row, pl.ds((f + half) * pitch, blocks), :]
            return re, im

        base = pl.multiple_of(j * wide, 8)
        for row in range(count):
            lanes = slice(row * LANES, (row + 1) * LANES)
            first_re, first_im = take(k, row)
            second_re, second_im = take(l, row)
            target_re, target_im = take(k + l, row)
            weight = weights[row]
            prod[pl.ds(base, wide), lanes] = jnp.concatenate(
                [
                    (first_re * second_re - first_im * second_im) * weight,
                    (first_re * second_im + first_im * second_re) * weight,
                ],
                axis=0,
            ).astype(BF16)
            target_ref[pl.ds(base, wide), lanes] = jnp.concatenate([target_re, target_im], axis=0).astype(BF16)

    tall = per * wide
    lane = lax.broadcasted_iota(jnp.int32, (wide, tall), 1)
    owner = lane // wide
    is_re = (lax.broadcasted_iota(jnp.int32, (blocks, tall), 1) % wide) < blocks

    def one_group(g, carry):
        for i in range(per):
            one_triad(g * per + i)
        at = pl.ds(pl.multiple_of(g * tall, 8), tall)
        every = lax.dot_general(
            prod[at, :], target_ref[at, :], (((1,), (1,)), ((), ())), preferred_element_type=F32
        )
        kept = every[0:wide]
        for i in range(1, per):
            kept = jnp.where(owner == i, every[i * wide : (i + 1) * wide], kept)
        by_re = kept[0:blocks]
        by_im = kept[blocks:wide]
        ahead = pltpu.roll(by_im, tall - blocks, 1)
        behind = pltpu.roll(by_im, blocks, 1)
        packed[pl.ds(pl.multiple_of(g * blocks, 8), blocks), :] = by_re + jnp.where(is_re, ahead, -behind)
        return carry

    lax.fori_loop(0, groups, one_group, 0, unroll=True)
    share = packed[...].T
    if not far:
        cross_refs[0][...] = share
        return
    share = share + before_ref[...]
    lower, upper = share[: tall // 2], share[tall // 2 :]
    second = core_ref[0] == 1
    cross_refs[0][...] = jnp.where(second, upper, lower)
    cross_refs[1][...] = jnp.where(second, lower, upper)


def cross_part(begin, count, odd, core, offsets, triads, z, sums, halos, weights, window, transform, before=None):
    sx, times, _ = z.shape
    blocks = offsets.shape[0]
    ntri = triads.shape[1]
    groups = LANES // blocks
    wide = 2 * blocks
    tall = ntri // groups * wide
    more = list(halos) + ([] if before is None else [before])
    parts = 1 if before is None else 2
    return pl.pallas_call(
        functools.partial(cross_kernel, sx, begin, len(halos)),
        out_shape=(jax.ShapeDtypeStruct((tall // parts, LANES), F32),) * parts
        + (jax.ShapeDtypeStruct((ntri * wide, count * LANES), BF16),),
        in_specs=[SMEM] * 4 + [VMEM] * (5 + len(more)),
        out_specs=(VMEM,) * (parts + 1),
        scratch_shapes=[
            pltpu.VMEM((count, times, LANES), F32),
            pltpu.VMEM((count, NFFT * (blocks + 1), LANES), F32),
            pltpu.VMEM((ntri * wide, count * LANES), BF16),
            pltpu.VMEM((LANES, tall), F32),
        ],
        compiler_params=limit(26),
        cost_estimate=pl.CostEstimate(flops=2000000000, bytes_accessed=4000000, transcendentals=0),
        name="cross_far" if begin else "cross_near",
    )(odd, core, offsets, triads, z, sums, weights, window, transform, *more)


def swap(x, axis, bit):
    count = lax.axis_size(axis)
    return lax.ppermute(x, axis, [(i, i ^ bit) for i in range(count)])


def sum_over_rest(x):
    slabs, parts = lax.axis_size("space"), lax.axis_size("freq")
    hops = [bit * parts for bit in bits_of(slabs)]
    across = [bit for bit in bits_of(parts)[1:]]
    first = hops[:1] + across + hops[1:]
    second = across + hops[:1] + hops[:0:-1]
    for one, other in zip(first, second, strict=True):
        pairs = [(i, i ^ (other if i % 2 else one)) for i in range(slabs * parts)]
        x = x + lax.ppermute(x, ("space", "freq"), pairs)
    return x


def bits_of(count):
    return [1 << n for n in range(count.bit_length() - 1)]


def modes_kernel(sx, blocks, scaling, odd_ref, core_ref, mine_ref, other_ref, near_ref, far_ref, values_ref, modes_ref, cross):
    tall = cross.shape[0]
    wide = 2 * blocks
    per = tall // wide
    groups = LANES // blocks
    odd = odd_ref[0]
    core = core_ref[0]
    half = tall // 2
    cross[pl.ds(pl.multiple_of(core * half, 8), half), :] = mine_ref[...] * scaling
    cross[pl.ds(pl.multiple_of((1 - core) * half, 8), half), :] = other_ref[...] * scaling
    lane = lax.broadcasted_iota(jnp.int32, (per, LANES), 1)
    start = lane - lane % blocks

    mat_re = [cross[pl.ds(c, per, stride=wide), :] for c in range(blocks)]
    mat_im = [cross[pl.ds(blocks + c, per, stride=wide), :] for c in range(blocks)]

    def pick(x, index):
        return jnp.take_along_axis(x, index, axis=1)

    spots = [start + c for c in range(blocks)]

    def tree(terms):
        while len(terms) > 1:
            terms = [sum(terms[n : n + 2]) for n in range(0, len(terms), 2)]
        return terms[0]

    def apply(part_re, part_im):
        re = [pick(part_re, spot) for spot in spots]
        im = [pick(part_im, spot) for spot in spots]
        every = range(blocks)
        out_re = tree([mat_re[c] * re[c] - mat_im[c] * im[c] for c in every])
        out_im = tree([mat_re[c] * im[c] + mat_im[c] * re[c] for c in every])
        return out_re, out_im

    def over_blocks(x):
        bit = 1
        while bit < blocks:
            if 4 * bit <= blocks:
                x = (x + pick(x, lane ^ bit)) + (pick(x, lane ^ (2 * bit)) + pick(x, lane ^ (3 * bit)))
                bit *= 4
            else:
                x = x + pick(x, lane ^ bit)
                bit *= 2
        return x

    vec_re = jnp.full((per, LANES), 1.0 / math.sqrt(blocks), F32)
    vec_im = jnp.zeros((per, LANES), F32)
    out_re, out_im = apply(vec_re, vec_im)
    for _ in range(POW):
        length = jnp.sqrt(over_blocks(out_re * out_re + out_im * out_im))
        vec_re = out_re / length
        vec_im = out_im / length
        out_re, out_im = apply(out_re, out_im)
        out_re = out_re / length
        out_im = out_im / length
    value_re = over_blocks(vec_re * out_re + vec_im * out_im)
    value_im = over_blocks(vec_re * out_im - vec_im * out_re)

    source = jnp.minimum(lane // per * blocks, LANES - 1)
    mine = lax.broadcasted_iota(jnp.int32, (per, LANES), 0) == lane % per
    for part, value in enumerate((value_re, value_im)):
        row = jnp.sum(jnp.where(mine, pick(value, source), 0.0), axis=0, keepdims=True)
        values_ref[part : part + 1, :] = row[:, : values_ref.shape[1]]

    own = lax.broadcasted_iota(jnp.int32, (per, tall), 1) // wide == lax.broadcasted_iota(jnp.int32, (per, tall), 0)
    is_re = lax.broadcasted_iota(jnp.int32, (per, tall), 1) % wide < blocks
    for g in range(groups):
        spot = g * blocks + lane % blocks
        re = jnp.concatenate([pick(vec_re, spot)] * (tall // LANES), axis=1)
        im = jnp.concatenate([pick(vec_im, spot)] * (tall // LANES), axis=1)
        rows = jnp.concatenate(
            [
                jnp.where(own, jnp.where(is_re, re, -im), 0.0),
                jnp.where(own, jnp.where(is_re, im, re), 0.0),
            ],
            axis=0,
        )
        high = rows.astype(BF16)
        both = jnp.concatenate([high, (rows - high.astype(F32)).astype(BF16)], axis=0)
        at = slice(g * tall, (g + 1) * tall)
        target = jnp.concatenate([near_ref[at, :], far_ref[at, :]], axis=1)
        out = jnp.dot(both, target, preferred_element_type=F32)
        out = out[: 2 * per] + out[2 * per :]
        for position in range(sx):
            lanes = slice(position * LANES, (position + 1) * LANES)
            row = row_at(position, sx, odd)
            for part in range(2):
                first = g * per * 2 * sx + part * sx
                modes_ref[pl.ds(first + row, per, stride=2 * sx), :] = out[part * per : (part + 1) * per, lanes]


def modes_part(odd, core, mine, other, near, far, blocks, ntri, sx, scaling):
    return pl.pallas_call(
        functools.partial(modes_kernel, sx, blocks, scaling),
        out_shape=(
            jax.ShapeDtypeStruct((2, ntri), F32),
            jax.ShapeDtypeStruct((ntri * 2 * sx, LANES), F32),
        ),
        in_specs=[SMEM] * 2 + [VMEM] * 4,
        out_specs=(VMEM,) * 2,
        scratch_shapes=[pltpu.VMEM((2 * mine.shape[0], LANES), F32)],
        compiler_params=limit(12),
        name="modes",
    )(odd, core, mine, other, near, far)


def between_pairs(count):
    inner = [(i, i + 1) for i in range(1, count - 1, 2)]
    return inner + [(b, a) for a, b in inner]


def on_device(u_velocity, v_velocity, cell_weights, block_offsets, triads):
    times, sx, columns = u_velocity.shape
    blocks = block_offsets.shape[0]
    ntri = triads.shape[0]
    slabs = lax.axis_size("space")
    cells = sx * columns * slabs * lax.axis_size("freq")
    scaling = 1.0 / (blocks * math.sqrt(cells))
    pieces = 8
    window, transform = make_table(NFFT)
    picks, places = edge_columns(pieces)
    shift = 0.5 * (np.eye(LANES, k=1, dtype=np.float32) - np.eye(LANES, k=-1, dtype=np.float32))
    v = v_velocity.reshape(times * sx, columns)
    u = u_velocity.reshape(times * sx, columns)
    odd = is_odd()[None]
    core = (lax.axis_index("freq") % 2)[None]
    pairs = triads.T

    near = []
    for begin, end in zip(CUTS[:-1], CUTS[1:]):
        begin, end = (times * cut // 1024 * 64 if cut < 16 else times for cut in (begin, end))
        edge = near_edge(odd, v[begin * sx : end * sx], sx)
        near.append(swap(edge, "space", 1))
    col_near, col_far = columns_edge(core, u, jnp.asarray(picks, BF16))
    col_near = swap(col_near, "freq", 1)
    col_far = lax.ppermute(col_far, "freq", between_pairs(lax.axis_size("freq")))
    z, sums = local_part(odd, core, v, u, jnp.asarray(shift, BF16), col_near, col_far, jnp.asarray(places, BF16), sx)
    far = far_edge(odd, v, sx)
    far = lax.ppermute(far, "space", between_pairs(slabs))
    window = jnp.asarray(np.ascontiguousarray(np.broadcast_to(window[:, None], (NFFT, LANES))))
    transform = jnp.asarray(transform, BF16)
    share, near_target = cross_part(
        0, sx - 1, odd, core, block_offsets, pairs, z, sums, near, cell_weights, window, transform
    )
    mine, other, far_target = cross_part(
        sx - 1, 1, odd, core, block_offsets, pairs, z, sums, [far], cell_weights, window, transform, share
    )
    mine = mine + swap(other, "freq", 1)
    mine = sum_over_rest(mine)
    other = swap(mine, "freq", 1)
    values, modes = modes_part(odd, core, mine, other, near_target, far_target, blocks, ntri, sx, scaling)
    return (values.T, modes.reshape(ntri, 2, sx, columns))


def solution(mesh):
    return jax.shard_map(
        on_device,
        mesh=mesh,
        in_specs=(P(None, "space", "freq"), P(None, "space", "freq"), P("space", "freq"), P(), P()),
        out_specs=(P(), P(None, None, "space", "freq")),
        check_vma=False,
    )
```

```python
import functools
import math

import jax
import jax.numpy as jnp
import numpy as np
from jax import lax
from jax.experimental import pallas as pl
from jax.experimental.pallas import tpu as pltpu
from jax.sharding import PartitionSpec as P


NFFT = 256
POW = 4
LANES = 128
AHEAD = 11
F32 = jnp.float32
BF16 = jnp.bfloat16
MIB = 2**20
VMEM = pl.BlockSpec(memory_space=pltpu.VMEM)
SMEM = pl.BlockSpec(memory_space=pltpu.SMEM)


def make_table(length):
    half_len = length // 2
    times_idx = np.arange(length)
    phases = np.arange(half_len)[:, None] * times_idx[None, :] % length
    angles = phases * (2.0 * math.pi / length)
    window = 0.5 - 0.5 * np.cos(times_idx * (2.0 * math.pi / length))
    scaling = 1.0 / np.sqrt(np.sum(window * window))
    transform = np.concatenate([np.cos(angles) * scaling, -np.sin(angles) * scaling], axis=0)
    return window.astype(np.float32), transform.astype(np.float32)


def edge_columns(pieces):
    picks = np.zeros((pieces, 2 * pieces, LANES), np.float32)
    places = np.zeros((pieces, 2 * pieces, LANES), np.float32)
    for m in range(pieces):
        picks[m, m, 0] = 1.0
        picks[m, pieces + m, LANES - 1] = 1.0
        places[m, m, 0] = 0.5
        places[m, pieces + m, LANES - 1] = -0.5
    return picks, places


def is_odd():
    return lax.axis_index("space") % 2


def row_at(position, sx, odd):
    return jnp.where(odd == 1, position, sx - 1 - position)


def limit(mib):
    return pltpu.CompilerParams(vmem_limit_bytes=mib * MIB)


def near_kernel(sx, odd_ref, v_ref, early_ref, late_ref, plain):
    plain[...] = v_ref[...].astype(F32)
    row = row_at(0, sx, odd_ref[0])
    early, late = early_ref.shape[0], late_ref.shape[0]
    early_ref[...] = plain[pl.ds(row, early, stride=sx), :].astype(BF16)
    late_ref[...] = plain[pl.ds(early * sx + row, late, stride=sx), :].astype(BF16)


def near_edge(odd, v, sx):
    rows = v.shape[0]
    early = rows // sx * AHEAD // 1024 * 64
    return pl.pallas_call(
        functools.partial(near_kernel, sx),
        out_shape=(
            jax.ShapeDtypeStruct((early, LANES), BF16),
            jax.ShapeDtypeStruct((rows // sx - early, LANES), BF16),
        ),
        in_specs=[SMEM, VMEM],
        out_specs=(VMEM,) * 2,
        scratch_shapes=[pltpu.VMEM((rows, LANES), F32)],
        compiler_params=limit(8),
        name="near",
    )(odd, v)


def far_kernel(sx, odd_ref, v_ref, far_ref, plain):
    plain[...] = v_ref[...].astype(F32)
    far_ref[...] = plain[pl.ds(row_at(sx - 1, sx, odd_ref[0]), far_ref.shape[0], stride=sx), :].astype(BF16)


def far_edge(odd, v, sx):
    rows = v.shape[0]
    return pl.pallas_call(
        functools.partial(far_kernel, sx),
        out_shape=jax.ShapeDtypeStruct((rows // sx, LANES), BF16),
        in_specs=[SMEM, VMEM],
        out_specs=VMEM,
        scratch_shapes=[pltpu.VMEM((rows, LANES), F32)],
        compiler_params=limit(8),
        name="far",
    )(odd, v)


def columns_kernel(pieces, side_ref, u_ref, picks_ref, near_ref, far_ref):
    rows = u_ref.shape[0]
    part = rows // pieces
    cols = jnp.zeros((2 * pieces, part), F32)
    for m in range(pieces):
        cols += lax.dot_general(
            picks_ref[m], u_ref[m * part : (m + 1) * part, :], (((1,), (1,)), ((), ())), preferred_element_type=F32
        )
    low, high = cols[:pieces], cols[pieces:]
    odd = side_ref[0] == 1
    near_ref[...] = jnp.where(odd, low, high).astype(BF16)
    far_ref[...] = jnp.where(odd, high, low).astype(BF16)


def columns_edge(side, u, picks):
    rows = u.shape[0]
    pieces = picks.shape[0]
    return pl.pallas_call(
        functools.partial(columns_kernel, pieces),
        out_shape=(jax.ShapeDtypeStruct((pieces, rows // pieces), BF16),) * 2,
        in_specs=[SMEM] + [VMEM] * 2,
        out_specs=(VMEM,) * 2,
        compiler_params=limit(8),
        name="columns",
    )(side, u, picks)


def local_kernel(
    sx, pieces, odd_ref, side_ref, v_ref, u_ref, shift_ref, near_ref, far_ref, places_ref, z_ref, sum_ref, plain, slope
):
    rows = v_ref.shape[0]
    times = rows // sx
    part = rows // pieces
    odd = odd_ref[0]
    sign = jnp.where(odd == 1, 0.5, -0.5)
    plain[...] = sign * v_ref[...].astype(F32)
    near, far = near_ref[...].astype(F32), far_ref[...].astype(F32)
    side = side_ref[0] == 1
    cols = jnp.concatenate([jnp.where(side, near, far), jnp.where(side, far, near)], axis=0).astype(BF16)
    for m in range(pieces):
        inner = jnp.dot(u_ref[m * part : (m + 1) * part, :], shift_ref[...], preferred_element_type=F32)
        outer = lax.dot_general(cols, places_ref[m], (((0,), (0,)), ((), ())), preferred_element_type=F32)
        slope[m * part : (m + 1) * part, :] = inner + outer
    for position in range(sx):
        z = slope[pl.ds(row_at(position, sx, odd), times, stride=sx), :]
        if position + 1 < sx:
            z += plain[pl.ds(row_at(position + 1, sx, odd), times, stride=sx), :]
        if position > 0:
            z -= plain[pl.ds(row_at(position - 1, sx, odd), times, stride=sx), :]
        z_ref[position] = z
        sum_ref[position] = jnp.sum(z.reshape(times // 8, 8, LANES), axis=0)


def local_part(odd, side, v, u, shift, near, far, places, sx):
    rows = v.shape[0]
    pieces = places.shape[0]
    times = rows // sx
    return pl.pallas_call(
        functools.partial(local_kernel, sx, pieces),
        out_shape=(
            jax.ShapeDtypeStruct((sx, times, LANES), F32),
            jax.ShapeDtypeStruct((sx, 8, LANES), F32),
        ),
        in_specs=[SMEM] * 2 + [VMEM] * 6,
        out_specs=(VMEM,) * 2,
        scratch_shapes=[pltpu.VMEM((rows, LANES), F32), pltpu.VMEM((rows, LANES), F32)],
        compiler_params=limit(20),
        cost_estimate=pl.CostEstimate(flops=1000000000, bytes_accessed=8000000, transcendentals=0),
        name="local",
    )(odd, side, v, u, shift, near, far, places)


def cross_kernel(
    sx, begin, pieces, odd_ref, core_ref, offsets_ref, triads_ref, z_ref, sum_ref, weights_ref, window_ref, transform_ref,
    *rest,
):
    far = begin > 0
    halo_refs, rest = rest[:pieces], rest[pieces:]
    if far:
        before_ref, *rest = rest
    *cross_refs, target_ref, full, spec, prod, packed = rest
    count, times, _ = full.shape
    blocks = offsets_ref.shape[0]
    ntri = triads_ref.shape[1]
    half = NFFT // 2
    groups = LANES // blocks
    per = ntri // groups
    wide = 2 * blocks
    pitch = blocks + 1
    odd = odd_ref[0]
    sign = jnp.where(odd == 1, 0.5, -0.5)
    if not far:
        sign = -sign
    touched = count - 1 if far else 0

    halo_sum = jnp.zeros((8, LANES), F32)
    base = 0
    for halo_ref in halo_refs:
        length = halo_ref.shape[0]
        steps = max(n for n in range(1, 9) if length % (16 * n) == 0)
        chunk = length // steps

        def add_halo(step, carry):
            at = pl.ds(pl.multiple_of(step * chunk, 8), chunk)
            to = pl.ds(pl.multiple_of(base + step * chunk, 8), chunk)
            halo = sign * halo_ref[at, :].astype(F32)
            for row in range(count):
                z = z_ref[begin + row, to, :]
                full[row, to, :] = z + halo if row == touched else z
            return carry + jnp.sum(halo.reshape(chunk // 8, 8, LANES), axis=0)

        halo_sum = lax.fori_loop(0, steps, add_halo, halo_sum)
        base += halo_ref.shape[0]
    means = []
    for row in range(count):
        total = sum_ref[begin + row]
        if row == touched:
            total = total + halo_sum
        means.append(jnp.sum(total, axis=0, keepdims=True) * (1.0 / times))

    def two_blocks(h, carry):
        window = window_ref[...]
        pair = (2 * h, 2 * h + 1)
        for row in range(count):
            windowed = [
                ((full[row, pl.ds(offsets_ref[b], NFFT), :] - means[row]) * window).astype(BF16) for b in pair
            ]
            out = jnp.dot(transform_ref[...], jnp.concatenate(windowed, axis=1), preferred_element_type=F32)
            for n, b in enumerate(pair):
                spec[row, pl.ds(b, NFFT, stride=pitch), :] = out[:, n * LANES : (n + 1) * LANES]
        return carry

    lax.fori_loop(0, blocks // 2, two_blocks, 0, unroll=True)
    weights = [weights_ref[pl.ds(row_at(begin + row, sx, odd), 1), :] for row in range(count)]

    def one_triad(j):
        k = triads_ref[0, j]
        l = triads_ref[1, j]

        def take(f, row):
            re = spec[row, pl.ds(f * pitch, blocks), :]
            im = spec[row, pl.ds((f + half) * pitch, blocks), :]
            return re, im

        base = pl.multiple_of(j * wide, 8)
        for row in range(count):
            lanes = slice(row * LANES, (row + 1) * LANES)
            first_re, first_im = take(k, row)
            second_re, second_im = take(l, row)
            target_re, target_im = take(k + l, row)
            weight = weights[row]
            prod[pl.ds(base, wide), lanes] = jnp.concatenate(
                [
                    (first_re * second_re - first_im * second_im) * weight,
                    (first_re * second_im + first_im * second_re) * weight,
                ],
                axis=0,
            ).astype(BF16)
            target_ref[pl.ds(base, wide), lanes] = jnp.concatenate([target_re, target_im], axis=0).astype(BF16)

    tall = per * wide
    lane = lax.broadcasted_iota(jnp.int32, (wide, tall), 1)
    owner = lane // wide
    is_re = (lax.broadcasted_iota(jnp.int32, (blocks, tall), 1) % wide) < blocks

    def one_group(g, carry):
        for i in range(per):
            one_triad(g * per + i)
        at = pl.ds(pl.multiple_of(g * tall, 8), tall)
        every = lax.dot_general(
            prod[at, :], target_ref[at, :], (((1,), (1,)), ((), ())), preferred_element_type=F32
        )
        kept = every[0:wide]
        for i in range(1, per):
            kept = jnp.where(owner == i, every[i * wide : (i + 1) * wide], kept)
        by_re = kept[0:blocks]
        by_im = kept[blocks:wide]
        ahead = pltpu.roll(by_im, tall - blocks, 1)
        behind = pltpu.roll(by_im, blocks, 1)
        packed[pl.ds(pl.multiple_of(g * blocks, 8), blocks), :] = by_re + jnp.where(is_re, ahead, -behind)
        return carry

    lax.fori_loop(0, groups, one_group, 0, unroll=True)
    share = packed[...].T
    if not far:
        cross_refs[0][...] = share
        return
    share = share + before_ref[...]
    lower, upper = share[: tall // 2], share[tall // 2 :]
    second = core_ref[0] == 1
    cross_refs[0][...] = jnp.where(second, upper, lower)
    cross_refs[1][...] = jnp.where(second, lower, upper)


def cross_part(begin, count, odd, core, offsets, triads, z, sums, halos, weights, window, transform, before=None):
    sx, times, _ = z.shape
    blocks = offsets.shape[0]
    ntri = triads.shape[1]
    groups = LANES // blocks
    wide = 2 * blocks
    tall = ntri // groups * wide
    more = list(halos) + ([] if before is None else [before])
    parts = 1 if before is None else 2
    return pl.pallas_call(
        functools.partial(cross_kernel, sx, begin, len(halos)),
        out_shape=(jax.ShapeDtypeStruct((tall // parts, LANES), F32),) * parts
        + (jax.ShapeDtypeStruct((ntri * wide, count * LANES), BF16),),
        in_specs=[SMEM] * 4 + [VMEM] * (5 + len(more)),
        out_specs=(VMEM,) * (parts + 1),
        scratch_shapes=[
            pltpu.VMEM((count, times, LANES), F32),
            pltpu.VMEM((count, NFFT * (blocks + 1), LANES), F32),
            pltpu.VMEM((ntri * wide, count * LANES), BF16),
            pltpu.VMEM((LANES, tall), F32),
        ],
        compiler_params=limit(26),
        cost_estimate=pl.CostEstimate(flops=2000000000, bytes_accessed=4000000, transcendentals=0),
        name="cross_far" if begin else "cross_near",
    )(odd, core, offsets, triads, z, sums, weights, window, transform, *more)


def swap(x, axis, bit):
    count = lax.axis_size(axis)
    return lax.ppermute(x, axis, [(i, i ^ bit) for i in range(count)])


def sum_over_rest(x):
    slabs, parts = lax.axis_size("space"), lax.axis_size("freq")
    hops = [bit * parts for bit in bits_of(slabs)]
    first = hops[:1] + bits_of(parts)[1:] + hops[1:]
    second = first[2:] + first[:2]

    def swapped(one, other):
        pairs = [(i, i ^ (other if i % 2 else one)) for i in range(slabs * parts)]
        return lax.ppermute(sent, ("space", "freq"), pairs).astype(F32)

    for n in range(0, len(first), 2):
        one, other = first[n : n + 2], second[n : n + 2]
        x = lax.reduce_precision(x, 8, 7)
        sent = x.astype(BF16)
        if len(one) == 1:
            x = x + swapped(one[0], other[0])
            continue
        near, far, both = swapped(one[0], other[0]), swapped(one[1], other[1]), swapped(sum(one), sum(other))
        x = (x + near) + (far + both)
    return x


def bits_of(count):
    return [1 << n for n in range(count.bit_length() - 1)]


def modes_kernel(sx, blocks, scaling, odd_ref, core_ref, mine_ref, other_ref, near_ref, far_ref, values_ref, modes_ref, cross):
    tall = cross.shape[0]
    wide = 2 * blocks
    per = tall // wide
    groups = LANES // blocks
    odd = odd_ref[0]
    core = core_ref[0]
    half = tall // 2
    cross[pl.ds(pl.multiple_of(core * half, 8), half), :] = mine_ref[...] * scaling
    cross[pl.ds(pl.multiple_of((1 - core) * half, 8), half), :] = other_ref[...] * scaling
    lane = lax.broadcasted_iota(jnp.int32, (per, LANES), 1)
    start = lane - lane % blocks

    mat_re = [cross[pl.ds(c, per, stride=wide), :] for c in range(blocks)]
    mat_im = [cross[pl.ds(blocks + c, per, stride=wide), :] for c in range(blocks)]

    def pick(x, index):
        return jnp.take_along_axis(x, index, axis=1)

    spots = [start + c for c in range(blocks)]

    def tree(terms):
        while len(terms) > 1:
            terms = [sum(terms[n : n + 2]) for n in range(0, len(terms), 2)]
        return terms[0]

    def apply(part_re, part_im):
        re = [pick(part_re, spot) for spot in spots]
        im = [pick(part_im, spot) for spot in spots]
        every = range(blocks)
        out_re = tree([mat_re[c] * re[c] - mat_im[c] * im[c] for c in every])
        out_im = tree([mat_re[c] * im[c] + mat_im[c] * re[c] for c in every])
        return out_re, out_im

    def over_blocks(x):
        bit = 1
        while bit < blocks:
            if 4 * bit <= blocks:
                x = (x + pick(x, lane ^ bit)) + (pick(x, lane ^ (2 * bit)) + pick(x, lane ^ (3 * bit)))
                bit *= 4
            else:
                x = x + pick(x, lane ^ bit)
                bit *= 2
        return x

    vec_re = jnp.full((per, LANES), 1.0 / math.sqrt(blocks), F32)
    vec_im = jnp.zeros((per, LANES), F32)
    out_re, out_im = apply(vec_re, vec_im)
    for _ in range(POW):
        length = jnp.sqrt(over_blocks(out_re * out_re + out_im * out_im))
        vec_re = out_re / length
        vec_im = out_im / length
        out_re, out_im = apply(out_re, out_im)
        out_re = out_re / length
        out_im = out_im / length
    value_re = over_blocks(vec_re * out_re + vec_im * out_im)
    value_im = over_blocks(vec_re * out_im - vec_im * out_re)

    source = jnp.minimum(lane // per * blocks, LANES - 1)
    mine = lax.broadcasted_iota(jnp.int32, (per, LANES), 0) == lane % per
    for part, value in enumerate((value_re, value_im)):
        row = jnp.sum(jnp.where(mine, pick(value, source), 0.0), axis=0, keepdims=True)
        values_ref[part : part + 1, :] = row[:, : values_ref.shape[1]]

    own = lax.broadcasted_iota(jnp.int32, (per, tall), 1) // wide == lax.broadcasted_iota(jnp.int32, (per, tall), 0)
    is_re = lax.broadcasted_iota(jnp.int32, (per, tall), 1) % wide < blocks
    for g in range(groups):
        spot = g * blocks + lane % blocks
        re = jnp.concatenate([pick(vec_re, spot)] * (tall // LANES), axis=1)
        im = jnp.concatenate([pick(vec_im, spot)] * (tall // LANES), axis=1)
        rows = jnp.concatenate(
            [
                jnp.where(own, jnp.where(is_re, re, -im), 0.0),
                jnp.where(own, jnp.where(is_re, im, re), 0.0),
            ],
            axis=0,
        )
        high = rows.astype(BF16)
        both = jnp.concatenate([high, (rows - high.astype(F32)).astype(BF16)], axis=0)
        at = slice(g * tall, (g + 1) * tall)
        target = jnp.concatenate([near_ref[at, :], far_ref[at, :]], axis=1)
        out = jnp.dot(both, target, preferred_element_type=F32)
        out = out[: 2 * per] + out[2 * per :]
        for position in range(sx):
            lanes = slice(position * LANES, (position + 1) * LANES)
            row = row_at(position, sx, odd)
            for part in range(2):
                first = g * per * 2 * sx + part * sx
                modes_ref[pl.ds(first + row, per, stride=2 * sx), :] = out[part * per : (part + 1) * per, lanes]


def modes_part(odd, core, mine, other, near, far, blocks, ntri, sx, scaling):
    return pl.pallas_call(
        functools.partial(modes_kernel, sx, blocks, scaling),
        out_shape=(
            jax.ShapeDtypeStruct((2, ntri), F32),
            jax.ShapeDtypeStruct((ntri * 2 * sx, LANES), F32),
        ),
        in_specs=[SMEM] * 2 + [VMEM] * 4,
        out_specs=(VMEM,) * 2,
        scratch_shapes=[pltpu.VMEM((2 * mine.shape[0], LANES), F32)],
        compiler_params=limit(12),
        name="modes",
    )(odd, core, mine, other, near, far)


def between_pairs(count):
    inner = [(i, i + 1) for i in range(1, count - 1, 2)]
    return inner + [(b, a) for a, b in inner]


def on_device(u_velocity, v_velocity, cell_weights, block_offsets, triads):
    times, sx, columns = u_velocity.shape
    blocks = block_offsets.shape[0]
    ntri = triads.shape[0]
    slabs = lax.axis_size("space")
    cells = sx * columns * slabs * lax.axis_size("freq")
    scaling = 1.0 / (blocks * math.sqrt(cells))
    pieces = 8
    window, transform = make_table(NFFT)
    picks, places = edge_columns(pieces)
    shift = 0.5 * (np.eye(LANES, k=1, dtype=np.float32) - np.eye(LANES, k=-1, dtype=np.float32))
    v = v_velocity.reshape(times * sx, columns)
    u = u_velocity.reshape(times * sx, columns)
    odd = is_odd()[None]
    core = (lax.axis_index("freq") % 2)[None]
    pairs = triads.T

    early, late = near_edge(odd, v, sx)
    early = swap(early, "space", 1)
    late = swap(late, "space", 1)
    col_near, col_far = columns_edge(core, u, jnp.asarray(picks, BF16))
    col_near = swap(col_near, "freq", 1)
    col_far = lax.ppermute(col_far, "freq", between_pairs(lax.axis_size("freq")))
    z, sums = local_part(odd, core, v, u, jnp.asarray(shift, BF16), col_near, col_far, jnp.asarray(places, BF16), sx)
    far = far_edge(odd, v, sx)
    far = lax.ppermute(far, "space", between_pairs(slabs))
    window = jnp.asarray(np.ascontiguousarray(np.broadcast_to(window[:, None], (NFFT, LANES))))
    transform = jnp.asarray(transform, BF16)
    share, near_target = cross_part(
        0, sx - 1, odd, core, block_offsets, pairs, z, sums, [early, late], cell_weights, window, transform
    )
    mine, other, far_target = cross_part(
        sx - 1, 1, odd, core, block_offsets, pairs, z, sums, [far], cell_weights, window, transform, share
    )
    mine = mine + swap(other, "freq", 1)
    mine = sum_over_rest(mine)
    other = swap(mine, "freq", 1)
    values, modes = modes_part(odd, core, mine, other, near_target, far_target, blocks, ntri, sx, scaling)
    return (values.T, modes.reshape(ntri, 2, sx, columns))


def solution(mesh):
    return jax.shard_map(
        on_device,
        mesh=mesh,
        in_specs=(P(None, "space", "freq"), P(None, "space", "freq"), P("space", "freq"), P(), P()),
        out_specs=(P(), P(None, None, "space", "freq")),
        check_vma=False,
    )
```

```python
import functools
import math

import jax
import jax.numpy as jnp
import numpy as np
from jax import lax
from jax.experimental import pallas as pl
from jax.experimental.pallas import tpu as pltpu
from jax.sharding import PartitionSpec as P


NFFT = 256
POW = 4
LANES = 128
AHEAD = 11
F32 = jnp.float32
BF16 = jnp.bfloat16
MIB = 2**20
VMEM = pl.BlockSpec(memory_space=pltpu.VMEM)
SMEM = pl.BlockSpec(memory_space=pltpu.SMEM)


def make_table(length):
    half_len = length // 2
    times_idx = np.arange(length)
    phases = np.arange(half_len)[:, None] * times_idx[None, :] % length
    angles = phases * (2.0 * math.pi / length)
    window = 0.5 - 0.5 * np.cos(times_idx * (2.0 * math.pi / length))
    scaling = 1.0 / np.sqrt(np.sum(window * window))
    transform = np.concatenate([np.cos(angles) * scaling, -np.sin(angles) * scaling], axis=0)
    return window.astype(np.float32), transform.astype(np.float32)


def edge_columns(pieces):
    picks = np.zeros((pieces, 2 * pieces, LANES), np.float32)
    places = np.zeros((pieces, 2 * pieces, LANES), np.float32)
    for m in range(pieces):
        picks[m, m, 0] = 1.0
        picks[m, pieces + m, LANES - 1] = 1.0
        places[m, m, 0] = 0.5
        places[m, pieces + m, LANES - 1] = -0.5
    return picks, places


def is_odd():
    return lax.axis_index("space") % 2


def row_at(position, sx, odd):
    return jnp.where(odd == 1, position, sx - 1 - position)


def limit(mib):
    return pltpu.CompilerParams(vmem_limit_bytes=mib * MIB)


def near_kernel(sx, odd_ref, v_ref, early_ref, late_ref, plain):
    plain[...] = v_ref[...].astype(F32)
    row = row_at(0, sx, odd_ref[0])
    early, late = early_ref.shape[0], late_ref.shape[0]
    early_ref[...] = plain[pl.ds(row, early, stride=sx), :].astype(BF16)
    late_ref[...] = plain[pl.ds(early * sx + row, late, stride=sx), :].astype(BF16)


def near_edge(odd, v, sx):
    rows = v.shape[0]
    early = rows // sx * AHEAD // 1024 * 64
    return pl.pallas_call(
        functools.partial(near_kernel, sx),
        out_shape=(
            jax.ShapeDtypeStruct((early, LANES), BF16),
            jax.ShapeDtypeStruct((rows // sx - early, LANES), BF16),
        ),
        in_specs=[SMEM, VMEM],
        out_specs=(VMEM,) * 2,
        scratch_shapes=[pltpu.VMEM((rows, LANES), F32)],
        compiler_params=limit(8),
        name="near",
    )(odd, v)


def far_kernel(sx, odd_ref, v_ref, far_ref, plain):
    plain[...] = v_ref[...].astype(F32)
    far_ref[...] = plain[pl.ds(row_at(sx - 1, sx, odd_ref[0]), far_ref.shape[0], stride=sx), :].astype(BF16)


def far_edge(odd, v, sx):
    rows = v.shape[0]
    return pl.pallas_call(
        functools.partial(far_kernel, sx),
        out_shape=jax.ShapeDtypeStruct((rows // sx, LANES), BF16),
        in_specs=[SMEM, VMEM],
        out_specs=VMEM,
        scratch_shapes=[pltpu.VMEM((rows, LANES), F32)],
        compiler_params=limit(8),
        name="far",
    )(odd, v)


def columns_kernel(pieces, side_ref, u_ref, picks_ref, near_ref, far_ref):
    rows = u_ref.shape[0]
    part = rows // pieces
    cols = jnp.zeros((2 * pieces, part), F32)
    for m in range(pieces):
        cols += lax.dot_general(
            picks_ref[m], u_ref[m * part : (m + 1) * part, :], (((1,), (1,)), ((), ())), preferred_element_type=F32
        )
    low, high = cols[:pieces], cols[pieces:]
    odd = side_ref[0] == 1
    near_ref[...] = jnp.where(odd, low, high).astype(BF16)
    far_ref[...] = jnp.where(odd, high, low).astype(BF16)


def columns_edge(side, u, picks):
    rows = u.shape[0]
    pieces = picks.shape[0]
    return pl.pallas_call(
        functools.partial(columns_kernel, pieces),
        out_shape=(jax.ShapeDtypeStruct((pieces, rows // pieces), BF16),) * 2,
        in_specs=[SMEM] + [VMEM] * 2,
        out_specs=(VMEM,) * 2,
        compiler_params=limit(8),
        name="columns",
    )(side, u, picks)


def local_kernel(
    sx, pieces, odd_ref, side_ref, v_ref, u_ref, shift_ref, near_ref, far_ref, places_ref, z_ref, sum_ref, plain, slope
):
    rows = v_ref.shape[0]
    times = rows // sx
    part = rows // pieces
    odd = odd_ref[0]
    sign = jnp.where(odd == 1, 0.5, -0.5)
    plain[...] = sign * v_ref[...].astype(F32)
    near, far = near_ref[...].astype(F32), far_ref[...].astype(F32)
    side = side_ref[0] == 1
    cols = jnp.concatenate([jnp.where(side, near, far), jnp.where(side, far, near)], axis=0).astype(BF16)
    for m in range(pieces):
        inner = jnp.dot(u_ref[m * part : (m + 1) * part, :], shift_ref[...], preferred_element_type=F32)
        outer = lax.dot_general(cols, places_ref[m], (((0,), (0,)), ((), ())), preferred_element_type=F32)
        slope[m * part : (m + 1) * part, :] = inner + outer
    for position in range(sx):
        z = slope[pl.ds(row_at(position, sx, odd), times, stride=sx), :]
        if position + 1 < sx:
            z += plain[pl.ds(row_at(position + 1, sx, odd), times, stride=sx), :]
        if position > 0:
            z -= plain[pl.ds(row_at(position - 1, sx, odd), times, stride=sx), :]
        z_ref[position] = z
        sum_ref[position] = jnp.sum(z.reshape(times // 8, 8, LANES), axis=0)


def local_part(odd, side, v, u, shift, near, far, places, sx):
    rows = v.shape[0]
    pieces = places.shape[0]
    times = rows // sx
    return pl.pallas_call(
        functools.partial(local_kernel, sx, pieces),
        out_shape=(
            jax.ShapeDtypeStruct((sx, times, LANES), F32),
            jax.ShapeDtypeStruct((sx, 8, LANES), F32),
        ),
        in_specs=[SMEM] * 2 + [VMEM] * 6,
        out_specs=(VMEM,) * 2,
        scratch_shapes=[pltpu.VMEM((rows, LANES), F32), pltpu.VMEM((rows, LANES), F32)],
        compiler_params=limit(20),
        cost_estimate=pl.CostEstimate(flops=1000000000, bytes_accessed=8000000, transcendentals=0),
        name="local",
    )(odd, side, v, u, shift, near, far, places)


def cross_kernel(
    sx, begin, pieces, odd_ref, offsets_ref, triads_ref, z_ref, sum_ref, weights_ref, window_ref, transform_ref,
    *rest,
):
    far = begin > 0
    halo_refs, rest = rest[:pieces], rest[pieces:]
    if far:
        before_ref, *rest = rest
    cross_ref, target_ref, full, spec, prod, packed = rest
    count, times, _ = full.shape
    blocks = offsets_ref.shape[0]
    ntri = triads_ref.shape[1]
    half = NFFT // 2
    groups = LANES // blocks
    per = ntri // groups
    wide = 2 * blocks
    pitch = blocks + 1
    odd = odd_ref[0]
    sign = jnp.where(odd == 1, 0.5, -0.5)
    if not far:
        sign = -sign
    touched = count - 1 if far else 0

    halo_sum = jnp.zeros((8, LANES), F32)
    base = 0
    for halo_ref in halo_refs:
        length = halo_ref.shape[0]
        steps = max(n for n in range(1, 9) if length % (16 * n) == 0)
        chunk = length // steps

        def add_halo(step, carry):
            at = pl.ds(pl.multiple_of(step * chunk, 8), chunk)
            to = pl.ds(pl.multiple_of(base + step * chunk, 8), chunk)
            halo = sign * halo_ref[at, :].astype(F32)
            for row in range(count):
                z = z_ref[begin + row, to, :]
                full[row, to, :] = z + halo if row == touched else z
            return carry + jnp.sum(halo.reshape(chunk // 8, 8, LANES), axis=0)

        halo_sum = lax.fori_loop(0, steps, add_halo, halo_sum)
        base += halo_ref.shape[0]
    means = []
    for row in range(count):
        total = sum_ref[begin + row]
        if row == touched:
            total = total + halo_sum
        means.append(jnp.sum(total, axis=0, keepdims=True) * (1.0 / times))

    def two_blocks(h, carry):
        window = window_ref[...]
        pair = (2 * h, 2 * h + 1)
        for row in range(count):
            windowed = [
                ((full[row, pl.ds(offsets_ref[b], NFFT), :] - means[row]) * window).astype(BF16) for b in pair
            ]
            out = jnp.dot(transform_ref[...], jnp.concatenate(windowed, axis=1), preferred_element_type=F32)
            for n, b in enumerate(pair):
                spec[row, pl.ds(b, NFFT, stride=pitch), :] = out[:, n * LANES : (n + 1) * LANES]
        return carry

    lax.fori_loop(0, blocks // 2, two_blocks, 0, unroll=True)
    weights = [weights_ref[pl.ds(row_at(begin + row, sx, odd), 1), :] for row in range(count)]

    def one_triad(j):
        k = triads_ref[0, j]
        l = triads_ref[1, j]

        def take(f, row):
            re = spec[row, pl.ds(f * pitch, blocks), :]
            im = spec[row, pl.ds((f + half) * pitch, blocks), :]
            return re, im

        base = pl.multiple_of(j * wide, 8)
        for row in range(count):
            lanes = slice(row * LANES, (row + 1) * LANES)
            first_re, first_im = take(k, row)
            second_re, second_im = take(l, row)
            target_re, target_im = take(k + l, row)
            weight = weights[row]
            prod[pl.ds(base, wide), lanes] = jnp.concatenate(
                [
                    (first_re * second_re - first_im * second_im) * weight,
                    (first_re * second_im + first_im * second_re) * weight,
                ],
                axis=0,
            ).astype(BF16)
            target_ref[pl.ds(base, wide), lanes] = jnp.concatenate([target_re, target_im], axis=0).astype(BF16)

    tall = per * wide
    lane = lax.broadcasted_iota(jnp.int32, (wide, tall), 1)
    owner = lane // wide
    is_re = (lax.broadcasted_iota(jnp.int32, (blocks, tall), 1) % wide) < blocks

    def one_group(g, carry):
        for i in range(per):
            one_triad(g * per + i)
        at = pl.ds(pl.multiple_of(g * tall, 8), tall)
        every = lax.dot_general(
            prod[at, :], target_ref[at, :], (((1,), (1,)), ((), ())), preferred_element_type=F32
        )
        kept = every[0:wide]
        for i in range(1, per):
            kept = jnp.where(owner == i, every[i * wide : (i + 1) * wide], kept)
        by_re = kept[0:blocks]
        by_im = kept[blocks:wide]
        ahead = pltpu.roll(by_im, tall - blocks, 1)
        behind = pltpu.roll(by_im, blocks, 1)
        packed[pl.ds(pl.multiple_of(g * blocks, 8), blocks), :] = by_re + jnp.where(is_re, ahead, -behind)
        return carry

    lax.fori_loop(0, groups, one_group, 0, unroll=True)
    share = packed[...].T
    if far:
        share = share + before_ref[...]
    cross_ref[...] = share


def cross_part(begin, count, odd, offsets, triads, z, sums, halos, weights, window, transform, before=None):
    sx, times, _ = z.shape
    blocks = offsets.shape[0]
    ntri = triads.shape[1]
    groups = LANES // blocks
    wide = 2 * blocks
    tall = ntri // groups * wide
    more = list(halos) + ([] if before is None else [before])
    return pl.pallas_call(
        functools.partial(cross_kernel, sx, begin, len(halos)),
        out_shape=(
            jax.ShapeDtypeStruct((tall, LANES), F32),
            jax.ShapeDtypeStruct((ntri * wide, count * LANES), BF16),
        ),
        in_specs=[SMEM] * 3 + [VMEM] * (5 + len(more)),
        out_specs=(VMEM,) * 2,
        scratch_shapes=[
            pltpu.VMEM((count, times, LANES), F32),
            pltpu.VMEM((count, NFFT * (blocks + 1), LANES), F32),
            pltpu.VMEM((ntri * wide, count * LANES), BF16),
            pltpu.VMEM((LANES, tall), F32),
        ],
        compiler_params=limit(26),
        cost_estimate=pl.CostEstimate(flops=2000000000, bytes_accessed=4000000, transcendentals=0),
        name="cross_far" if begin else "cross_near",
    )(odd, offsets, triads, z, sums, weights, window, transform, *more)


def swap(x, axis, bit):
    count = lax.axis_size(axis)
    return lax.ppermute(x, axis, [(i, i ^ bit) for i in range(count)])


def sum_over_rest(x):
    slabs, parts = lax.axis_size("space"), lax.axis_size("freq")
    hops = [bit * parts for bit in bits_of(slabs)]
    first = hops[:1] + bits_of(parts)[1:] + hops[1:]
    second = first[2:] + first[:2]

    def swapped(one, other):
        pairs = [(i, i ^ (other if i % 2 else one)) for i in range(slabs * parts)]
        return lax.ppermute(sent, ("space", "freq"), pairs).astype(F32)

    for n in range(0, len(first), 2):
        one, other = first[n : n + 2], second[n : n + 2]
        x = lax.reduce_precision(x, 8, 7)
        sent = x.astype(BF16)
        if len(one) == 1:
            x = x + swapped(one[0], other[0])
            continue
        near, far, both = swapped(one[0], other[0]), swapped(one[1], other[1]), swapped(sum(one), sum(other))
        x = (x + near) + (far + both)
    return x


def bits_of(count):
    return [1 << n for n in range(count.bit_length() - 1)]


def modes_kernel(sx, blocks, scaling, odd_ref, mine_ref, other_ref, near_ref, far_ref, values_ref, modes_ref, cross):
    tall = cross.shape[0]
    wide = 2 * blocks
    per = tall // wide
    groups = LANES // blocks
    odd = odd_ref[0]
    cross[...] = (mine_ref[...] + other_ref[...]) * scaling
    lane = lax.broadcasted_iota(jnp.int32, (per, LANES), 1)
    start = lane - lane % blocks

    mat_re = [cross[pl.ds(c, per, stride=wide), :] for c in range(blocks)]
    mat_im = [cross[pl.ds(blocks + c, per, stride=wide), :] for c in range(blocks)]

    def pick(x, index):
        return jnp.take_along_axis(x, index, axis=1)

    spots = [start + c for c in range(blocks)]

    def tree(terms):
        while len(terms) > 1:
            terms = [sum(terms[n : n + 2]) for n in range(0, len(terms), 2)]
        return terms[0]

    def apply(part_re, part_im):
        re = [pick(part_re, spot) for spot in spots]
        im = [pick(part_im, spot) for spot in spots]
        every = range(blocks)
        out_re = tree([mat_re[c] * re[c] - mat_im[c] * im[c] for c in every])
        out_im = tree([mat_re[c] * im[c] + mat_im[c] * re[c] for c in every])
        return out_re, out_im

    def over_blocks(x):
        bit = 1
        while bit < blocks:
            if 4 * bit <= blocks:
                x = (x + pick(x, lane ^ bit)) + (pick(x, lane ^ (2 * bit)) + pick(x, lane ^ (3 * bit)))
                bit *= 4
            else:
                x = x + pick(x, lane ^ bit)
                bit *= 2
        return x

    vec_re = jnp.full((per, LANES), 1.0 / math.sqrt(blocks), F32)
    vec_im = jnp.zeros((per, LANES), F32)
    out_re, out_im = apply(vec_re, vec_im)
    for _ in range(POW):
        length = jnp.sqrt(over_blocks(out_re * out_re + out_im * out_im))
        vec_re = out_re / length
        vec_im = out_im / length
        out_re, out_im = apply(out_re, out_im)
        out_re = out_re / length
        out_im = out_im / length
    value_re = over_blocks(vec_re * out_re + vec_im * out_im)
    value_im = over_blocks(vec_re * out_im - vec_im * out_re)

    source = jnp.minimum(lane // per * blocks, LANES - 1)
    mine = lax.broadcasted_iota(jnp.int32, (per, LANES), 0) == lane % per
    for part, value in enumerate((value_re, value_im)):
        row = jnp.sum(jnp.where(mine, pick(value, source), 0.0), axis=0, keepdims=True)
        values_ref[part : part + 1, :] = row[:, : values_ref.shape[1]]

    own = lax.broadcasted_iota(jnp.int32, (per, tall), 1) // wide == lax.broadcasted_iota(jnp.int32, (per, tall), 0)
    is_re = lax.broadcasted_iota(jnp.int32, (per, tall), 1) % wide < blocks
    for g in range(groups):
        spot = g * blocks + lane % blocks
        re = jnp.concatenate([pick(vec_re, spot)] * (tall // LANES), axis=1)
        im = jnp.concatenate([pick(vec_im, spot)] * (tall // LANES), axis=1)
        rows = jnp.concatenate(
            [
                jnp.where(own, jnp.where(is_re, re, -im), 0.0),
                jnp.where(own, jnp.where(is_re, im, re), 0.0),
            ],
            axis=0,
        )
        high = rows.astype(BF16)
        both = jnp.concatenate([high, (rows - high.astype(F32)).astype(BF16)], axis=0)
        at = slice(g * tall, (g + 1) * tall)
        target = jnp.concatenate([near_ref[at, :], far_ref[at, :]], axis=1)
        out = jnp.dot(both, target, preferred_element_type=F32)
        out = out[: 2 * per] + out[2 * per :]
        for position in range(sx):
            lanes = slice(position * LANES, (position + 1) * LANES)
            row = row_at(position, sx, odd)
            for part in range(2):
                first = g * per * 2 * sx + part * sx
                modes_ref[pl.ds(first + row, per, stride=2 * sx), :] = out[part * per : (part + 1) * per, lanes]


def modes_part(odd, mine, other, near, far, blocks, ntri, sx, scaling):
    return pl.pallas_call(
        functools.partial(modes_kernel, sx, blocks, scaling),
        out_shape=(
            jax.ShapeDtypeStruct((2, ntri), F32),
            jax.ShapeDtypeStruct((ntri * 2 * sx, LANES), F32),
        ),
        in_specs=[SMEM] + [VMEM] * 4,
        out_specs=(VMEM,) * 2,
        scratch_shapes=[pltpu.VMEM(mine.shape, F32)],
        compiler_params=limit(12),
        name="modes",
    )(odd, mine, other, near, far)


def between_pairs(count):
    inner = [(i, i + 1) for i in range(1, count - 1, 2)]
    return inner + [(b, a) for a, b in inner]


def on_device(u_velocity, v_velocity, cell_weights, block_offsets, triads):
    times, sx, columns = u_velocity.shape
    blocks = block_offsets.shape[0]
    ntri = triads.shape[0]
    slabs = lax.axis_size("space")
    cells = sx * columns * slabs * lax.axis_size("freq")
    scaling = 1.0 / (blocks * math.sqrt(cells))
    pieces = 8
    window, transform = make_table(NFFT)
    picks, places = edge_columns(pieces)
    shift = 0.5 * (np.eye(LANES, k=1, dtype=np.float32) - np.eye(LANES, k=-1, dtype=np.float32))
    v = v_velocity.reshape(times * sx, columns)
    u = u_velocity.reshape(times * sx, columns)
    odd = is_odd()[None]
    core = (lax.axis_index("freq") % 2)[None]
    pairs = triads.T

    early, late = near_edge(odd, v, sx)
    early = swap(early, "space", 1)
    late = swap(late, "space", 1)
    col_near, col_far = columns_edge(core, u, jnp.asarray(picks, BF16))
    col_near = swap(col_near, "freq", 1)
    col_far = lax.ppermute(col_far, "freq", between_pairs(lax.axis_size("freq")))
    z, sums = local_part(odd, core, v, u, jnp.asarray(shift, BF16), col_near, col_far, jnp.asarray(places, BF16), sx)
    far = far_edge(odd, v, sx)
    far = lax.ppermute(far, "space", between_pairs(slabs))
    window = jnp.asarray(np.ascontiguousarray(np.broadcast_to(window[:, None], (NFFT, LANES))))
    transform = jnp.asarray(transform, BF16)
    share, near_target = cross_part(
        0, sx - 1, odd, block_offsets, pairs, z, sums, [early, late], cell_weights, window, transform
    )
    share, far_target = cross_part(
        sx - 1, 1, odd, block_offsets, pairs, z, sums, [far], cell_weights, window, transform, share
    )
    mine = sum_over_rest(share)
    other = swap(mine, "freq", 1)
    values, modes = modes_part(odd, mine, other, near_target, far_target, blocks, ntri, sx, scaling)
    return (values.T, modes.reshape(ntri, 2, sx, columns))


def solution(mesh):
    return jax.shard_map(
        on_device,
        mesh=mesh,
        in_specs=(P(None, "space", "freq"), P(None, "space", "freq"), P("space", "freq"), P(), P()),
        out_specs=(P(), P(None, None, "space", "freq")),
        check_vma=False,
    )
```

```python
import functools
import math

import jax
import jax.numpy as jnp
import numpy as np
from jax import lax
from jax.experimental import pallas as pl
from jax.experimental.pallas import tpu as pltpu
from jax.sharding import PartitionSpec as P


NFFT = 256
POW = 4
LANES = 128
AHEAD = 21
F32 = jnp.float32
BF16 = jnp.bfloat16
MIB = 2**20
VMEM = pl.BlockSpec(memory_space=pltpu.VMEM)
SMEM = pl.BlockSpec(memory_space=pltpu.SMEM)


def make_table(length):
    half_len = length // 2
    times_idx = np.arange(length)
    phases = np.arange(half_len)[:, None] * times_idx[None, :] % length
    angles = phases * (2.0 * math.pi / length)
    window = 0.5 - 0.5 * np.cos(times_idx * (2.0 * math.pi / length))
    scaling = 1.0 / np.sqrt(np.sum(window * window))
    transform = np.concatenate([np.cos(angles) * scaling, -np.sin(angles) * scaling], axis=0)
    return window.astype(np.float32), transform.astype(np.float32)


def edge_columns(pieces):
    picks = np.zeros((pieces, 2 * pieces, LANES), np.float32)
    places = np.zeros((pieces, 2 * pieces, LANES), np.float32)
    for m in range(pieces):
        picks[m, m, 0] = 1.0
        picks[m, pieces + m, LANES - 1] = 1.0
        places[m, m, 0] = 0.5
        places[m, pieces + m, LANES - 1] = -0.5
    return picks, places


def is_odd():
    return lax.axis_index("space") % 2


def row_at(position, sx, odd):
    return jnp.where(odd == 1, position, sx - 1 - position)


def limit(mib):
    return pltpu.CompilerParams(vmem_limit_bytes=mib * MIB)


def near_kernel(sx, odd_ref, v_ref, early_ref, late_ref, plain):
    plain[...] = v_ref[...].astype(F32)
    row = row_at(0, sx, odd_ref[0])
    early, late = early_ref.shape[0], late_ref.shape[0]
    early_ref[...] = plain[pl.ds(row, early, stride=sx), :].astype(BF16)
    late_ref[...] = plain[pl.ds(early * sx + row, late, stride=sx), :].astype(BF16)


def near_edge(odd, v, sx):
    rows = v.shape[0]
    early = rows // sx * AHEAD // 2048 * 64
    return pl.pallas_call(
        functools.partial(near_kernel, sx),
        out_shape=(
            jax.ShapeDtypeStruct((early, LANES), BF16),
            jax.ShapeDtypeStruct((rows // sx - early, LANES), BF16),
        ),
        in_specs=[SMEM, VMEM],
        out_specs=(VMEM,) * 2,
        scratch_shapes=[pltpu.VMEM((rows, LANES), F32)],
        compiler_params=limit(8),
        name="near",
    )(odd, v)


def far_kernel(sx, odd_ref, v_ref, far_ref, plain):
    plain[...] = v_ref[...].astype(F32)
    far_ref[...] = plain[pl.ds(row_at(sx - 1, sx, odd_ref[0]), far_ref.shape[0], stride=sx), :].astype(BF16)


def far_edge(odd, v, sx):
    rows = v.shape[0]
    return pl.pallas_call(
        functools.partial(far_kernel, sx),
        out_shape=jax.ShapeDtypeStruct((rows // sx, LANES), BF16),
        in_specs=[SMEM, VMEM],
        out_specs=VMEM,
        scratch_shapes=[pltpu.VMEM((rows, LANES), F32)],
        compiler_params=limit(8),
        name="far",
    )(odd, v)


def columns_kernel(pieces, side_ref, u_ref, picks_ref, near_ref, far_ref):
    rows = u_ref.shape[0]
    part = rows // pieces
    cols = jnp.zeros((2 * pieces, part), F32)
    for m in range(pieces):
        cols += lax.dot_general(
            picks_ref[m], u_ref[m * part : (m + 1) * part, :], (((1,), (1,)), ((), ())), preferred_element_type=F32
        )
    low, high = cols[:pieces], cols[pieces:]
    odd = side_ref[0] == 1
    near_ref[...] = jnp.where(odd, low, high).astype(BF16)
    far_ref[...] = jnp.where(odd, high, low).astype(BF16)


def columns_edge(side, u, picks):
    rows = u.shape[0]
    pieces = picks.shape[0]
    return pl.pallas_call(
        functools.partial(columns_kernel, pieces),
        out_shape=(jax.ShapeDtypeStruct((pieces, rows // pieces), BF16),) * 2,
        in_specs=[SMEM] + [VMEM] * 2,
        out_specs=(VMEM,) * 2,
        compiler_params=limit(8),
        name="columns",
    )(side, u, picks)


def local_kernel(
    sx, pieces, odd_ref, side_ref, v_ref, u_ref, shift_ref, near_ref, far_ref, places_ref, z_ref, sum_ref, plain, slope
):
    rows = v_ref.shape[0]
    times = rows // sx
    part = rows // pieces
    odd = odd_ref[0]
    sign = jnp.where(odd == 1, 0.5, -0.5)
    plain[...] = sign * v_ref[...].astype(F32)
    near, far = near_ref[...].astype(F32), far_ref[...].astype(F32)
    side = side_ref[0] == 1
    cols = jnp.concatenate([jnp.where(side, near, far), jnp.where(side, far, near)], axis=0).astype(BF16)
    for m in range(pieces):
        inner = jnp.dot(u_ref[m * part : (m + 1) * part, :], shift_ref[...], preferred_element_type=F32)
        outer = lax.dot_general(cols, places_ref[m], (((0,), (0,)), ((), ())), preferred_element_type=F32)
        slope[m * part : (m + 1) * part, :] = inner + outer
    for position in range(sx):
        z = slope[pl.ds(row_at(position, sx, odd), times, stride=sx), :]
        if position + 1 < sx:
            z += plain[pl.ds(row_at(position + 1, sx, odd), times, stride=sx), :]
        if position > 0:
            z -= plain[pl.ds(row_at(position - 1, sx, odd), times, stride=sx), :]
        z_ref[position] = z
        sum_ref[position] = jnp.sum(z.reshape(times // 8, 8, LANES), axis=0)


def local_part(odd, side, v, u, shift, near, far, places, sx):
    rows = v.shape[0]
    pieces = places.shape[0]
    times = rows // sx
    return pl.pallas_call(
        functools.partial(local_kernel, sx, pieces),
        out_shape=(
            jax.ShapeDtypeStruct((sx, times, LANES), F32),
            jax.ShapeDtypeStruct((sx, 8, LANES), F32),
        ),
        in_specs=[SMEM] * 2 + [VMEM] * 6,
        out_specs=(VMEM,) * 2,
        scratch_shapes=[pltpu.VMEM((rows, LANES), F32), pltpu.VMEM((rows, LANES), F32)],
        compiler_params=limit(20),
        cost_estimate=pl.CostEstimate(flops=1000000000, bytes_accessed=8000000, transcendentals=0),
        name="local",
    )(odd, side, v, u, shift, near, far, places)


def cross_kernel(
    sx, begin, pieces, odd_ref, offsets_ref, triads_ref, z_ref, sum_ref, weights_ref, window_ref, transform_ref,
    *rest,
):
    far = begin > 0
    halo_refs, rest = rest[:pieces], rest[pieces:]
    if far:
        before_ref, *rest = rest
    cross_ref, target_ref, full, spec, prod, packed = rest
    count, times, _ = full.shape
    blocks = offsets_ref.shape[0]
    ntri = triads_ref.shape[1]
    half = NFFT // 2
    groups = LANES // blocks
    per = ntri // groups
    wide = 2 * blocks
    pitch = blocks + 1
    odd = odd_ref[0]
    sign = jnp.where(odd == 1, 0.5, -0.5)
    if not far:
        sign = -sign
    touched = count - 1 if far else 0

    halo_sum = jnp.zeros((8, LANES), F32)
    base = 0
    for halo_ref in halo_refs:
        length = halo_ref.shape[0]
        steps = max(n for n in range(1, 9) if length % (16 * n) == 0)
        chunk = length // steps

        def add_halo(step, carry):
            at = pl.ds(pl.multiple_of(step * chunk, 8), chunk)
            to = pl.ds(pl.multiple_of(base + step * chunk, 8), chunk)
            halo = sign * halo_ref[at, :].astype(F32)
            for row in range(count):
                z = z_ref[begin + row, to, :]
                full[row, to, :] = z + halo if row == touched else z
            return carry + jnp.sum(halo.reshape(chunk // 8, 8, LANES), axis=0)

        halo_sum = lax.fori_loop(0, steps, add_halo, halo_sum)
        base += halo_ref.shape[0]
    means = []
    for row in range(count):
        total = sum_ref[begin + row]
        if row == touched:
            total = total + halo_sum
        means.append(jnp.sum(total, axis=0, keepdims=True) * (1.0 / times))

    def two_blocks(h, carry):
        window = window_ref[...]
        pair = (2 * h, 2 * h + 1)
        for row in range(count):
            windowed = [
                ((full[row, pl.ds(offsets_ref[b], NFFT), :] - means[row]) * window).astype(BF16) for b in pair
            ]
            out = jnp.dot(transform_ref[...], jnp.concatenate(windowed, axis=1), preferred_element_type=F32)
            for n, b in enumerate(pair):
                spec[row, pl.ds(b, NFFT, stride=pitch), :] = out[:, n * LANES : (n + 1) * LANES]
        return carry

    lax.fori_loop(0, blocks // 2, two_blocks, 0, unroll=True)
    weights = [weights_ref[pl.ds(row_at(begin + row, sx, odd), 1), :] for row in range(count)]

    def one_triad(j):
        k = triads_ref[0, j]
        l = triads_ref[1, j]

        def take(f, row):
            re = spec[row, pl.ds(f * pitch, blocks), :]
            im = spec[row, pl.ds((f + half) * pitch, blocks), :]
            return re, im

        base = pl.multiple_of(j * wide, 8)
        for row in range(count):
            lanes = slice(row * LANES, (row + 1) * LANES)
            first_re, first_im = take(k, row)
            second_re, second_im = take(l, row)
            target_re, target_im = take(k + l, row)
            weight = weights[row]
            prod[pl.ds(base, wide), lanes] = jnp.concatenate(
                [
                    (first_re * second_re - first_im * second_im) * weight,
                    (first_re * second_im + first_im * second_re) * weight,
                ],
                axis=0,
            ).astype(BF16)
            target_ref[pl.ds(base, wide), lanes] = jnp.concatenate([target_re, target_im], axis=0).astype(BF16)

    tall = per * wide
    lane = lax.broadcasted_iota(jnp.int32, (wide, tall), 1)
    owner = lane // wide
    is_re = (lax.broadcasted_iota(jnp.int32, (blocks, tall), 1) % wide) < blocks

    def one_group(g, carry):
        for i in range(per):
            one_triad(g * per + i)
        at = pl.ds(pl.multiple_of(g * tall, 8), tall)
        every = lax.dot_general(
            prod[at, :], target_ref[at, :], (((1,), (1,)), ((), ())), preferred_element_type=F32
        )
        kept = every[0:wide]
        for i in range(1, per):
            kept = jnp.where(owner == i, every[i * wide : (i + 1) * wide], kept)
        by_re = kept[0:blocks]
        by_im = kept[blocks:wide]
        ahead = pltpu.roll(by_im, tall - blocks, 1)
        behind = pltpu.roll(by_im, blocks, 1)
        packed[pl.ds(pl.multiple_of(g * blocks, 8), blocks), :] = by_re + jnp.where(is_re, ahead, -behind)
        return carry

    lax.fori_loop(0, groups, one_group, 0, unroll=True)
    share = packed[...].T
    if far:
        share = share + before_ref[...]
    cross_ref[...] = share


def cross_part(begin, count, odd, offsets, triads, z, sums, halos, weights, window, transform, before=None):
    sx, times, _ = z.shape
    blocks = offsets.shape[0]
    ntri = triads.shape[1]
    groups = LANES // blocks
    wide = 2 * blocks
    tall = ntri // groups * wide
    more = list(halos) + ([] if before is None else [before])
    return pl.pallas_call(
        functools.partial(cross_kernel, sx, begin, len(halos)),
        out_shape=(
            jax.ShapeDtypeStruct((tall, LANES), F32),
            jax.ShapeDtypeStruct((ntri * wide, count * LANES), BF16),
        ),
        in_specs=[SMEM] * 3 + [VMEM] * (5 + len(more)),
        out_specs=(VMEM,) * 2,
        scratch_shapes=[
            pltpu.VMEM((count, times, LANES), F32),
            pltpu.VMEM((count, NFFT * (blocks + 1), LANES), F32),
            pltpu.VMEM((ntri * wide, count * LANES), BF16),
            pltpu.VMEM((LANES, tall), F32),
        ],
        compiler_params=limit(26),
        cost_estimate=pl.CostEstimate(flops=2000000000, bytes_accessed=4000000, transcendentals=0),
        name="cross_far" if begin else "cross_near",
    )(odd, offsets, triads, z, sums, weights, window, transform, *more)


def swap(x, axis, bit):
    count = lax.axis_size(axis)
    return lax.ppermute(x, axis, [(i, i ^ bit) for i in range(count)])


def sum_over_rest(x):
    slabs, parts = lax.axis_size("space"), lax.axis_size("freq")
    hops = [bit * parts for bit in bits_of(slabs)]
    first = hops[:1] + bits_of(parts)[1:] + hops[1:]
    second = first

    def swapped(one, other):
        pairs = [(i, i ^ (other if i % 2 else one)) for i in range(slabs * parts)]
        return lax.ppermute(sent, ("space", "freq"), pairs).astype(F32)

    for n in range(0, len(first), 2):
        one, other = first[n : n + 2], second[n : n + 2]
        x = lax.reduce_precision(x, 8, 7)
        sent = x.astype(BF16)
        if len(one) == 1:
            x = x + swapped(one[0], other[0])
            continue
        near, far, both = swapped(one[0], other[0]), swapped(one[1], other[1]), swapped(sum(one), sum(other))
        x = (x + near) + (far + both)
    return x


def bits_of(count):
    return [1 << n for n in range(count.bit_length() - 1)]


def modes_kernel(sx, blocks, scaling, odd_ref, mine_ref, other_ref, near_ref, far_ref, values_ref, modes_ref, cross):
    tall = cross.shape[0]
    wide = 2 * blocks
    per = tall // wide
    groups = LANES // blocks
    odd = odd_ref[0]
    cross[...] = (mine_ref[...] + other_ref[...]) * scaling
    lane = lax.broadcasted_iota(jnp.int32, (per, LANES), 1)
    start = lane - lane % blocks

    mat_re = [cross[pl.ds(c, per, stride=wide), :] for c in range(blocks)]
    mat_im = [cross[pl.ds(blocks + c, per, stride=wide), :] for c in range(blocks)]

    def pick(x, index):
        return jnp.take_along_axis(x, index, axis=1)

    spots = [start + c for c in range(blocks)]

    def tree(terms):
        while len(terms) > 1:
            terms = [sum(terms[n : n + 2]) for n in range(0, len(terms), 2)]
        return terms[0]

    def apply(part_re, part_im):
        re = [pick(part_re, spot) for spot in spots]
        im = [pick(part_im, spot) for spot in spots]
        every = range(blocks)
        out_re = tree([mat_re[c] * re[c] - mat_im[c] * im[c] for c in every])
        out_im = tree([mat_re[c] * im[c] + mat_im[c] * re[c] for c in every])
        return out_re, out_im

    def over_blocks(x):
        bit = 1
        while bit < blocks:
            if 4 * bit <= blocks:
                x = (x + pick(x, lane ^ bit)) + (pick(x, lane ^ (2 * bit)) + pick(x, lane ^ (3 * bit)))
                bit *= 4
            else:
                x = x + pick(x, lane ^ bit)
                bit *= 2
        return x

    vec_re = jnp.full((per, LANES), 1.0 / math.sqrt(blocks), F32)
    vec_im = jnp.zeros((per, LANES), F32)
    out_re, out_im = apply(vec_re, vec_im)
    for _ in range(POW):
        length = jnp.sqrt(over_blocks(out_re * out_re + out_im * out_im))
        vec_re = out_re / length
        vec_im = out_im / length
        out_re, out_im = apply(out_re, out_im)
        out_re = out_re / length
        out_im = out_im / length
    value_re = over_blocks(vec_re * out_re + vec_im * out_im)
    value_im = over_blocks(vec_re * out_im - vec_im * out_re)

    source = jnp.minimum(lane // per * blocks, LANES - 1)
    mine = lax.broadcasted_iota(jnp.int32, (per, LANES), 0) == lane % per
    for part, value in enumerate((value_re, value_im)):
        row = jnp.sum(jnp.where(mine, pick(value, source), 0.0), axis=0, keepdims=True)
        values_ref[part : part + 1, :] = row[:, : values_ref.shape[1]]

    own = lax.broadcasted_iota(jnp.int32, (per, tall), 1) // wide == lax.broadcasted_iota(jnp.int32, (per, tall), 0)
    is_re = lax.broadcasted_iota(jnp.int32, (per, tall), 1) % wide < blocks
    for g in range(groups):
        spot = g * blocks + lane % blocks
        re = jnp.concatenate([pick(vec_re, spot)] * (tall // LANES), axis=1)
        im = jnp.concatenate([pick(vec_im, spot)] * (tall // LANES), axis=1)
        rows = jnp.concatenate(
            [
                jnp.where(own, jnp.where(is_re, re, -im), 0.0),
                jnp.where(own, jnp.where(is_re, im, re), 0.0),
            ],
            axis=0,
        )
        high = rows.astype(BF16)
        both = jnp.concatenate([high, (rows - high.astype(F32)).astype(BF16)], axis=0)
        at = slice(g * tall, (g + 1) * tall)
        target = jnp.concatenate([near_ref[at, :], far_ref[at, :]], axis=1)
        out = jnp.dot(both, target, preferred_element_type=F32)
        out = out[: 2 * per] + out[2 * per :]
        for position in range(sx):
            lanes = slice(position * LANES, (position + 1) * LANES)
            row = row_at(position, sx, odd)
            for part in range(2):
                first = g * per * 2 * sx + part * sx
                modes_ref[pl.ds(first + row, per, stride=2 * sx), :] = out[part * per : (part + 1) * per, lanes]


def modes_part(odd, mine, other, near, far, blocks, ntri, sx, scaling):
    return pl.pallas_call(
        functools.partial(modes_kernel, sx, blocks, scaling),
        out_shape=(
            jax.ShapeDtypeStruct((2, ntri), F32),
            jax.ShapeDtypeStruct((ntri * 2 * sx, LANES), F32),
        ),
        in_specs=[SMEM] + [VMEM] * 4,
        out_specs=(VMEM,) * 2,
        scratch_shapes=[pltpu.VMEM(mine.shape, F32)],
        compiler_params=limit(12),
        name="modes",
    )(odd, mine, other, near, far)


def between_pairs(count):
    inner = [(i, i + 1) for i in range(1, count - 1, 2)]
    return inner + [(b, a) for a, b in inner]


def on_device(u_velocity, v_velocity, cell_weights, block_offsets, triads):
    times, sx, columns = u_velocity.shape
    blocks = block_offsets.shape[0]
    ntri = triads.shape[0]
    slabs = lax.axis_size("space")
    cells = sx * columns * slabs * lax.axis_size("freq")
    scaling = 1.0 / (blocks * math.sqrt(cells))
    pieces = 8
    window, transform = make_table(NFFT)
    picks, places = edge_columns(pieces)
    shift = 0.5 * (np.eye(LANES, k=1, dtype=np.float32) - np.eye(LANES, k=-1, dtype=np.float32))
    v = v_velocity.reshape(times * sx, columns)
    u = u_velocity.reshape(times * sx, columns)
    odd = is_odd()[None]
    core = (lax.axis_index("freq") % 2)[None]
    pairs = triads.T

    early, late = near_edge(odd, v, sx)
    early = swap(early, "space", 1)
    late = swap(late, "space", 1)
    col_near, col_far = columns_edge(core, u, jnp.asarray(picks, BF16))
    col_near = swap(col_near, "freq", 1)
    col_far = lax.ppermute(col_far, "freq", between_pairs(lax.axis_size("freq")))
    z, sums = local_part(odd, core, v, u, jnp.asarray(shift, BF16), col_near, col_far, jnp.asarray(places, BF16), sx)
    far = far_edge(odd, v, sx)
    far = lax.ppermute(far, "space", between_pairs(slabs))
    window = jnp.asarray(np.ascontiguousarray(np.broadcast_to(window[:, None], (NFFT, LANES))))
    transform = jnp.asarray(transform, BF16)
    share, near_target = cross_part(
        0, sx - 1, odd, block_offsets, pairs, z, sums, [early, late], cell_weights, window, transform
    )
    share, far_target = cross_part(
        sx - 1, 1, odd, block_offsets, pairs, z, sums, [far], cell_weights, window, transform, share
    )
    mine = sum_over_rest(share)
    other = swap(mine, "freq", 1)
    values, modes = modes_part(odd, mine, other, near_target, far_target, blocks, ntri, sx, scaling)
    return (values.T, modes.reshape(ntri, 2, sx, columns))


def solution(mesh):
    return jax.shard_map(
        on_device,
        mesh=mesh,
        in_specs=(P(None, "space", "freq"), P(None, "space", "freq"), P("space", "freq"), P(), P()),
        out_specs=(P(), P(None, None, "space", "freq")),
        check_vma=False,
    )
```
